512 devices in a mesh: page: 16 (over z), blk: 32 (over y, x, core).
Axes of the slice: x: 4, y: 4, z: 16, core: 2. Of those that a mesh axis runs over, the one named last changes fastest.
Arguments:
- queries: bfloat16 [64, 2, 32, 128], P(None, None, 'blk'), may hold values from -192 to 192
- prompt_kv: bfloat16 [256, 64, 32, 256], P('page', None, 'blk'), may hold values from -36 to 36
- tail_kv: bfloat16 [64, 256, 32, 256], P('page', None, 'blk'), may hold values from -36 to 36
- page_table: int32 [4, 64], replicated, may hold values from 0 to 255, as said below
- prompt_len: int32 [4], replicated, may hold values from 1 to 4096, 10240 in all
- tail_len: int32 [64], replicated, may hold values from 0 to 254, as said below
- sample_prompt: int32 [64], replicated, may hold values from 0 to 3, as said below
- stream_in: bfloat16 [64, 2, 7168], P(None, None, 'blk'), may hold values from -6 to 6
- w_out: bfloat16 [4096, 7168], P('blk'), may hold values from -0.09375 to 0.09375
- b_out: bfloat16 [7168], replicated, may hold values from -3 to 3
- ln_gain: bfloat16 [7168], P('page'), may hold values from 0.25 to 1.75
- ln_bias: bfloat16 [7168], P('page'), may hold values from -3 to 3
- w_up: bfloat16 [7168, 28672], P('page', 'blk'), may hold values from -0.0625 to 0.0625
- b_up: bfloat16 [28672], P('blk'), may hold values from -3 to 3
- w_down: bfloat16 [28672, 7168], P('blk', 'page'), may hold values from -0.046875 to 0.046875
- b_down: bfloat16 [7168], P(('page', 'blk')), may hold values from -3 to 3
- w_score: bfloat16 [7168], P(('page', 'blk')), may hold values from -0.0625 to 0.0625
Outputs:
- layer_output: bfloat16 [64, 2, 7168], P(None, None, ('page', 'blk'))
- sample_score: float32 [64, 2], replicated
The draws below stay inside these ranges and needn't reach their ends.
Inputs may be any that keep to these rules, and one draw needn't show every extreme that they name: `page_table`: every slot number appears exactly once in the table. `tail_len`: some sample reaches the largest value. `sample_prompt`: each prompt has exactly 16 samples.
All inputs are finite; a program needn't handle non-finite values.
Results may differ from the reference program's by a relative error of at most 0.03.
Values may be sent and summed in bfloat16 or wider, within the bound.
A program may use at most 64 MiB of HBM per device.

```python
import math
import jax
import jax.numpy as jnp
import numpy as np
from jax import lax

D = 7168
FF = 28672
HEADS = 32
HD = 128
PAGE_LEN = 64
PROMPTS = 4
NEW = 2
TAIL_MAX = 256
SAMPLES = 64
ROWS = 128
SLOTS = 256
PAGES_MAX = 64
PROMPT_MAX = 4096
N_PAGE = 16


def paged_values(key, shape, offset_shape):
    count = shape[0]
    noise = jnp.clip(jax.random.normal(key, shape, jnp.float32), -4.0, 4.0)
    offset = jnp.clip(jax.random.normal(jax.random.fold_in(key, 3), offset_shape, jnp.float32), -3.0, 3.0)
    reach = 6.0
    common = jax.random.uniform(jax.random.fold_in(key, 7), (1, 1, HEADS, HD), jnp.float32, -1.0, 1.0)
    rise = jnp.exp(math.log(reach) * jnp.arange(count, dtype=jnp.float32) / (count - 1)).reshape(count, 1, 1, 1)
    mixed = noise + offset
    key_half = 0.7 * mixed[..., :HD]
    value_half = (0.35 * mixed[..., HD:] + common) * rise
    return jnp.concatenate([key_half, value_half], axis=-1).astype(jnp.bfloat16)


def draw_queries(key, part):
    shape = (SAMPLES, NEW, HEADS, HD)
    base = jnp.clip(jax.random.normal(key, shape, jnp.float32), -4.0, 4.0)
    return base.astype(jnp.bfloat16)


def draw_prompt_kv(key, part):
    return paged_values(key, (SLOTS, PAGE_LEN, HEADS, 2 * HD), (SLOTS, 1, HEADS, 2 * HD))


def draw_tail_kv(key, part):
    return paged_values(key, (SAMPLES, TAIL_MAX, HEADS, 2 * HD), (SAMPLES, 1, HEADS, 2 * HD))


def draw_page_table(key, part):
    return jax.random.permutation(key, SLOTS).astype(jnp.int32).reshape(PROMPTS, PAGES_MAX)


def draw_tail_len(key, part):
    values = jax.random.randint(key, (SAMPLES,), 0, TAIL_MAX - 1, dtype=jnp.int32)
    chosen = jax.random.randint(jax.random.fold_in(key, 1), (), 0, SAMPLES, dtype=jnp.int32)
    return jnp.where(jnp.arange(SAMPLES, dtype=jnp.int32) == chosen, TAIL_MAX - 2, values).astype(jnp.int32)


def draw_sample_prompt(key, part):
    return (jax.random.permutation(key, SAMPLES).astype(jnp.int32) % PROMPTS).astype(jnp.int32)


def block_levels(own_key, extent, shards, least, high):
    gain = 1.0
    for position, blocks in shards:
        heights = jax.random.uniform(jax.random.fold_in(jax.random.fold_in(own_key, 6), position), (blocks,), jnp.float32, least / len(shards), high / len(shards))
        gain = gain * jnp.repeat(jnp.exp(heights), extent[position] // blocks).reshape((-1,) + (1,) * (len(extent) - 1 - position))
    return gain


def profile(number_of, total, most, skew):
    loads = [(1 << 20) // math.isqrt(rank ** skew) + 1 for rank in range(2, number_of + 1)]
    surplus, holding = total - most - (number_of - 1), [1] * (number_of - 1)
    while surplus > 0:
        free = [i for i in range(number_of - 1) if holding[i] < most]
        whole, budget = sum([loads[i] for i in free]), surplus
        for i in free:
            more = min(most - holding[i], max(1, budget * loads[i] // whole), surplus)
            holding[i] = holding[i] + more
            surplus = surplus - more
    return np.array([most] + holding)


def ragged_sizes(stream_key, amount, total, most, skew):
    if amount == 2:
        one = jax.random.randint(stream_key, (), max(1, total - most), min(most, total - 1) + 1)
        return jnp.stack([one, total - one])
    tallies = jnp.asarray(profile(amount, total, most, skew), jnp.int32)
    twos = (amount - 1) // 2
    donor, taker = tallies[1:1 + 2 * twos:2], tallies[2:2 + 2 * twos:2]
    slack = jnp.minimum(donor - 1, most - taker)
    moved = jax.random.randint(jax.random.fold_in(stream_key, 1), (twos,), 0, 1 << 20) % (slack + 1)
    tallies = tallies.at[1:1 + 2 * twos:2].set(donor - moved).at[2:2 + 2 * twos:2].set(taker + moved)
    return tallies[jax.random.permutation(jax.random.fold_in(stream_key, 2), amount)]


def bell_draw(rng, extent, spread, most, cuts=(), held_as=jnp.bfloat16):
    values = jax.random.normal(rng, extent, jnp.float32) * spread
    if len(cuts) > 0:
        values = block_levels(rng, extent, cuts, -0.22, 0.18) * values
    return jnp.clip(values, min=-most, max=most).astype(held_as)


def setup_inputs(seed: int = 0) -> dict:
    key_of = jax.random.split(jax.random.key(seed), 18)
    queries = draw_queries(jax.random.fold_in(key_of[17], 71), 0)
    prompt_kv = draw_prompt_kv(jax.random.fold_in(key_of[17], 71), 0)
    tail_kv = draw_tail_kv(jax.random.fold_in(key_of[17], 71), 0)
    page_table = draw_page_table(jax.random.fold_in(key_of[17], 71), 0)
    prompt_len = ragged_sizes(key_of[4], PROMPTS, 5 * PROMPT_MAX * PROMPTS // 8, PROMPT_MAX, 2).astype(jnp.int32)
    tail_len = draw_tail_len(jax.random.fold_in(key_of[17], 71), 0)
    sample_prompt = draw_sample_prompt(jax.random.fold_in(key_of[17], 71), 0)
    stream_in = bell_draw(key_of[7], (SAMPLES, NEW, D), 1.0, 6.0, ((2, 32),))
    w_out = bell_draw(key_of[8], (HEADS * HD, D), (HEADS * HD) ** -0.5, 0.09375, ((0, 32),))
    b_out = bell_draw(key_of[9], (D,), 0.5, 3.0)
    ln_gain = jnp.clip(1.0 + 0.15 * jax.random.normal(key_of[10], (D,), jnp.float32), 0.25, 1.75).astype(jnp.bfloat16)
    ln_bias = bell_draw(key_of[11], (D,), 0.5, 3.0, ((0, 16),))
    w_up = bell_draw(key_of[12], (D, FF), D ** -0.5, 0.0625, ((0, 16), (1, 32)))
    b_up = bell_draw(key_of[13], (FF,), 0.5, 3.0, ((0, 32),))
    w_down = bell_draw(key_of[14], (FF, D), (FF // 2) ** -0.5, 0.046875, ((0, 32), (1, 16)))
    b_down = bell_draw(key_of[15], (D,), 0.5, 3.0, ((0, 512),))
    w_score = bell_draw(key_of[16], (D,), D ** -0.5, 0.0625, ((0, 512),))
    return dict(queries=queries, prompt_kv=prompt_kv, tail_kv=tail_kv, page_table=page_table, prompt_len=prompt_len, tail_len=tail_len, sample_prompt=sample_prompt, stream_in=stream_in, w_out=w_out, b_out=b_out, ln_gain=ln_gain, ln_bias=ln_bias, w_up=w_up, b_up=b_up, w_down=w_down, b_down=b_down, w_score=w_score)


NEGATIVE = -1e+30

def reference(queries, prompt_kv, tail_kv, page_table, prompt_len, tail_len, sample_prompt, stream_in, w_out, b_out, ln_gain, ln_bias, w_up, b_up, w_down, b_down, w_score):
    inv_sqrt = 1.0 / math.sqrt(HD)
    owner_index = jnp.zeros((SLOTS,), jnp.int32).at[page_table.reshape(-1)].set(jnp.arange(SLOTS, dtype=jnp.int32))
    slot_prompt = owner_index // PAGES_MAX
    slot_page = owner_index % PAGES_MAX
    key_pos = slot_page[:, None] * PAGE_LEN + jnp.arange(PAGE_LEN, dtype=jnp.int32)[None, :]
    key_live = (key_pos < prompt_len[slot_prompt][:, None]).reshape(-1)
    key_prompt = jnp.repeat(slot_prompt, PAGE_LEN)
    prompt_visible = (sample_prompt[:, None] == key_prompt[None, :]) & key_live[None, :]
    reach_pos = tail_len[:, None] + jnp.arange(NEW, dtype=jnp.int32)[None, :]
    tail_visible = jnp.arange(TAIL_MAX, dtype=jnp.int32)[None, None, :] <= reach_pos[:, :, None]
    by_head = (jnp.moveaxis(queries, 2, 0), jnp.moveaxis(prompt_kv.reshape(SLOTS * PAGE_LEN, HEADS, 2 * HD), 1, 0), jnp.moveaxis(tail_kv, 2, 0))

    def one_head(operands):
        query_f = operands[0].astype(jnp.float32)
        prompt_f = operands[1].astype(jnp.float32)
        tail_f = operands[2].astype(jnp.float32)
        prompt_scores = jnp.einsum('snd,kd->snk', query_f, prompt_f[:, :HD]) * inv_sqrt
        tail_scores = jnp.einsum('snd,std->snt', query_f, tail_f[:, :, :HD]) * inv_sqrt
        prompt_mask = prompt_visible[:, None, :]
        highest = jnp.maximum(lax.optimization_barrier(jnp.max(jnp.where(prompt_mask, prompt_scores, NEGATIVE), axis=-1)), lax.optimization_barrier(jnp.max(jnp.where(tail_visible, tail_scores, NEGATIVE), axis=-1)))
        prompt_w = jnp.where(prompt_mask, jnp.exp(prompt_scores - highest[..., None]), 0.0)
        tail_w = jnp.where(tail_visible, jnp.exp(tail_scores - highest[..., None]), 0.0)
        weight_sum = lax.optimization_barrier(jnp.sum(prompt_w, axis=-1)) + lax.optimization_barrier(jnp.sum(tail_w, axis=-1))
        prompt_r = lax.optimization_barrier(prompt_w.astype(jnp.bfloat16)).astype(jnp.float32)
        tail_r = lax.optimization_barrier(tail_w.astype(jnp.bfloat16)).astype(jnp.float32)
        weighted = jnp.einsum('snk,kd->snd', prompt_r, prompt_f[:, HD:]) + jnp.einsum('snt,std->snd', tail_r, tail_f[:, :, HD:])
        return (weighted / weight_sum[..., None]).astype(jnp.bfloat16)
    heads_out = lax.map(one_head, by_head)
    attention = jnp.moveaxis(heads_out, 0, 2).reshape(ROWS, HEADS * HD)
    rows_in = stream_in.reshape(ROWS, D).astype(jnp.float32)
    residual = (jnp.dot(attention, w_out, preferred_element_type=jnp.float32) + rows_in + b_out.astype(jnp.float32)).astype(jnp.bfloat16)
    residual_f = residual.astype(jnp.float32)
    row_mean = lax.optimization_barrier(jnp.mean(residual_f, axis=-1, keepdims=True))
    centred = residual_f - row_mean
    inverse_std = lax.rsqrt(lax.optimization_barrier(jnp.mean(centred * centred, axis=-1, keepdims=True)) + 1e-05)
    normed = (centred * inverse_std * ln_gain.astype(jnp.float32) + ln_bias.astype(jnp.float32)).astype(jnp.bfloat16)
    group_width = D // N_PAGE
    normed_groups = jnp.moveaxis(normed.reshape(ROWS, N_PAGE, group_width), 1, 0)
    up_groups = w_up.reshape(N_PAGE, group_width, FF)

    def group_product(operands):
        return lax.optimization_barrier(jnp.dot(operands[0], operands[1], preferred_element_type=jnp.float32).astype(jnp.bfloat16))
    hidden_sum = lax.optimization_barrier(jnp.sum(lax.map(group_product, (normed_groups, up_groups)).astype(jnp.float32), axis=0))
    hidden = jnp.maximum(hidden_sum + b_up.astype(jnp.float32), 0.0).astype(jnp.bfloat16)
    output = (jnp.dot(hidden, w_down, preferred_element_type=jnp.float32) + residual_f + b_down.astype(jnp.float32)).astype(jnp.bfloat16)
    row_score = lax.optimization_barrier(jnp.sum(output.astype(jnp.float32) * w_score.astype(jnp.float32), axis=-1))
    return (output.reshape(SAMPLES, NEW, D), row_score.reshape(SAMPLES, NEW))
```

```python
import math

import jax
import jax.numpy as jnp
from jax import lax
from jax.sharding import PartitionSpec as P

NEGATIVE = -1e30


def exchange(x, axis):
    return lax.all_to_all(x, axis, 0, 0, tiled=True)


def softmax_part(scores, visible):
    masked = jnp.where(visible, scores, NEGATIVE)
    highest = jnp.max(masked, axis=-1)
    weights = jnp.where(visible, jnp.exp(scores - highest[..., None]), 0.0)
    return (highest, jnp.sum(weights, axis=-1), weights.astype(jnp.bfloat16))


def ordered_sum(stack):
    total = stack[0]
    for j in range(1, stack.shape[0]):
        total = total + stack[j]
    return total


def body(
    queries,
    prompt_kv,
    tail_kv,
    page_table,
    prompt_len,
    tail_len,
    sample_prompt,
    stream_in,
    w_out,
    b_out,
    ln_gain,
    ln_bias,
    w_up,
    b_up,
    w_down,
    b_down,
    w_score,
):
    samples, new_count, heads_dev, head_dim = queries.shape
    slots_dev, page_len = (prompt_kv.shape[0], prompt_kv.shape[1])
    own_count, tail_max = (tail_kv.shape[0], tail_kv.shape[1])
    prompts, pages_max = page_table.shape
    n_page = samples // own_count
    page_pos = lax.axis_index("page")
    blk_pos = lax.axis_index("blk")
    inv_sqrt = 1.0 / math.sqrt(head_dim)
    width = w_out.shape[1]
    rows_own = own_count * new_count

    entries = page_table.reshape(-1)
    slot_ids = page_pos * slots_dev + jnp.arange(slots_dev, dtype=jnp.int32)
    matched = (entries[:, None] == slot_ids[None, :]).astype(jnp.int32)
    owner_index = jnp.sum(matched * jnp.arange(entries.shape[0], dtype=jnp.int32)[:, None], axis=0)
    slot_prompt = owner_index // pages_max
    slot_page = owner_index % pages_max
    prompt_pick = (slot_prompt[:, None] == jnp.arange(prompts, dtype=jnp.int32)[None, :]).astype(
        jnp.int32
    )
    slot_limit = jnp.sum(prompt_pick * prompt_len[None, :], axis=1)
    key_pos = slot_page[:, None] * page_len + jnp.arange(page_len, dtype=jnp.int32)[None, :]
    key_live = (key_pos < slot_limit[:, None]).reshape(-1)
    key_prompt = jnp.repeat(slot_prompt, page_len)
    prompt_visible = ((sample_prompt[:, None] == key_prompt[None, :]) & key_live[None, :])[
        :, None, None, :
    ]

    cache_rows = prompt_kv.reshape(slots_dev * page_len, heads_dev, 2 * head_dim)
    prompt_scores = (
        jnp.einsum(
            "snhd,khd->snhk",
            queries,
            cache_rows[:, :, :head_dim],
            preferred_element_type=jnp.float32,
        )
        * inv_sqrt
    )
    high_p, sum_p, weights_p = softmax_part(prompt_scores, prompt_visible)
    mixed_p = jnp.einsum(
        "snhk,khd->snhd", weights_p, cache_rows[:, :, head_dim:], preferred_element_type=jnp.float32
    )

    first_row = page_pos * own_count
    own_queries = lax.dynamic_slice_in_dim(queries, first_row, own_count, 0)
    own_lengths = lax.dynamic_slice_in_dim(tail_len, first_row, own_count, 0)
    tail_scores = (
        jnp.einsum(
            "snhd,sthd->snht",
            own_queries,
            tail_kv[..., :head_dim],
            preferred_element_type=jnp.float32,
        )
        * inv_sqrt
    )
    reach_pos = own_lengths[:, None] + jnp.arange(new_count, dtype=jnp.int32)[None, :]
    tail_visible = (
        jnp.arange(tail_max, dtype=jnp.int32)[None, None, None, :] <= reach_pos[:, :, None, None]
    )
    high_t, sum_t, weights_t = softmax_part(tail_scores, tail_visible)
    mixed_t = jnp.einsum(
        "snht,sthd->snhd", weights_t, tail_kv[..., head_dim:], preferred_element_type=jnp.float32
    )

    packed = jnp.concatenate([mixed_p, high_p[..., None], sum_p[..., None]], axis=-1)
    packed = packed.reshape(n_page, rows_own * heads_dev, head_dim + 2)
    got = exchange(packed, "page")
    high_all = got[..., head_dim]
    sum_all = got[..., head_dim + 1]
    mixed_all = got[..., :head_dim]
    high_t = high_t.reshape(rows_own * heads_dev)
    sum_t = sum_t.reshape(rows_own * heads_dev)
    mixed_t = mixed_t.reshape(rows_own * heads_dev, head_dim)
    highest = jnp.maximum(jnp.max(high_all, axis=0), high_t)
    scale_all = jnp.exp(high_all - highest[None, :])
    scale_t = jnp.exp(high_t - highest)
    weight_sum = ordered_sum(sum_all * scale_all) + sum_t * scale_t
    weighted = ordered_sum(mixed_all * scale_all[..., None]) + mixed_t * scale_t[..., None]
    attention = (
        (weighted / weight_sum[..., None])
        .astype(jnp.bfloat16)
        .reshape(rows_own, heads_dev * head_dim)
    )

    contrib = jnp.dot(attention, w_out, preferred_element_type=jnp.float32)
    slice_width = stream_in.shape[2]
    column = blk_pos * slice_width
    own_stream = (
        lax.dynamic_slice_in_dim(stream_in, first_row, own_count, 0)
        .reshape(rows_own, slice_width)
        .astype(jnp.float32)
    )
    contrib = lax.dynamic_update_slice_in_dim(
        contrib, lax.dynamic_slice_in_dim(contrib, column, slice_width, 1) + own_stream, column, 1
    )
    n_blk = width // slice_width
    pieces = contrib.reshape(rows_own, n_blk, slice_width).transpose(1, 0, 2)
    summed = ordered_sum(exchange(pieces, "blk"))
    own_bias = lax.dynamic_slice_in_dim(b_out, column, slice_width, 0).astype(jnp.float32)
    res_piece = (summed + own_bias).astype(jnp.bfloat16).astype(jnp.float32)
    gathered = exchange(jnp.broadcast_to(res_piece[None], (n_blk,) + res_piece.shape), "blk")
    residual_f = gathered.transpose(1, 0, 2).reshape(rows_own, width)

    row_mean = jnp.mean(residual_f, axis=-1, keepdims=True)
    centred = residual_f - row_mean
    inverse_std = lax.rsqrt(jnp.mean(centred * centred, axis=-1, keepdims=True) + 1e-05)
    scaled = centred * inverse_std

    feature_count = ln_gain.shape[0]
    piece_width = b_down.shape[0]
    scaled3 = scaled.reshape(rows_own, n_page, feature_count)
    res3 = lax.dynamic_slice_in_dim(
        residual_f.reshape(rows_own, n_page, feature_count), blk_pos * piece_width, piece_width, 2
    )
    outgoing = jnp.concatenate([scaled3, res3], axis=-1).transpose(1, 0, 2)
    incoming = exchange(outgoing, "page").reshape(samples * new_count, feature_count + piece_width)
    normed = (
        incoming[:, :feature_count] * ln_gain.astype(jnp.float32) + ln_bias.astype(jnp.float32)
    ).astype(jnp.bfloat16)
    residual_piece = incoming[:, feature_count:]

    up_part = jnp.dot(normed, w_up, preferred_element_type=jnp.float32).astype(jnp.bfloat16)
    up_rows = exchange(up_part.astype(jnp.float32).reshape(n_page, rows_own, -1), "page")
    hidden_rows = jnp.maximum(ordered_sum(up_rows) + b_up.astype(jnp.float32), 0.0)
    hidden_rows = hidden_rows.astype(jnp.bfloat16).astype(jnp.float32)
    hidden = exchange(
        jnp.broadcast_to(hidden_rows[None], (n_page,) + hidden_rows.shape), "page"
    ).reshape(samples * new_count, -1)

    projected = jnp.dot(hidden.astype(jnp.bfloat16), w_down, preferred_element_type=jnp.float32)
    proj_pieces = projected.reshape(samples * new_count, n_blk, piece_width).transpose(1, 0, 2)
    out_share = ordered_sum(exchange(proj_pieces, "blk"))
    output = (out_share + residual_piece + b_down.astype(jnp.float32)).astype(jnp.bfloat16)

    score_part = jnp.sum(output.astype(jnp.float32) * w_score.astype(jnp.float32), axis=-1)
    score_part = score_part.reshape(1, samples * new_count)
    blk_sum = ordered_sum(
        exchange(jnp.broadcast_to(score_part[None], (n_blk,) + score_part.shape), "blk")
    )
    row_score = ordered_sum(
        exchange(jnp.broadcast_to(blk_sum[None], (n_page,) + blk_sum.shape), "page")
    )
    return (output.reshape(samples, new_count, piece_width), row_score.reshape(samples, new_count))


def solution(mesh):
    placed = (
        P(None, None, "blk", None),
        P("page", None, "blk", None),
        P("page", None, "blk", None),
        P(),
        P(),
        P(),
        P(),
        P(None, None, "blk"),
        P("blk", None),
        P(),
        P("page"),
        P("page"),
        P("page", "blk"),
        P("blk"),
        P("blk", "page"),
        P(("page", "blk")),
        P(("page", "blk")),
    )
    return jax.shard_map(
        body,
        mesh=mesh,
        in_specs=placed,
        out_specs=(P(None, None, ("page", "blk")), P()),
        check_vma=False,
    )
```

```python
import math

import jax
import jax.numpy as jnp
from jax import lax
from jax.experimental import pallas as pl
from jax.experimental.pallas import tpu as pltpu
from jax.sharding import PartitionSpec as P

NEGATIVE = -1e30
AXES = ("page", "blk")
MESH_ID = pl.DeviceIdType.MESH


def exchange_kernel(axis, n, mode, x_ref, o_ref, buf, send_sem, recv_sem):
    me = lax.axis_index(axis)
    coords = [lax.axis_index(name) for name in AXES]

    def device(j):
        return tuple(j if name == axis else c for name, c in zip(AXES, coords))

    if mode == "gather":
        buf[me] = x_ref[...]
    else:
        buf[me] = x_ref[me]
    barrier = pltpu.get_barrier_semaphore()
    for k in range(1, n):
        peer = lax.rem(me + k, n)
        pl.semaphore_signal(barrier, inc=1, device_id=device(peer), device_id_type=MESH_ID)
    pl.semaphore_wait(barrier, n - 1)
    copies = []
    for k in range(1, n):
        peer = lax.rem(me + k, n)
        source = x_ref if mode == "gather" else x_ref.at[peer]
        copy = pltpu.make_async_remote_copy(
            src_ref=source,
            dst_ref=buf.at[me],
            send_sem=send_sem.at[k],
            recv_sem=recv_sem.at[k],
            device_id=device(peer),
            device_id_type=MESH_ID,
        )
        copy.start()
        copies.append(copy)
    for copy in copies:
        copy.wait()
    if mode == "sum":
        total = buf[0]
        for j in range(1, n):
            total = total + buf[j]
        o_ref[...] = total
    else:
        o_ref[...] = buf[...]


CALL_IDS = {}


def exchange(x, axis, mode="swap"):
    n = lax.axis_size(axis)
    x = x.astype(jnp.float32)
    chunk = x.shape if mode == "gather" else x.shape[1:]
    out_shape = chunk if mode == "sum" else (n,) + tuple(chunk)
    cid = len(CALL_IDS)
    CALL_IDS[cid] = axis
    return pl.pallas_call(
        lambda *refs: exchange_kernel(axis, n, mode, *refs),
        out_shape=jax.ShapeDtypeStruct(out_shape, jnp.float32),
        in_specs=[pl.BlockSpec(memory_space=pltpu.VMEM)],
        out_specs=pl.BlockSpec(memory_space=pltpu.VMEM),
        scratch_shapes=[
            pltpu.VMEM((n,) + tuple(chunk), jnp.float32),
            pltpu.SemaphoreType.DMA((n,)),
            pltpu.SemaphoreType.DMA((n,)),
        ],
        compiler_params=pltpu.CompilerParams(collective_id=cid, has_side_effects=True),
    )(x)


def softmax_part(scores, visible):
    masked = jnp.where(visible, scores, NEGATIVE)
    highest = jnp.max(masked, axis=-1)
    weights = jnp.where(visible, jnp.exp(scores - highest[..., None]), 0.0)
    return (highest, jnp.sum(weights, axis=-1), weights.astype(jnp.bfloat16))


def ordered_sum(stack):
    total = stack[0]
    for j in range(1, stack.shape[0]):
        total = total + stack[j]
    return total


def body(
    queries,
    prompt_kv,
    tail_kv,
    page_table,
    prompt_len,
    tail_len,
    sample_prompt,
    stream_in,
    w_out,
    b_out,
    ln_gain,
    ln_bias,
    w_up,
    b_up,
    w_down,
    b_down,
    w_score,
):
    CALL_IDS.clear()
    samples, new_count, heads_dev, head_dim = queries.shape
    slots_dev, page_len = (prompt_kv.shape[0], prompt_kv.shape[1])
    own_count, tail_max = (tail_kv.shape[0], tail_kv.shape[1])
    prompts, pages_max = page_table.shape
    n_page = samples // own_count
    page_pos = lax.axis_index("page")
    blk_pos = lax.axis_index("blk")
    inv_sqrt = 1.0 / math.sqrt(head_dim)
    width = w_out.shape[1]
    rows_own = own_count * new_count

    entries = page_table.reshape(-1)
    slot_ids = page_pos * slots_dev + jnp.arange(slots_dev, dtype=jnp.int32)
    matched = (entries[:, None] == slot_ids[None, :]).astype(jnp.int32)
    owner_index = jnp.sum(matched * jnp.arange(entries.shape[0], dtype=jnp.int32)[:, None], axis=0)
    slot_prompt = owner_index // pages_max
    slot_page = owner_index % pages_max
    prompt_pick = (slot_prompt[:, None] == jnp.arange(prompts, dtype=jnp.int32)[None, :]).astype(
        jnp.int32
    )
    slot_limit = jnp.sum(prompt_pick * prompt_len[None, :], axis=1)
    key_pos = slot_page[:, None] * page_len + jnp.arange(page_len, dtype=jnp.int32)[None, :]
    key_live = (key_pos < slot_limit[:, None]).reshape(-1)
    key_prompt = jnp.repeat(slot_prompt, page_len)
    prompt_visible = ((sample_prompt[:, None] == key_prompt[None, :]) & key_live[None, :])[
        :, None, None, :
    ]

    cache_rows = prompt_kv.reshape(slots_dev * page_len, heads_dev, 2 * head_dim)
    prompt_scores = (
        jnp.einsum(
            "snhd,khd->snhk",
            queries,
            cache_rows[:, :, :head_dim],
            preferred_element_type=jnp.float32,
        )
        * inv_sqrt
    )
    high_p, sum_p, weights_p = softmax_part(prompt_scores, prompt_visible)
    mixed_p = jnp.einsum(
        "snhk,khd->snhd", weights_p, cache_rows[:, :, head_dim:], preferred_element_type=jnp.float32
    )

    first_row = page_pos * own_count
    own_queries = lax.dynamic_slice_in_dim(queries, first_row, own_count, 0)
    own_lengths = lax.dynamic_slice_in_dim(tail_len, first_row, own_count, 0)
    tail_scores = (
        jnp.einsum(
            "snhd,sthd->snht",
            own_queries,
            tail_kv[..., :head_dim],
            preferred_element_type=jnp.float32,
        )
        * inv_sqrt
    )
    reach_pos = own_lengths[:, None] + jnp.arange(new_count, dtype=jnp.int32)[None, :]
    tail_visible = (
        jnp.arange(tail_max, dtype=jnp.int32)[None, None, None, :] <= reach_pos[:, :, None, None]
    )
    high_t, sum_t, weights_t = softmax_part(tail_scores, tail_visible)
    mixed_t = jnp.einsum(
        "snht,sthd->snhd", weights_t, tail_kv[..., head_dim:], preferred_element_type=jnp.float32
    )

    packed = jnp.concatenate([mixed_p, high_p[..., None], sum_p[..., None]], axis=-1)
    packed = packed.reshape(n_page, rows_own * heads_dev, head_dim + 2)
    got = exchange(packed, "page")
    high_all = got[..., head_dim]
    sum_all = got[..., head_dim + 1]
    mixed_all = got[..., :head_dim]
    high_t = high_t.reshape(rows_own * heads_dev)
    sum_t = sum_t.reshape(rows_own * heads_dev)
    mixed_t = mixed_t.reshape(rows_own * heads_dev, head_dim)
    highest = jnp.maximum(jnp.max(high_all, axis=0), high_t)
    scale_all = jnp.exp(high_all - highest[None, :])
    scale_t = jnp.exp(high_t - highest)
    weight_sum = ordered_sum(sum_all * scale_all) + sum_t * scale_t
    weighted = ordered_sum(mixed_all * scale_all[..., None]) + mixed_t * scale_t[..., None]
    attention = (
        (weighted / weight_sum[..., None])
        .astype(jnp.bfloat16)
        .reshape(rows_own, heads_dev * head_dim)
    )

    contrib = jnp.dot(attention, w_out, preferred_element_type=jnp.float32)
    slice_width = stream_in.shape[2]
    column = blk_pos * slice_width
    own_stream = (
        lax.dynamic_slice_in_dim(stream_in, first_row, own_count, 0)
        .reshape(rows_own, slice_width)
        .astype(jnp.float32)
    )
    contrib = lax.dynamic_update_slice_in_dim(
        contrib, lax.dynamic_slice_in_dim(contrib, column, slice_width, 1) + own_stream, column, 1
    )
    n_blk = width // slice_width
    pieces = contrib.reshape(rows_own, n_blk, slice_width).transpose(1, 0, 2)
    summed = exchange(pieces, "blk", "sum")
    own_bias = lax.dynamic_slice_in_dim(b_out, column, slice_width, 0).astype(jnp.float32)
    res_piece = (summed + own_bias).astype(jnp.bfloat16).astype(jnp.float32)
    gathered = exchange(res_piece, "blk", "gather")
    residual_f = gathered.transpose(1, 0, 2).reshape(rows_own, width)

    row_mean = jnp.mean(residual_f, axis=-1, keepdims=True)
    centred = residual_f - row_mean
    inverse_std = lax.rsqrt(jnp.mean(centred * centred, axis=-1, keepdims=True) + 1e-05)
    scaled = centred * inverse_std

    feature_count = ln_gain.shape[0]
    piece_width = b_down.shape[0]
    scaled3 = scaled.reshape(rows_own, n_page, feature_count)
    res3 = lax.dynamic_slice_in_dim(
        residual_f.reshape(rows_own, n_page, feature_count), blk_pos * piece_width, piece_width, 2
    )
    outgoing = jnp.concatenate([scaled3, res3], axis=-1).transpose(1, 0, 2)
    incoming = exchange(outgoing, "page").reshape(samples * new_count, feature_count + piece_width)
    normed = (
        incoming[:, :feature_count] * ln_gain.astype(jnp.float32) + ln_bias.astype(jnp.float32)
    ).astype(jnp.bfloat16)
    residual_piece = incoming[:, feature_count:]

    up_part = jnp.dot(normed, w_up, preferred_element_type=jnp.float32).astype(jnp.bfloat16)
    up_rows = exchange(up_part.astype(jnp.float32).reshape(n_page, rows_own, -1), "page", "sum")
    hidden_rows = jnp.maximum(up_rows + b_up.astype(jnp.float32), 0.0)
    hidden_rows = hidden_rows.astype(jnp.bfloat16).astype(jnp.float32)
    hidden = exchange(hidden_rows, "page", "gather").reshape(samples * new_count, -1)

    projected = jnp.dot(hidden.astype(jnp.bfloat16), w_down, preferred_element_type=jnp.float32)
    proj_pieces = projected.reshape(samples * new_count, n_blk, piece_width).transpose(1, 0, 2)
    out_share = exchange(proj_pieces, "blk", "sum")
    output = (out_share + residual_piece + b_down.astype(jnp.float32)).astype(jnp.bfloat16)

    score_part = jnp.sum(output.astype(jnp.float32) * w_score.astype(jnp.float32), axis=-1)
    score_part = score_part.reshape(1, samples * new_count)
    blk_sum = ordered_sum(exchange(score_part, "blk", "gather"))
    row_score = ordered_sum(exchange(blk_sum, "page", "gather"))
    return (output.reshape(samples, new_count, piece_width), row_score.reshape(samples, new_count))


def solution(mesh):
    placed = (
        P(None, None, "blk", None),
        P("page", None, "blk", None),
        P("page", None, "blk", None),
        P(),
        P(),
        P(),
        P(),
        P(None, None, "blk"),
        P("blk", None),
        P(),
        P("page"),
        P("page"),
        P("page", "blk"),
        P("blk"),
        P("blk", "page"),
        P(("page", "blk")),
        P(("page", "blk")),
    )
    return jax.shard_map(
        body,
        mesh=mesh,
        in_specs=placed,
        out_specs=(P(None, None, ("page", "blk")), P()),
        check_vma=False,
    )
```

```python
import math

import jax
import jax.numpy as jnp
from jax import lax
from jax.experimental import pallas as pl
from jax.experimental.pallas import tpu as pltpu
from jax.sharding import PartitionSpec as P

NEGATIVE = -1e30
AXES = ("page", "blk")
MESH_ID = pl.DeviceIdType.MESH


def device_on(axis, j):
    return tuple(j if name == axis else lax.axis_index(name) for name in AXES)


def enter(sizes):
    barrier = pltpu.get_barrier_semaphore()
    total = 0
    for axis, n in sizes:
        me = lax.axis_index(axis)
        for k in range(1, n):
            peer = lax.rem(me + k, n)
            pl.semaphore_signal(barrier, inc=1, device_id=device_on(axis, peer), device_id_type=MESH_ID)
        total += n - 1
    pl.semaphore_wait(barrier, total)


def send_round(axis, n, source, buf, send_sem, recv_sem):
    me = lax.axis_index(axis)
    copies = []
    for k in range(1, n):
        peer = lax.rem(me + k, n)
        copy = pltpu.make_async_remote_copy(
            src_ref=source(peer),
            dst_ref=buf.at[me],
            send_sem=send_sem.at[k],
            recv_sem=recv_sem.at[k],
            device_id=device_on(axis, peer),
            device_id_type=MESH_ID,
        )
        copy.start()
        copies.append(copy)
    for copy in copies:
        copy.wait()


def slot_sum(buf, n):
    total = buf[0].astype(jnp.float32)
    for j in range(1, n):
        total = total + buf[j].astype(jnp.float32)
    return total


def exchange_kernel(axis, n, x_ref, o_ref, buf, send_sem, recv_sem):
    me = lax.axis_index(axis)
    buf[me] = x_ref[me]
    enter([(axis, n)])
    send_round(axis, n, lambda peer: x_ref.at[peer], buf, send_sem, recv_sem)
    o_ref[...] = buf[...]


def sum_gather_kernel(axis, n, finish, x_ref, extra_ref, o_ref, buf, gat, sems):
    me = lax.axis_index(axis)
    buf[me] = x_ref[me]
    enter([(axis, n)])
    send_round(axis, n, lambda peer: x_ref.at[peer], buf, sems.at[0], sems.at[1])
    gat[me] = finish(slot_sum(buf, n), extra_ref[...]).astype(gat.dtype)
    send_round(axis, n, lambda peer: gat.at[me], gat, sems.at[2], sems.at[3])
    o_ref[...] = gat[...]


def output_kernel(n_blk, n_page, x_ref, res_ref, bias_ref, score_w_ref, out_ref, score_ref,
                  buf, blk_buf, page_buf, sems):
    me_blk = lax.axis_index("blk")
    me_page = lax.axis_index("page")
    buf[me_blk] = x_ref[me_blk]
    enter([("blk", n_blk), ("page", n_page)])
    send_round("blk", n_blk, lambda peer: x_ref.at[peer], buf, sems.at[0], sems.at[1])
    output = (slot_sum(buf, n_blk) + res_ref[...] + bias_ref[...]).astype(jnp.bfloat16)
    out_ref[...] = output
    blk_buf[me_blk] = jnp.sum(output.astype(jnp.float32) * score_w_ref[...], axis=0, keepdims=True)
    send_round("blk", n_blk, lambda peer: blk_buf.at[me_blk], blk_buf, sems.at[2], sems.at[3])
    page_buf[me_page] = slot_sum(blk_buf, n_blk)
    send_round("page", n_page, lambda peer: page_buf.at[me_page], page_buf, sems.at[4], sems.at[5])
    score_ref[...] = slot_sum(page_buf, n_page)


CALL_IDS = {}


def next_id(axis):
    cid = len(CALL_IDS)
    CALL_IDS[cid] = axis
    return cid


def vmem_specs(count):
    return [pl.BlockSpec(memory_space=pltpu.VMEM)] * count


def exchange(x, axis):
    n = lax.axis_size(axis)
    return pl.pallas_call(
        lambda *refs: exchange_kernel(axis, n, *refs),
        out_shape=jax.ShapeDtypeStruct(x.shape, x.dtype),
        in_specs=vmem_specs(1),
        out_specs=vmem_specs(1)[0],
        scratch_shapes=[
            pltpu.VMEM(x.shape, x.dtype),
            pltpu.SemaphoreType.DMA((n,)),
            pltpu.SemaphoreType.DMA((n,)),
        ],
        compiler_params=pltpu.CompilerParams(collective_id=next_id(axis), has_side_effects=True),
    )(x)


def sum_gather(x, extra, axis, finish, out_dtype):
    n = lax.axis_size(axis)
    return pl.pallas_call(
        lambda *refs: sum_gather_kernel(axis, n, finish, *refs),
        out_shape=jax.ShapeDtypeStruct(x.shape, out_dtype),
        in_specs=vmem_specs(2),
        out_specs=vmem_specs(1)[0],
        scratch_shapes=[
            pltpu.VMEM(x.shape, x.dtype),
            pltpu.VMEM(x.shape, out_dtype),
            pltpu.SemaphoreType.DMA((4, n)),
        ],
        compiler_params=pltpu.CompilerParams(collective_id=next_id(axis), has_side_effects=True),
    )(x, extra)


def output_and_score(x, res, bias, score_w):
    n_blk = lax.axis_size("blk")
    n_page = lax.axis_size("page")
    lanes = x.shape[2]
    return pl.pallas_call(
        lambda *refs: output_kernel(n_blk, n_page, *refs),
        out_shape=(
            jax.ShapeDtypeStruct(x.shape[1:], jnp.bfloat16),
            jax.ShapeDtypeStruct((1, lanes), jnp.float32),
        ),
        in_specs=vmem_specs(4),
        out_specs=tuple(vmem_specs(2)),
        scratch_shapes=[
            pltpu.VMEM(x.shape, jnp.float32),
            pltpu.VMEM((n_blk, 1, lanes), jnp.float32),
            pltpu.VMEM((n_page, 1, lanes), jnp.float32),
            pltpu.SemaphoreType.DMA((6, max(n_blk, n_page))),
        ],
        compiler_params=pltpu.CompilerParams(collective_id=next_id("both"), has_side_effects=True),
    )(x, res, bias, score_w)


def softmax_part(scores, visible):
    masked = jnp.where(visible, scores, NEGATIVE)
    highest = jnp.max(masked, axis=-1)
    weights = jnp.where(visible, jnp.exp(scores - highest[..., None]), 0.0)
    return (highest, jnp.sum(weights, axis=-1), weights.astype(jnp.bfloat16))


def ordered_sum(stack):
    total = stack[0]
    for j in range(1, stack.shape[0]):
        total = total + stack[j]
    return total


def body(
    queries,
    prompt_kv,
    tail_kv,
    page_table,
    prompt_len,
    tail_len,
    sample_prompt,
    stream_in,
    w_out,
    b_out,
    ln_gain,
    ln_bias,
    w_up,
    b_up,
    w_down,
    b_down,
    w_score,
):
    CALL_IDS.clear()
    samples, new_count, heads_dev, head_dim = queries.shape
    slots_dev, page_len = (prompt_kv.shape[0], prompt_kv.shape[1])
    own_count, tail_max = (tail_kv.shape[0], tail_kv.shape[1])
    prompts, pages_max = page_table.shape
    n_page = samples // own_count
    page_pos = lax.axis_index("page")
    blk_pos = lax.axis_index("blk")
    inv_sqrt = 1.0 / math.sqrt(head_dim)
    width = w_out.shape[1]
    rows_own = own_count * new_count

    entries = page_table.reshape(-1)
    slot_ids = page_pos * slots_dev + jnp.arange(slots_dev, dtype=jnp.int32)
    matched = (entries[:, None] == slot_ids[None, :]).astype(jnp.int32)
    owner_index = jnp.sum(matched * jnp.arange(entries.shape[0], dtype=jnp.int32)[:, None], axis=0)
    slot_prompt = owner_index // pages_max
    slot_page = owner_index % pages_max
    prompt_pick = (slot_prompt[:, None] == jnp.arange(prompts, dtype=jnp.int32)[None, :]).astype(
        jnp.int32
    )
    slot_limit = jnp.sum(prompt_pick * prompt_len[None, :], axis=1)
    key_pos = slot_page[:, None] * page_len + jnp.arange(page_len, dtype=jnp.int32)[None, :]
    key_live = (key_pos < slot_limit[:, None]).reshape(-1)
    key_prompt = jnp.repeat(slot_prompt, page_len)
    prompt_visible = ((sample_prompt[:, None] == key_prompt[None, :]) & key_live[None, :])[
        :, None, None, :
    ]

    cache_rows = prompt_kv.reshape(slots_dev * page_len, heads_dev, 2 * head_dim)
    prompt_scores = (
        jnp.einsum(
            "snhd,khd->snhk",
            queries,
            cache_rows[:, :, :head_dim],
            preferred_element_type=jnp.float32,
        )
        * inv_sqrt
    )
    high_p, sum_p, weights_p = softmax_part(prompt_scores, prompt_visible)
    mixed_p = jnp.einsum(
        "snhk,khd->snhd", weights_p, cache_rows[:, :, head_dim:], preferred_element_type=jnp.float32
    )

    first_row = page_pos * own_count
    own_queries = lax.dynamic_slice_in_dim(queries, first_row, own_count, 0)
    own_lengths = lax.dynamic_slice_in_dim(tail_len, first_row, own_count, 0)
    tail_scores = (
        jnp.einsum(
            "snhd,sthd->snht",
            own_queries,
            tail_kv[..., :head_dim],
            preferred_element_type=jnp.float32,
        )
        * inv_sqrt
    )
    reach_pos = own_lengths[:, None] + jnp.arange(new_count, dtype=jnp.int32)[None, :]
    tail_visible = (
        jnp.arange(tail_max, dtype=jnp.int32)[None, None, None, :] <= reach_pos[:, :, None, None]
    )
    high_t, sum_t, weights_t = softmax_part(tail_scores, tail_visible)
    mixed_t = jnp.einsum(
        "snht,sthd->snhd", weights_t, tail_kv[..., head_dim:], preferred_element_type=jnp.float32
    )

    packed = jnp.concatenate([mixed_p, high_p[..., None], sum_p[..., None]], axis=-1)
    packed = packed.reshape(n_page, rows_own * heads_dev, head_dim + 2)
    got = exchange(packed, "page")
    high_all = got[..., head_dim]
    sum_all = got[..., head_dim + 1]
    mixed_all = got[..., :head_dim]
    high_t = high_t.reshape(rows_own * heads_dev)
    sum_t = sum_t.reshape(rows_own * heads_dev)
    mixed_t = mixed_t.reshape(rows_own * heads_dev, head_dim)
    highest = jnp.maximum(jnp.max(high_all, axis=0), high_t)
    scale_all = jnp.exp(high_all - highest[None, :])
    scale_t = jnp.exp(high_t - highest)
    weight_sum = ordered_sum(sum_all * scale_all) + sum_t * scale_t
    weighted = ordered_sum(mixed_all * scale_all[..., None]) + mixed_t * scale_t[..., None]
    attention = (
        (weighted / weight_sum[..., None])
        .astype(jnp.bfloat16)
        .reshape(rows_own, heads_dev * head_dim)
    )

    contrib = jnp.dot(attention, w_out, preferred_element_type=jnp.float32)
    slice_width = stream_in.shape[2]
    column = blk_pos * slice_width
    own_stream = (
        lax.dynamic_slice_in_dim(stream_in, first_row, own_count, 0)
        .reshape(rows_own, slice_width)
        .astype(jnp.float32)
    )
    contrib = lax.dynamic_update_slice_in_dim(
        contrib, lax.dynamic_slice_in_dim(contrib, column, slice_width, 1) + own_stream, column, 1
    )
    n_blk = width // slice_width
    pieces = contrib.reshape(rows_own, n_blk, slice_width).transpose(1, 0, 2)
    own_bias = lax.dynamic_slice_in_dim(b_out, column, slice_width, 0).astype(jnp.float32)
    gathered = sum_gather(
        pieces,
        own_bias.reshape(1, slice_width),
        "blk",
        lambda total, bias: (total + bias).astype(jnp.bfloat16),
        jnp.float32,
    )
    residual_f = gathered.transpose(1, 0, 2).reshape(rows_own, width)

    row_mean = jnp.mean(residual_f, axis=-1, keepdims=True)
    centred = residual_f - row_mean
    inverse_std = lax.rsqrt(jnp.mean(centred * centred, axis=-1, keepdims=True) + 1e-05)
    scaled = centred * inverse_std

    feature_count = ln_gain.shape[0]
    piece_width = b_down.shape[0]
    scaled3 = scaled.reshape(rows_own, n_page, feature_count)
    res3 = lax.dynamic_slice_in_dim(
        residual_f.reshape(rows_own, n_page, feature_count), blk_pos * piece_width, piece_width, 2
    )
    outgoing = jnp.concatenate([scaled3, res3], axis=-1).transpose(1, 0, 2)
    incoming = exchange(outgoing, "page").reshape(samples * new_count, feature_count + piece_width)
    normed = (
        incoming[:, :feature_count] * ln_gain.astype(jnp.float32) + ln_bias.astype(jnp.float32)
    ).astype(jnp.bfloat16)
    residual_piece = incoming[:, feature_count:]

    up_part = jnp.dot(normed, w_up, preferred_element_type=jnp.float32).astype(jnp.bfloat16)
    ff_dev = up_part.shape[1]
    lane_rows = rows_own * ff_dev // feature_count
    up_chunks = up_part.reshape(n_page, lane_rows, feature_count)
    bias_rows = jnp.tile(b_up.astype(jnp.float32).reshape(-1, feature_count), (lane_rows * feature_count // ff_dev, 1))
    hidden = sum_gather(
        up_chunks,
        bias_rows,
        "page",
        lambda total, bias: jnp.maximum(total + bias, 0.0),
        jnp.bfloat16,
    ).reshape(samples * new_count, ff_dev)

    projected_t = jnp.einsum("rf,fk->kr", hidden, w_down, preferred_element_type=jnp.float32)
    proj_pieces = projected_t.reshape(n_blk, piece_width, samples * new_count)
    output_t, row_score = output_and_score(
        proj_pieces,
        residual_piece.T,
        b_down.astype(jnp.float32).reshape(piece_width, 1),
        w_score.astype(jnp.float32).reshape(piece_width, 1),
    )
    output = output_t.T
    return (output.reshape(samples, new_count, piece_width), row_score.reshape(samples, new_count))


def solution(mesh):
    placed = (
        P(None, None, "blk", None),
        P("page", None, "blk", None),
        P("page", None, "blk", None),
        P(),
        P(),
        P(),
        P(),
        P(None, None, "blk"),
        P("blk", None),
        P(),
        P("page"),
        P("page"),
        P("page", "blk"),
        P("blk"),
        P("blk", "page"),
        P(("page", "blk")),
        P(("page", "blk")),
    )
    return jax.shard_map(
        body,
        mesh=mesh,
        in_specs=placed,
        out_specs=(P(None, None, ("page", "blk")), P()),
        check_vma=False,
    )
```

```python
import math

import jax
import jax.numpy as jnp
from jax import lax
from jax.experimental import pallas as pl
from jax.experimental.pallas import tpu as pltpu
from jax.sharding import PartitionSpec as P

NEGATIVE = -1e30
AXES = ("page", "blk")
MESH_ID = pl.DeviceIdType.MESH


def device_on(axis, j):
    return tuple(j if name == axis else lax.axis_index(name) for name in AXES)


def enter(sizes):
    barrier = pltpu.get_barrier_semaphore()
    total = 0
    for axis, n in sizes:
        me = lax.axis_index(axis)
        for k in range(1, n):
            peer = lax.rem(me + k, n)
            pl.semaphore_signal(barrier, inc=1, device_id=device_on(axis, peer), device_id_type=MESH_ID)
        total += n - 1
    pl.semaphore_wait(barrier, total)


def send_round(axis, n, source, buf, send_sem, recv_sem):
    me = lax.axis_index(axis)
    copies = []
    for k in range(1, n):
        peer = lax.rem(me + k, n)
        copy = pltpu.make_async_remote_copy(
            src_ref=source(peer),
            dst_ref=buf.at[me],
            send_sem=send_sem.at[k],
            recv_sem=recv_sem.at[k],
            device_id=device_on(axis, peer),
            device_id_type=MESH_ID,
        )
        copy.start()
        copies.append(copy)
    for copy in copies:
        copy.wait()


def slot_sum(buf, n):
    total = buf[0].astype(jnp.float32)
    for j in range(1, n):
        total = total + buf[j].astype(jnp.float32)
    return total


def exchange_kernel(axis, n, x_ref, o_ref, buf, send_sem, recv_sem):
    me = lax.axis_index(axis)
    buf[me] = x_ref[me]
    enter([(axis, n)])
    send_round(axis, n, lambda peer: x_ref.at[peer], buf, send_sem, recv_sem)
    o_ref[...] = buf[...]


def sum_gather_kernel(axis, n, finish, x_ref, extra_ref, o_ref, buf, gat, sems):
    me = lax.axis_index(axis)
    buf[me] = x_ref[me]
    enter([(axis, n)])
    send_round(axis, n, lambda peer: x_ref.at[peer], buf, sems.at[0], sems.at[1])
    gat[me] = finish(slot_sum(buf, n), extra_ref[...]).astype(gat.dtype)
    send_round(axis, n, lambda peer: gat.at[me], gat, sems.at[2], sems.at[3])
    o_ref[...] = gat[...]


def output_kernel(n_blk, n_page, x_ref, res_ref, bias_ref, score_w_ref, out_ref, score_ref,
                  buf, blk_buf, page_buf, sems):
    me_blk = lax.axis_index("blk")
    me_page = lax.axis_index("page")
    buf[me_blk] = x_ref[me_blk]
    enter([("blk", n_blk), ("page", n_page)])
    send_round("blk", n_blk, lambda peer: x_ref.at[peer], buf, sems.at[0], sems.at[1])
    output = (slot_sum(buf, n_blk) + res_ref[...] + bias_ref[...]).astype(jnp.bfloat16)
    out_ref[...] = output
    blk_buf[me_blk] = jnp.sum(output.astype(jnp.float32) * score_w_ref[...], axis=0, keepdims=True)
    send_round("blk", n_blk, lambda peer: blk_buf.at[me_blk], blk_buf, sems.at[2], sems.at[3])
    page_buf[me_page] = slot_sum(blk_buf, n_blk)
    send_round("page", n_page, lambda peer: page_buf.at[me_page], page_buf, sems.at[4], sems.at[5])
    score_ref[...] = slot_sum(page_buf, n_page)


def attention_out_kernel(n_page, n_blk, heads, part_ref, tail_ref, w_ref, stream_ref, bias_ref,
                         o_ref, recv, contrib, red, gat, sems):
    me_page = lax.axis_index("page")
    me_blk = lax.axis_index("blk")
    recv[me_page] = part_ref[me_page]
    enter([("page", n_page), ("blk", n_blk)])
    send_round("page", n_page, lambda peer: part_ref.at[peer], recv, sems.at[0], sems.at[1])
    hd = w_ref.shape[1] // heads
    tail = tail_ref[...]
    highest = tail[:, hd:2 * hd]
    for j in range(n_page):
        highest = jnp.maximum(highest, recv[j][:, hd:2 * hd])
    scale = jnp.exp(tail[:, hd:2 * hd] - highest)
    weight_sum = tail[:, 2 * hd:] * scale
    weighted = tail[:, :hd] * scale
    for j in range(n_page):
        part = recv[j]
        scale = jnp.exp(part[:, hd:2 * hd] - highest)
        weight_sum = weight_sum + part[:, 2 * hd:] * scale
        weighted = weighted + part[:, :hd] * scale
    attention = (weighted / weight_sum).astype(jnp.bfloat16)
    rows = attention.shape[0] // heads
    if heads > 1:
        attention = jnp.concatenate([attention[h * rows:(h + 1) * rows] for h in range(heads)], axis=1)
    for j in range(n_blk):
        contrib[j] = jnp.dot(attention, w_ref[j], preferred_element_type=jnp.float32)
    red[me_blk] = contrib[me_blk] + stream_ref[...]
    send_round("blk", n_blk, lambda peer: contrib.at[peer], red, sems.at[2], sems.at[3])
    total = slot_sum(red, n_blk) + bias_ref[...]
    gat[me_blk] = total.astype(jnp.bfloat16).astype(jnp.float32)
    send_round("blk", n_blk, lambda peer: gat.at[me_blk], gat, sems.at[4], sems.at[5])
    o_ref[...] = gat[...]


CALL_IDS = {}


def next_id(axis):
    cid = len(CALL_IDS)
    CALL_IDS[cid] = axis
    return cid


def vmem_specs(count):
    return [pl.BlockSpec(memory_space=pltpu.VMEM)] * count


def exchange(x, axis):
    n = lax.axis_size(axis)
    return pl.pallas_call(
        lambda *refs: exchange_kernel(axis, n, *refs),
        out_shape=jax.ShapeDtypeStruct(x.shape, x.dtype),
        in_specs=vmem_specs(1),
        out_specs=vmem_specs(1)[0],
        scratch_shapes=[
            pltpu.VMEM(x.shape, x.dtype),
            pltpu.SemaphoreType.DMA((n,)),
            pltpu.SemaphoreType.DMA((n,)),
        ],
        compiler_params=pltpu.CompilerParams(collective_id=next_id(axis), has_side_effects=True),
    )(x)


def sum_gather(x, extra, axis, finish, out_dtype):
    n = lax.axis_size(axis)
    return pl.pallas_call(
        lambda *refs: sum_gather_kernel(axis, n, finish, *refs),
        out_shape=jax.ShapeDtypeStruct(x.shape, out_dtype),
        in_specs=vmem_specs(2),
        out_specs=vmem_specs(1)[0],
        scratch_shapes=[
            pltpu.VMEM(x.shape, x.dtype),
            pltpu.VMEM(x.shape, out_dtype),
            pltpu.SemaphoreType.DMA((4, n)),
        ],
        compiler_params=pltpu.CompilerParams(collective_id=next_id(axis), has_side_effects=True),
    )(x, extra)


def attention_out(part, tail, w_chunks, stream, bias):
    n_page = lax.axis_size("page")
    n_blk = lax.axis_size("blk")
    heads = w_chunks.shape[1] // (part.shape[2] // 3)
    chunk = (stream.shape[0], w_chunks.shape[2])
    return pl.pallas_call(
        lambda *refs: attention_out_kernel(n_page, n_blk, heads, *refs),
        out_shape=jax.ShapeDtypeStruct((n_blk,) + chunk, jnp.float32),
        in_specs=vmem_specs(5),
        out_specs=vmem_specs(1)[0],
        scratch_shapes=[
            pltpu.VMEM(part.shape, jnp.float32),
            pltpu.VMEM((n_blk,) + chunk, jnp.float32),
            pltpu.VMEM((n_blk,) + chunk, jnp.float32),
            pltpu.VMEM((n_blk,) + chunk, jnp.float32),
            pltpu.SemaphoreType.DMA((6, max(n_blk, n_page))),
        ],
        compiler_params=pltpu.CompilerParams(collective_id=next_id("both"), has_side_effects=True),
    )(part, tail, w_chunks, stream, bias)


def output_and_score(x, res, bias, score_w):
    n_blk = lax.axis_size("blk")
    n_page = lax.axis_size("page")
    lanes = x.shape[2]
    return pl.pallas_call(
        lambda *refs: output_kernel(n_blk, n_page, *refs),
        out_shape=(
            jax.ShapeDtypeStruct(x.shape[1:], jnp.bfloat16),
            jax.ShapeDtypeStruct((1, lanes), jnp.float32),
        ),
        in_specs=vmem_specs(4),
        out_specs=tuple(vmem_specs(2)),
        scratch_shapes=[
            pltpu.VMEM(x.shape, jnp.float32),
            pltpu.VMEM((n_blk, 1, lanes), jnp.float32),
            pltpu.VMEM((n_page, 1, lanes), jnp.float32),
            pltpu.SemaphoreType.DMA((6, max(n_blk, n_page))),
        ],
        compiler_params=pltpu.CompilerParams(collective_id=next_id("both"), has_side_effects=True),
    )(x, res, bias, score_w)


def softmax_part(scores, visible):
    masked = jnp.where(visible, scores, NEGATIVE)
    highest = jnp.max(masked, axis=-1)
    weights = jnp.where(visible, jnp.exp(scores - highest[..., None]), 0.0)
    return (highest, jnp.sum(weights, axis=-1), weights.astype(jnp.bfloat16))


def ordered_sum(stack):
    total = stack[0]
    for j in range(1, stack.shape[0]):
        total = total + stack[j]
    return total


def body(
    queries,
    prompt_kv,
    tail_kv,
    page_table,
    prompt_len,
    tail_len,
    sample_prompt,
    stream_in,
    w_out,
    b_out,
    ln_gain,
    ln_bias,
    w_up,
    b_up,
    w_down,
    b_down,
    w_score,
):
    CALL_IDS.clear()
    samples, new_count, heads_dev, head_dim = queries.shape
    slots_dev, page_len = (prompt_kv.shape[0], prompt_kv.shape[1])
    own_count, tail_max = (tail_kv.shape[0], tail_kv.shape[1])
    prompts, pages_max = page_table.shape
    n_page = samples // own_count
    page_pos = lax.axis_index("page")
    blk_pos = lax.axis_index("blk")
    inv_sqrt = 1.0 / math.sqrt(head_dim)
    width = w_out.shape[1]
    rows_own = own_count * new_count

    entries = page_table.reshape(-1)
    slot_ids = page_pos * slots_dev + jnp.arange(slots_dev, dtype=jnp.int32)
    matched = (entries[:, None] == slot_ids[None, :]).astype(jnp.int32)
    owner_index = jnp.sum(matched * jnp.arange(entries.shape[0], dtype=jnp.int32)[:, None], axis=0)
    slot_prompt = owner_index // pages_max
    slot_page = owner_index % pages_max
    prompt_pick = (slot_prompt[:, None] == jnp.arange(prompts, dtype=jnp.int32)[None, :]).astype(
        jnp.int32
    )
    slot_limit = jnp.sum(prompt_pick * prompt_len[None, :], axis=1)
    key_pos = slot_page[:, None] * page_len + jnp.arange(page_len, dtype=jnp.int32)[None, :]
    key_live = (key_pos < slot_limit[:, None]).reshape(-1)
    key_prompt = jnp.repeat(slot_prompt, page_len)
    prompt_visible = ((sample_prompt[:, None] == key_prompt[None, :]) & key_live[None, :])[
        :, None, None, :
    ]

    cache_rows = prompt_kv.reshape(slots_dev * page_len, heads_dev, 2 * head_dim)
    prompt_scores = (
        jnp.einsum(
            "snhd,khd->snhk",
            queries,
            cache_rows[:, :, :head_dim],
            preferred_element_type=jnp.float32,
        )
        * inv_sqrt
    )
    high_p, sum_p, weights_p = softmax_part(prompt_scores, prompt_visible)
    mixed_p = jnp.einsum(
        "snhk,khd->snhd", weights_p, cache_rows[:, :, head_dim:], preferred_element_type=jnp.float32
    )

    first_row = page_pos * own_count
    own_queries = lax.dynamic_slice_in_dim(queries, first_row, own_count, 0)
    own_lengths = lax.dynamic_slice_in_dim(tail_len, first_row, own_count, 0)
    tail_scores = (
        jnp.einsum(
            "snhd,sthd->snht",
            own_queries,
            tail_kv[..., :head_dim],
            preferred_element_type=jnp.float32,
        )
        * inv_sqrt
    )
    reach_pos = own_lengths[:, None] + jnp.arange(new_count, dtype=jnp.int32)[None, :]
    tail_visible = (
        jnp.arange(tail_max, dtype=jnp.int32)[None, None, None, :] <= reach_pos[:, :, None, None]
    )
    high_t, sum_t, weights_t = softmax_part(tail_scores, tail_visible)
    mixed_t = jnp.einsum(
        "snht,sthd->snhd", weights_t, tail_kv[..., head_dim:], preferred_element_type=jnp.float32
    )

    def pack(mixed, high, total):
        lanes = mixed.shape[-1]
        parts = [mixed, jnp.broadcast_to(high[..., None], mixed.shape), jnp.broadcast_to(total[..., None], mixed.shape)]
        whole = jnp.concatenate(parts, axis=-1)
        whole = whole.reshape(-1, own_count, new_count, heads_dev, 3 * lanes).transpose(0, 3, 1, 2, 4)
        return whole.reshape(-1, heads_dev * rows_own, 3 * lanes)

    slice_width = stream_in.shape[2]
    column = blk_pos * slice_width
    n_blk = width // slice_width
    own_stream = (
        lax.dynamic_slice_in_dim(stream_in, first_row, own_count, 0)
        .reshape(rows_own, slice_width)
        .astype(jnp.float32)
    )
    own_bias = lax.dynamic_slice_in_dim(b_out, column, slice_width, 0).astype(jnp.float32)
    w_chunks = w_out.reshape(heads_dev * head_dim, n_blk, slice_width).transpose(1, 0, 2)
    gathered = attention_out(
        pack(mixed_p, high_p, sum_p),
        pack(mixed_t, high_t, sum_t)[0],
        w_chunks,
        own_stream,
        own_bias.reshape(1, slice_width),
    )
    residual_f = gathered.transpose(1, 0, 2).reshape(rows_own, width)

    row_mean = jnp.mean(residual_f, axis=-1, keepdims=True)
    centred = residual_f - row_mean
    inverse_std = lax.rsqrt(jnp.mean(centred * centred, axis=-1, keepdims=True) + 1e-05)
    scaled = centred * inverse_std

    feature_count = ln_gain.shape[0]
    piece_width = b_down.shape[0]
    scaled3 = scaled.reshape(rows_own, n_page, feature_count)
    res3 = lax.dynamic_slice_in_dim(
        residual_f.reshape(rows_own, n_page, feature_count), blk_pos * piece_width, piece_width, 2
    )
    outgoing = jnp.concatenate([scaled3, res3], axis=-1).transpose(1, 0, 2)
    incoming = exchange(outgoing, "page").reshape(samples * new_count, feature_count + piece_width)
    normed = (
        incoming[:, :feature_count] * ln_gain.astype(jnp.float32) + ln_bias.astype(jnp.float32)
    ).astype(jnp.bfloat16)
    residual_piece = incoming[:, feature_count:]

    up_part = jnp.dot(normed, w_up, preferred_element_type=jnp.float32).astype(jnp.bfloat16)
    ff_dev = up_part.shape[1]
    lane_rows = rows_own * ff_dev // feature_count
    up_chunks = up_part.reshape(n_page, lane_rows, feature_count)
    bias_rows = jnp.tile(b_up.astype(jnp.float32).reshape(-1, feature_count), (lane_rows * feature_count // ff_dev, 1))
    hidden = sum_gather(
        up_chunks,
        bias_rows,
        "page",
        lambda total, bias: jnp.maximum(total + bias, 0.0),
        jnp.bfloat16,
    ).reshape(samples * new_count, ff_dev)

    projected_t = jnp.einsum("rf,fk->kr", hidden, w_down, preferred_element_type=jnp.float32)
    proj_pieces = projected_t.reshape(n_blk, piece_width, samples * new_count)
    output_t, row_score = output_and_score(
        proj_pieces,
        residual_piece.T,
        b_down.astype(jnp.float32).reshape(piece_width, 1),
        w_score.astype(jnp.float32).reshape(piece_width, 1),
    )
    output = output_t.T
    return (output.reshape(samples, new_count, piece_width), row_score.reshape(samples, new_count))


def solution(mesh):
    placed = (
        P(None, None, "blk", None),
        P("page", None, "blk", None),
        P("page", None, "blk", None),
        P(),
        P(),
        P(),
        P(),
        P(None, None, "blk"),
        P("blk", None),
        P(),
        P("page"),
        P("page"),
        P("page", "blk"),
        P("blk"),
        P("blk", "page"),
        P(("page", "blk")),
        P(("page", "blk")),
    )
    return jax.shard_map(
        body,
        mesh=mesh,
        in_specs=placed,
        out_specs=(P(None, None, ("page", "blk")), P()),
        check_vma=False,
    )
```

```python
import math

import jax
import jax.numpy as jnp
from jax import lax
from jax.experimental import pallas as pl
from jax.experimental.pallas import tpu as pltpu
from jax.sharding import PartitionSpec as P

NEGATIVE = -1e30
AXES = ("page", "blk")
MESH_ID = pl.DeviceIdType.MESH


def device_on(axis, j):
    return tuple(j if name == axis else lax.axis_index(name) for name in AXES)


def enter(sizes):
    barrier = pltpu.get_barrier_semaphore()
    total = 0
    for axis, n in sizes:
        me = lax.axis_index(axis)
        for k in range(1, n):
            peer = lax.rem(me + k, n)
            pl.semaphore_signal(barrier, inc=1, device_id=device_on(axis, peer), device_id_type=MESH_ID)
        total += n - 1
    pl.semaphore_wait(barrier, total)


def send_round(axis, n, source, buf, send_sem, recv_sem):
    me = lax.axis_index(axis)
    copies = []
    for k in range(1, n):
        peer = lax.rem(me + k, n)
        copy = pltpu.make_async_remote_copy(
            src_ref=source(peer),
            dst_ref=buf.at[me],
            send_sem=send_sem.at[k],
            recv_sem=recv_sem.at[k],
            device_id=device_on(axis, peer),
            device_id_type=MESH_ID,
        )
        copy.start()
        copies.append(copy)
    for copy in copies:
        copy.wait()


def slot_sum(buf, n):
    total = buf[0].astype(jnp.float32)
    for j in range(1, n):
        total = total + buf[j].astype(jnp.float32)
    return total


def exchange_kernel(axis, n, x_ref, o_ref, buf, send_sem, recv_sem):
    me = lax.axis_index(axis)
    buf[me] = x_ref[me]
    enter([(axis, n)])
    send_round(axis, n, lambda peer: x_ref.at[peer], buf, send_sem, recv_sem)
    o_ref[...] = buf[...]


def sum_gather_kernel(axis, n, finish, x_ref, extra_ref, o_ref, buf, gat, sems):
    me = lax.axis_index(axis)
    buf[me] = x_ref[me]
    enter([(axis, n)])
    send_round(axis, n, lambda peer: x_ref.at[peer], buf, sems.at[0], sems.at[1])
    gat[me] = finish(slot_sum(buf, n), extra_ref[...]).astype(gat.dtype)
    send_round(axis, n, lambda peer: gat.at[me], gat, sems.at[2], sems.at[3])
    o_ref[...] = gat[...]


def output_kernel(n_blk, n_page, x_ref, res_ref, bias_ref, score_w_ref, out_ref, score_ref,
                  buf, blk_buf, page_buf, sems):
    me_blk = lax.axis_index("blk")
    me_page = lax.axis_index("page")
    buf[me_blk] = x_ref[me_blk]
    enter([("blk", n_blk), ("page", n_page)])
    send_round("blk", n_blk, lambda peer: x_ref.at[peer], buf, sems.at[0], sems.at[1])
    output = (slot_sum(buf, n_blk) + res_ref[...] + bias_ref[...]).astype(jnp.bfloat16)
    out_ref[...] = output
    blk_buf[me_blk] = jnp.sum(output.astype(jnp.float32) * score_w_ref[...], axis=0, keepdims=True)
    send_round("blk", n_blk, lambda peer: blk_buf.at[me_blk], blk_buf, sems.at[2], sems.at[3])
    page_buf[me_page] = slot_sum(blk_buf, n_blk)
    send_round("page", n_page, lambda peer: page_buf.at[me_page], page_buf, sems.at[4], sems.at[5])
    score_ref[...] = slot_sum(page_buf, n_page)


def attention_out_kernel(n_page, n_blk, heads, part_ref, tail_ref, w_ref, stream_ref, bias_ref,
                         res_ref, scaled_ref, recv, full, red, gat, sems):
    me_page = lax.axis_index("page")
    me_blk = lax.axis_index("blk")
    recv[me_page] = part_ref[me_page]
    enter([("page", n_page), ("blk", n_blk)])
    send_round("page", n_page, lambda peer: part_ref.at[peer], recv, sems.at[0], sems.at[1])
    hd = w_ref.shape[0] // heads
    tail = tail_ref[...]
    highest = tail[:, hd:2 * hd]
    for j in range(n_page):
        highest = jnp.maximum(highest, recv[j][:, hd:2 * hd])
    scale = jnp.exp(tail[:, hd:2 * hd] - highest)
    weight_sum = tail[:, 2 * hd:] * scale
    weighted = tail[:, :hd] * scale
    for j in range(n_page):
        part = recv[j]
        scale = jnp.exp(part[:, hd:2 * hd] - highest)
        weight_sum = weight_sum + part[:, 2 * hd:] * scale
        weighted = weighted + part[:, :hd] * scale
    attention = (weighted / weight_sum).astype(jnp.bfloat16)
    rows = attention.shape[0] // heads
    if heads > 1:
        attention = jnp.concatenate([attention[h * rows:(h + 1) * rows] for h in range(heads)], axis=1)
    full[...] = jnp.dot(attention, w_ref[...], preferred_element_type=jnp.float32) + stream_ref[...]
    lanes = red.shape[2]
    n_chunk = gat.shape[0]

    def own(ref):
        return ref[:, pl.ds(pl.multiple_of(me_blk * lanes, lanes), lanes)]

    def scatter_copy(t):
        return pltpu.make_async_remote_copy(
            src_ref=full.at[:, pl.ds(t * lanes, lanes)],
            dst_ref=red.at[me_blk],
            send_sem=sems.at[2, t],
            recv_sem=sems.at[3, me_blk],
            device_id=device_on("blk", t),
            device_id_type=MESH_ID,
        )

    def scatter_arrival(s):
        return pltpu.make_async_remote_copy(
            src_ref=full.at[:, pl.ds(0, lanes)],
            dst_ref=red.at[s],
            send_sem=sems.at[2, 0],
            recv_sem=sems.at[3, s],
            device_id=device_on("blk", s),
            device_id_type=MESH_ID,
        )

    def gather_copy(k):
        return pltpu.make_async_remote_copy(
            src_ref=gat.at[me_blk],
            dst_ref=gat.at[me_blk],
            send_sem=sems.at[4, k],
            recv_sem=sems.at[5, me_blk],
            device_id=device_on("blk", lax.rem(me_blk + k, n_blk)),
            device_id_type=MESH_ID,
        )

    def gather_arrival(s):
        return pltpu.make_async_remote_copy(
            src_ref=gat.at[s],
            dst_ref=gat.at[s],
            send_sem=sems.at[4, 0],
            recv_sem=sems.at[5, s],
            device_id=device_on("blk", s),
            device_id_type=MESH_ID,
        )

    for t in range(n_chunk):
        @pl.when(me_blk != t)
        def _():
            scatter_copy(t).start()

    @pl.when(me_blk < n_chunk)
    def _():
        red[me_blk] = own(full)
        for s in range(n_blk):
            @pl.when(me_blk != s)
            def _():
                scatter_arrival(s).wait_recv()
        total = slot_sum(red, n_blk) + own(bias_ref)
        gat[me_blk] = total.astype(jnp.bfloat16).astype(jnp.float32)
        for k in range(1, n_blk):
            gather_copy(k).start()

    for t in range(n_chunk):
        @pl.when(me_blk != t)
        def _():
            scatter_copy(t).wait_send()

    @pl.when(me_blk < n_chunk)
    def _():
        for k in range(1, n_blk):
            gather_copy(k).wait_send()

    for s in range(n_chunk):
        @pl.when(me_blk != s)
        def _():
            gather_arrival(s).wait_recv()

    for t in range(n_chunk):
        res_ref[:, t * lanes:(t + 1) * lanes] = gat[t]
    residual = res_ref[...]
    row_mean = jnp.mean(residual, axis=-1, keepdims=True)
    centred = residual - row_mean
    inverse_std = lax.rsqrt(jnp.mean(centred * centred, axis=-1, keepdims=True) + 1e-05)
    scaled_ref[...] = centred * inverse_std

CALL_IDS = {}


def next_id(axis):
    cid = len(CALL_IDS)
    CALL_IDS[cid] = axis
    return cid


def vmem_specs(count):
    return [pl.BlockSpec(memory_space=pltpu.VMEM)] * count


def exchange(x, axis):
    n = lax.axis_size(axis)
    return pl.pallas_call(
        lambda *refs: exchange_kernel(axis, n, *refs),
        out_shape=jax.ShapeDtypeStruct(x.shape, x.dtype),
        in_specs=vmem_specs(1),
        out_specs=vmem_specs(1)[0],
        scratch_shapes=[
            pltpu.VMEM(x.shape, x.dtype),
            pltpu.SemaphoreType.DMA((n,)),
            pltpu.SemaphoreType.DMA((n,)),
        ],
        compiler_params=pltpu.CompilerParams(collective_id=next_id(axis), has_side_effects=True),
    )(x)


def sum_gather(x, extra, axis, finish, out_dtype):
    n = lax.axis_size(axis)
    return pl.pallas_call(
        lambda *refs: sum_gather_kernel(axis, n, finish, *refs),
        out_shape=jax.ShapeDtypeStruct(x.shape, out_dtype),
        in_specs=vmem_specs(2),
        out_specs=vmem_specs(1)[0],
        scratch_shapes=[
            pltpu.VMEM(x.shape, x.dtype),
            pltpu.VMEM(x.shape, out_dtype),
            pltpu.SemaphoreType.DMA((4, n)),
        ],
        compiler_params=pltpu.CompilerParams(collective_id=next_id(axis), has_side_effects=True),
    )(x, extra)


def attention_out(part, tail, w_out, stream, bias):
    n_page = lax.axis_size("page")
    n_blk = lax.axis_size("blk")
    rows, width = stream.shape
    heads = w_out.shape[0] // (part.shape[2] // 3)
    lanes = 128 * (-(-width // (128 * n_blk)))
    n_chunk = width // lanes
    assert n_chunk * lanes == width
    return pl.pallas_call(
        lambda *refs: attention_out_kernel(n_page, n_blk, heads, *refs),
        out_shape=(
            jax.ShapeDtypeStruct((rows, width), jnp.float32),
            jax.ShapeDtypeStruct((rows, width), jnp.float32),
        ),
        in_specs=vmem_specs(5),
        out_specs=tuple(vmem_specs(2)),
        scratch_shapes=[
            pltpu.VMEM(part.shape, jnp.float32),
            pltpu.VMEM((rows, width), jnp.float32),
            pltpu.VMEM((n_blk, rows, lanes), jnp.float32),
            pltpu.VMEM((n_chunk, rows, lanes), jnp.float32),
            pltpu.SemaphoreType.DMA((6, max(n_blk, n_page))),
        ],
        compiler_params=pltpu.CompilerParams(collective_id=next_id("both"), has_side_effects=True),
    )(part, tail, w_out, stream, bias)


def output_and_score(x, res, bias, score_w):
    n_blk = lax.axis_size("blk")
    n_page = lax.axis_size("page")
    lanes = x.shape[2]
    return pl.pallas_call(
        lambda *refs: output_kernel(n_blk, n_page, *refs),
        out_shape=(
            jax.ShapeDtypeStruct(x.shape[1:], jnp.bfloat16),
            jax.ShapeDtypeStruct((1, lanes), jnp.float32),
        ),
        in_specs=vmem_specs(4),
        out_specs=tuple(vmem_specs(2)),
        scratch_shapes=[
            pltpu.VMEM(x.shape, jnp.float32),
            pltpu.VMEM((n_blk, 1, lanes), jnp.float32),
            pltpu.VMEM((n_page, 1, lanes), jnp.float32),
            pltpu.SemaphoreType.DMA((6, max(n_blk, n_page))),
        ],
        compiler_params=pltpu.CompilerParams(collective_id=next_id("both"), has_side_effects=True),
    )(x, res, bias, score_w)


def softmax_part(scores, visible):
    masked = jnp.where(visible, scores, NEGATIVE)
    highest = jnp.max(masked, axis=-1)
    weights = jnp.where(visible, jnp.exp(scores - highest[..., None]), 0.0)
    return (highest, jnp.sum(weights, axis=-1), weights.astype(jnp.bfloat16))


def ordered_sum(stack):
    total = stack[0]
    for j in range(1, stack.shape[0]):
        total = total + stack[j]
    return total


def body(
    queries,
    prompt_kv,
    tail_kv,
    page_table,
    prompt_len,
    tail_len,
    sample_prompt,
    stream_in,
    w_out,
    b_out,
    ln_gain,
    ln_bias,
    w_up,
    b_up,
    w_down,
    b_down,
    w_score,
):
    CALL_IDS.clear()
    samples, new_count, heads_dev, head_dim = queries.shape
    slots_dev, page_len = (prompt_kv.shape[0], prompt_kv.shape[1])
    own_count, tail_max = (tail_kv.shape[0], tail_kv.shape[1])
    prompts, pages_max = page_table.shape
    n_page = samples // own_count
    page_pos = lax.axis_index("page")
    blk_pos = lax.axis_index("blk")
    inv_sqrt = 1.0 / math.sqrt(head_dim)
    width = w_out.shape[1]
    rows_own = own_count * new_count

    entries = page_table.reshape(-1)
    slot_ids = page_pos * slots_dev + jnp.arange(slots_dev, dtype=jnp.int32)
    matched = (entries[:, None] == slot_ids[None, :]).astype(jnp.int32)
    owner_index = jnp.sum(matched * jnp.arange(entries.shape[0], dtype=jnp.int32)[:, None], axis=0)
    slot_prompt = owner_index // pages_max
    slot_page = owner_index % pages_max
    prompt_pick = (slot_prompt[:, None] == jnp.arange(prompts, dtype=jnp.int32)[None, :]).astype(
        jnp.int32
    )
    slot_limit = jnp.sum(prompt_pick * prompt_len[None, :], axis=1)
    key_pos = slot_page[:, None] * page_len + jnp.arange(page_len, dtype=jnp.int32)[None, :]
    key_live = (key_pos < slot_limit[:, None]).reshape(-1)
    key_prompt = jnp.repeat(slot_prompt, page_len)
    prompt_visible = ((sample_prompt[:, None] == key_prompt[None, :]) & key_live[None, :])[
        :, None, None, :
    ]

    cache_rows = prompt_kv.reshape(slots_dev * page_len, heads_dev, 2 * head_dim)
    prompt_scores = (
        jnp.einsum(
            "snhd,khd->snhk",
            queries,
            cache_rows[:, :, :head_dim],
            preferred_element_type=jnp.float32,
        )
        * inv_sqrt
    )
    high_p, sum_p, weights_p = softmax_part(prompt_scores, prompt_visible)
    mixed_p = jnp.einsum(
        "snhk,khd->snhd", weights_p, cache_rows[:, :, head_dim:], preferred_element_type=jnp.float32
    )

    first_row = page_pos * own_count
    own_queries = lax.dynamic_slice_in_dim(queries, first_row, own_count, 0)
    own_lengths = lax.dynamic_slice_in_dim(tail_len, first_row, own_count, 0)
    tail_scores = (
        jnp.einsum(
            "snhd,sthd->snht",
            own_queries,
            tail_kv[..., :head_dim],
            preferred_element_type=jnp.float32,
        )
        * inv_sqrt
    )
    reach_pos = own_lengths[:, None] + jnp.arange(new_count, dtype=jnp.int32)[None, :]
    tail_visible = (
        jnp.arange(tail_max, dtype=jnp.int32)[None, None, None, :] <= reach_pos[:, :, None, None]
    )
    high_t, sum_t, weights_t = softmax_part(tail_scores, tail_visible)
    mixed_t = jnp.einsum(
        "snht,sthd->snhd", weights_t, tail_kv[..., head_dim:], preferred_element_type=jnp.float32
    )

    def pack(mixed, high, total):
        lanes = mixed.shape[-1]
        parts = [mixed, jnp.broadcast_to(high[..., None], mixed.shape), jnp.broadcast_to(total[..., None], mixed.shape)]
        whole = jnp.concatenate(parts, axis=-1)
        whole = whole.reshape(-1, own_count, new_count, heads_dev, 3 * lanes).transpose(0, 3, 1, 2, 4)
        return whole.reshape(-1, heads_dev * rows_own, 3 * lanes)

    slice_width = stream_in.shape[2]
    column = blk_pos * slice_width
    n_blk = width // slice_width
    own_stream = (
        lax.dynamic_slice_in_dim(stream_in, first_row, own_count, 0)
        .reshape(rows_own, slice_width)
        .astype(jnp.float32)
    )
    stream_full = lax.dynamic_update_slice_in_dim(
        jnp.zeros((rows_own, width), jnp.float32), own_stream, column, 1
    )
    residual_f, scaled = attention_out(
        pack(mixed_p, high_p, sum_p),
        pack(mixed_t, high_t, sum_t)[0],
        w_out,
        stream_full,
        b_out.astype(jnp.float32).reshape(1, width),
    )

    feature_count = ln_gain.shape[0]
    piece_width = b_down.shape[0]
    scaled3 = scaled.reshape(rows_own, n_page, feature_count)
    res3 = lax.dynamic_slice_in_dim(
        residual_f.reshape(rows_own, n_page, feature_count), blk_pos * piece_width, piece_width, 2
    )
    outgoing = jnp.concatenate([scaled3, res3], axis=-1).transpose(1, 0, 2)
    incoming = exchange(outgoing, "page").reshape(samples * new_count, feature_count + piece_width)
    normed = (
        incoming[:, :feature_count] * ln_gain.astype(jnp.float32) + ln_bias.astype(jnp.float32)
    ).astype(jnp.bfloat16)
    residual_piece = incoming[:, feature_count:]

    up_part = jnp.dot(normed, w_up, preferred_element_type=jnp.float32).astype(jnp.bfloat16)
    ff_dev = up_part.shape[1]
    lane_rows = rows_own * ff_dev // feature_count
    up_chunks = up_part.reshape(n_page, lane_rows, feature_count)
    bias_rows = jnp.tile(b_up.astype(jnp.float32).reshape(-1, feature_count), (lane_rows * feature_count // ff_dev, 1))
    hidden = sum_gather(
        up_chunks,
        bias_rows,
        "page",
        lambda total, bias: jnp.maximum(total + bias, 0.0),
        jnp.bfloat16,
    ).reshape(samples * new_count, ff_dev)

    projected_t = jnp.einsum("rf,fk->kr", hidden, w_down, preferred_element_type=jnp.float32)
    proj_pieces = projected_t.reshape(n_blk, piece_width, samples * new_count)
    output_t, row_score = output_and_score(
        proj_pieces,
        residual_piece.T,
        b_down.astype(jnp.float32).reshape(piece_width, 1),
        w_score.astype(jnp.float32).reshape(piece_width, 1),
    )
    output = output_t.T
    return (output.reshape(samples, new_count, piece_width), row_score.reshape(samples, new_count))


def solution(mesh):
    placed = (
        P(None, None, "blk", None),
        P("page", None, "blk", None),
        P("page", None, "blk", None),
        P(),
        P(),
        P(),
        P(),
        P(None, None, "blk"),
        P("blk", None),
        P(),
        P("page"),
        P("page"),
        P("page", "blk"),
        P("blk"),
        P("blk", "page"),
        P(("page", "blk")),
        P(("page", "blk")),
    )
    return jax.shard_map(
        body,
        mesh=mesh,
        in_specs=placed,
        out_specs=(P(None, None, ("page", "blk")), P()),
        check_vma=False,
    )
```

```python
import math

import jax
import jax.numpy as jnp
from jax import lax
from jax.experimental import pallas as pl
from jax.experimental.pallas import tpu as pltpu
from jax.sharding import PartitionSpec as P

NEGATIVE = -1e30
AXES = ("page", "blk")
MESH_ID = pl.DeviceIdType.MESH


def device_on(axis, j):
    return tuple(j if name == axis else lax.axis_index(name) for name in AXES)


def enter(sizes):
    barrier = pltpu.get_barrier_semaphore()
    total = 0
    for axis, n in sizes:
        me = lax.axis_index(axis)
        for k in range(1, n):
            peer = lax.rem(me + k, n)
            pl.semaphore_signal(barrier, inc=1, device_id=device_on(axis, peer), device_id_type=MESH_ID)
        total += n - 1
    pl.semaphore_wait(barrier, total)


def send_round(axis, n, source, buf, send_sem, recv_sem):
    me = lax.axis_index(axis)
    copies = []
    for k in range(1, n):
        peer = lax.rem(me + k, n)
        copy = pltpu.make_async_remote_copy(
            src_ref=source(peer),
            dst_ref=buf.at[me],
            send_sem=send_sem.at[k],
            recv_sem=recv_sem.at[k],
            device_id=device_on(axis, peer),
            device_id_type=MESH_ID,
        )
        copy.start()
        copies.append(copy)
    for copy in copies:
        copy.wait()


def slot_sum(buf, n):
    total = buf[0].astype(jnp.float32)
    for j in range(1, n):
        total = total + buf[j].astype(jnp.float32)
    return total


def exchange_kernel(axis, n, x_ref, o_ref, buf, send_sem, recv_sem):
    me = lax.axis_index(axis)
    buf[me] = x_ref[me]
    enter([(axis, n)])
    send_round(axis, n, lambda peer: x_ref.at[peer], buf, send_sem, recv_sem)
    o_ref[...] = buf[...]


def sum_gather_kernel(axis, n, finish, x_ref, extra_ref, o_ref, buf, gat, sems):
    me = lax.axis_index(axis)
    buf[me] = x_ref[me]
    enter([(axis, n)])
    send_round(axis, n, lambda peer: x_ref.at[peer], buf, sems.at[0], sems.at[1])
    gat[me] = finish(slot_sum(buf, n), extra_ref[...]).astype(gat.dtype)
    send_round(axis, n, lambda peer: gat.at[me], gat, sems.at[2], sems.at[3])
    o_ref[...] = gat[...]


def output_kernel(n_blk, n_page, x_ref, res_ref, bias_ref, score_w_ref, out_ref, score_ref,
                  buf, blk_buf, page_buf, sems):
    me_blk = lax.axis_index("blk")
    me_page = lax.axis_index("page")
    buf[me_blk] = x_ref[me_blk]
    enter([("blk", n_blk), ("page", n_page)])
    send_round("blk", n_blk, lambda peer: x_ref.at[peer], buf, sems.at[0], sems.at[1])
    output = (slot_sum(buf, n_blk) + res_ref[...] + bias_ref[...]).astype(jnp.bfloat16)
    out_ref[...] = output
    blk_buf[me_blk] = jnp.sum(output.astype(jnp.float32) * score_w_ref[...], axis=0, keepdims=True)
    send_round("blk", n_blk, lambda peer: blk_buf.at[me_blk], blk_buf, sems.at[2], sems.at[3])
    page_buf[me_page] = slot_sum(blk_buf, n_blk)
    send_round("page", n_page, lambda peer: page_buf.at[me_page], page_buf, sems.at[4], sems.at[5])
    score_ref[...] = slot_sum(page_buf, n_page)


def attention_out_kernel(n_page, n_blk, heads, part_ref, tail_ref, w_ref, stream_ref, bias_ref,
                         res_ref, scaled_ref, recv, full, red, gat, sems):
    me_page = lax.axis_index("page")
    me_blk = lax.axis_index("blk")
    recv[me_page] = part_ref[me_page]
    enter([("page", n_page), ("blk", n_blk)])
    send_round("page", n_page, lambda peer: part_ref.at[peer], recv, sems.at[0], sems.at[1])
    hd = w_ref.shape[0] // heads
    tail = tail_ref[...]
    highest = tail[:, hd:2 * hd]
    for j in range(n_page):
        highest = jnp.maximum(highest, recv[j][:, hd:2 * hd])
    scale = jnp.exp(tail[:, hd:2 * hd] - highest)
    weight_sum = tail[:, 2 * hd:] * scale
    weighted = tail[:, :hd] * scale
    for j in range(n_page):
        part = recv[j]
        scale = jnp.exp(part[:, hd:2 * hd] - highest)
        weight_sum = weight_sum + part[:, 2 * hd:] * scale
        weighted = weighted + part[:, :hd] * scale
    attention = (weighted / weight_sum).astype(jnp.bfloat16)
    rows = attention.shape[0] // heads
    if heads > 1:
        attention = jnp.concatenate([attention[h * rows:(h + 1) * rows] for h in range(heads)], axis=1)
    full[...] = jnp.dot(attention, w_ref[...], preferred_element_type=jnp.float32) + stream_ref[...]
    lanes = red.shape[2]
    n_chunk = gat.shape[0]

    def own(ref):
        return ref[:, pl.ds(pl.multiple_of(me_blk * lanes, lanes), lanes)]

    def scatter_copy(t):
        return pltpu.make_async_remote_copy(
            src_ref=full.at[:, pl.ds(t * lanes, lanes)],
            dst_ref=red.at[me_blk],
            send_sem=sems.at[2, t],
            recv_sem=sems.at[3, me_blk],
            device_id=device_on("blk", t),
            device_id_type=MESH_ID,
        )

    def scatter_arrival(s):
        return pltpu.make_async_remote_copy(
            src_ref=full.at[:, pl.ds(0, lanes)],
            dst_ref=red.at[s],
            send_sem=sems.at[2, 0],
            recv_sem=sems.at[3, s],
            device_id=device_on("blk", s),
            device_id_type=MESH_ID,
        )

    def gather_copy(k):
        return pltpu.make_async_remote_copy(
            src_ref=gat.at[me_blk],
            dst_ref=gat.at[me_blk],
            send_sem=sems.at[4, k],
            recv_sem=sems.at[5, me_blk],
            device_id=device_on("blk", lax.rem(me_blk + k, n_blk)),
            device_id_type=MESH_ID,
        )

    def gather_arrival(s):
        return pltpu.make_async_remote_copy(
            src_ref=gat.at[s],
            dst_ref=gat.at[s],
            send_sem=sems.at[4, 0],
            recv_sem=sems.at[5, s],
            device_id=device_on("blk", s),
            device_id_type=MESH_ID,
        )

    for t in range(n_chunk):
        @pl.when(me_blk != t)
        def _():
            scatter_copy(t).start()

    @pl.when(me_blk < n_chunk)
    def _():
        red[me_blk] = own(full)
        for s in range(n_blk):
            @pl.when(me_blk != s)
            def _():
                scatter_arrival(s).wait_recv()
        total = slot_sum(red, n_blk) + own(bias_ref)
        gat[me_blk] = total.astype(jnp.bfloat16).astype(jnp.float32)
        for k in range(1, n_blk):
            gather_copy(k).start()

    for t in range(n_chunk):
        @pl.when(me_blk != t)
        def _():
            scatter_copy(t).wait_send()

    @pl.when(me_blk < n_chunk)
    def _():
        for k in range(1, n_blk):
            gather_copy(k).wait_send()

    for s in range(n_chunk):
        @pl.when(me_blk != s)
        def _():
            gather_arrival(s).wait_recv()

    for t in range(n_chunk):
        res_ref[:, t * lanes:(t + 1) * lanes] = gat[t]
    residual = res_ref[...]
    row_mean = jnp.mean(residual, axis=-1, keepdims=True)
    centred = residual - row_mean
    inverse_std = lax.rsqrt(jnp.mean(centred * centred, axis=-1, keepdims=True) + 1e-05)
    scaled_ref[...] = centred * inverse_std

def up_kernel(n_page, x_ref, gain_ref, bias_ref, w_ref, b_up_ref, recv_out_ref, hid_out_ref,
              recv, up_s, red, hid_ref, sems):
    me = lax.axis_index("page")
    recv[me] = x_ref[me]
    enter([("page", n_page)])
    send_round("page", n_page, lambda peer: x_ref.at[peer], recv, sems.at[0], sems.at[1])
    recv_out_ref[...] = recv[...]
    features = gain_ref.shape[1]
    rows = recv.shape[1]
    scaled = jnp.concatenate([recv[j][:, :features] for j in range(n_page)], axis=0)
    normed = (scaled * gain_ref[...] + bias_ref[...]).astype(jnp.bfloat16)
    up_s[...] = jnp.dot(normed, w_ref[...], preferred_element_type=jnp.float32).astype(jnp.bfloat16)
    block = red.shape[1]
    n_recv = up_s.shape[0] // block

    def rows_of(k):
        return pl.ds(k * block, block)

    def scatter_copy(k):
        return pltpu.make_async_remote_copy(
            src_ref=up_s.at[rows_of(k)],
            dst_ref=red.at[me],
            send_sem=sems.at[2, k],
            recv_sem=sems.at[3, me],
            device_id=device_on("page", 2 * k),
            device_id_type=MESH_ID,
        )

    def scatter_arrival(s):
        return pltpu.make_async_remote_copy(
            src_ref=up_s.at[rows_of(0)],
            dst_ref=red.at[s],
            send_sem=sems.at[2, 0],
            recv_sem=sems.at[3, s],
            device_id=device_on("page", s),
            device_id_type=MESH_ID,
        )

    def gather_copy(k, mine):
        return pltpu.make_async_remote_copy(
            src_ref=hid_ref.at[rows_of(mine)],
            dst_ref=hid_ref.at[rows_of(mine)],
            send_sem=sems.at[4, k],
            recv_sem=sems.at[5, mine],
            device_id=device_on("page", lax.rem(me + k, n_page)),
            device_id_type=MESH_ID,
        )

    def gather_arrival(k):
        return pltpu.make_async_remote_copy(
            src_ref=hid_ref.at[rows_of(k)],
            dst_ref=hid_ref.at[rows_of(k)],
            send_sem=sems.at[4, 0],
            recv_sem=sems.at[5, k],
            device_id=device_on("page", 2 * k),
            device_id_type=MESH_ID,
        )

    for k in range(n_recv):
        @pl.when(me != 2 * k)
        def _():
            scatter_copy(k).start()

    mine = me // 2

    @pl.when(me % 2 == 0)
    def _():
        red[me] = up_s[pl.ds(pl.multiple_of(mine * block, block), block)]
        for s in range(n_page):
            @pl.when(me != s)
            def _():
                scatter_arrival(s).wait_recv()
        total = slot_sum(red, n_page) + b_up_ref[...]
        hid_ref[pl.ds(pl.multiple_of(mine * block, block), block)] = jnp.maximum(total, 0.0).astype(
            jnp.bfloat16
        )
        for k in range(1, n_page):
            gather_copy(k, mine).start()

    for k in range(n_recv):
        @pl.when(me != 2 * k)
        def _():
            scatter_copy(k).wait_send()

    @pl.when(me % 2 == 0)
    def _():
        for k in range(1, n_page):
            gather_copy(k, mine).wait_send()

    for k in range(n_recv):
        @pl.when(me != 2 * k)
        def _():
            gather_arrival(k).wait_recv()

    hid_out_ref[...] = hid_ref[...]


CALL_IDS = {}


def next_id(axis):
    cid = len(CALL_IDS)
    CALL_IDS[cid] = axis
    return cid


def vmem_specs(count):
    return [pl.BlockSpec(memory_space=pltpu.VMEM)] * count


def exchange(x, axis):
    n = lax.axis_size(axis)
    return pl.pallas_call(
        lambda *refs: exchange_kernel(axis, n, *refs),
        out_shape=jax.ShapeDtypeStruct(x.shape, x.dtype),
        in_specs=vmem_specs(1),
        out_specs=vmem_specs(1)[0],
        scratch_shapes=[
            pltpu.VMEM(x.shape, x.dtype),
            pltpu.SemaphoreType.DMA((n,)),
            pltpu.SemaphoreType.DMA((n,)),
        ],
        compiler_params=pltpu.CompilerParams(collective_id=next_id(axis), has_side_effects=True),
    )(x)


def sum_gather(x, extra, axis, finish, out_dtype):
    n = lax.axis_size(axis)
    return pl.pallas_call(
        lambda *refs: sum_gather_kernel(axis, n, finish, *refs),
        out_shape=jax.ShapeDtypeStruct(x.shape, out_dtype),
        in_specs=vmem_specs(2),
        out_specs=vmem_specs(1)[0],
        scratch_shapes=[
            pltpu.VMEM(x.shape, x.dtype),
            pltpu.VMEM(x.shape, out_dtype),
            pltpu.SemaphoreType.DMA((4, n)),
        ],
        compiler_params=pltpu.CompilerParams(collective_id=next_id(axis), has_side_effects=True),
    )(x, extra)


def attention_out(part, tail, w_out, stream, bias):
    n_page = lax.axis_size("page")
    n_blk = lax.axis_size("blk")
    rows, width = stream.shape
    heads = w_out.shape[0] // (part.shape[2] // 3)
    lanes = 128 * (-(-width // (128 * n_blk)))
    n_chunk = width // lanes
    assert n_chunk * lanes == width
    return pl.pallas_call(
        lambda *refs: attention_out_kernel(n_page, n_blk, heads, *refs),
        out_shape=(
            jax.ShapeDtypeStruct((rows, width), jnp.float32),
            jax.ShapeDtypeStruct((rows, width), jnp.float32),
        ),
        in_specs=vmem_specs(5),
        out_specs=tuple(vmem_specs(2)),
        scratch_shapes=[
            pltpu.VMEM(part.shape, jnp.float32),
            pltpu.VMEM((rows, width), jnp.float32),
            pltpu.VMEM((n_blk, rows, lanes), jnp.float32),
            pltpu.VMEM((n_chunk, rows, lanes), jnp.float32),
            pltpu.SemaphoreType.DMA((6, max(n_blk, n_page))),
        ],
        compiler_params=pltpu.CompilerParams(collective_id=next_id("both"), has_side_effects=True),
    )(part, tail, w_out, stream, bias)


def up_project(outgoing, gain, bias, w_up, b_up):
    n_page = lax.axis_size("page")
    rows = outgoing.shape[0] * outgoing.shape[1]
    ff = w_up.shape[1]
    block = 2 * rows // n_page
    return pl.pallas_call(
        lambda *refs: up_kernel(n_page, *refs),
        out_shape=(
            jax.ShapeDtypeStruct(outgoing.shape, jnp.float32),
            jax.ShapeDtypeStruct((rows, ff), jnp.bfloat16),
        ),
        in_specs=vmem_specs(5),
        out_specs=tuple(vmem_specs(2)),
        scratch_shapes=[
            pltpu.VMEM(outgoing.shape, jnp.float32),
            pltpu.VMEM((rows, ff), jnp.bfloat16),
            pltpu.VMEM((n_page, block, ff), jnp.bfloat16),
            pltpu.VMEM((rows, ff), jnp.bfloat16),
            pltpu.SemaphoreType.DMA((6, n_page)),
        ],
        compiler_params=pltpu.CompilerParams(collective_id=next_id("page"), has_side_effects=True),
    )(outgoing, gain, bias, w_up, b_up)


def output_and_score(x, res, bias, score_w):
    n_blk = lax.axis_size("blk")
    n_page = lax.axis_size("page")
    lanes = x.shape[2]
    return pl.pallas_call(
        lambda *refs: output_kernel(n_blk, n_page, *refs),
        out_shape=(
            jax.ShapeDtypeStruct(x.shape[1:], jnp.bfloat16),
            jax.ShapeDtypeStruct((1, lanes), jnp.float32),
        ),
        in_specs=vmem_specs(4),
        out_specs=tuple(vmem_specs(2)),
        scratch_shapes=[
            pltpu.VMEM(x.shape, jnp.float32),
            pltpu.VMEM((n_blk, 1, lanes), jnp.float32),
            pltpu.VMEM((n_page, 1, lanes), jnp.float32),
            pltpu.SemaphoreType.DMA((6, max(n_blk, n_page))),
        ],
        compiler_params=pltpu.CompilerParams(collective_id=next_id("both"), has_side_effects=True),
    )(x, res, bias, score_w)


def softmax_part(scores, visible):
    masked = jnp.where(visible, scores, NEGATIVE)
    highest = jnp.max(masked, axis=-1)
    weights = jnp.where(visible, jnp.exp(scores - highest[..., None]), 0.0)
    return (highest, jnp.sum(weights, axis=-1), weights.astype(jnp.bfloat16))


def ordered_sum(stack):
    total = stack[0]
    for j in range(1, stack.shape[0]):
        total = total + stack[j]
    return total


def body(
    queries,
    prompt_kv,
    tail_kv,
    page_table,
    prompt_len,
    tail_len,
    sample_prompt,
    stream_in,
    w_out,
    b_out,
    ln_gain,
    ln_bias,
    w_up,
    b_up,
    w_down,
    b_down,
    w_score,
):
    CALL_IDS.clear()
    samples, new_count, heads_dev, head_dim = queries.shape
    slots_dev, page_len = (prompt_kv.shape[0], prompt_kv.shape[1])
    own_count, tail_max = (tail_kv.shape[0], tail_kv.shape[1])
    prompts, pages_max = page_table.shape
    n_page = samples // own_count
    page_pos = lax.axis_index("page")
    blk_pos = lax.axis_index("blk")
    inv_sqrt = 1.0 / math.sqrt(head_dim)
    width = w_out.shape[1]
    rows_own = own_count * new_count

    entries = page_table.reshape(-1)
    slot_ids = page_pos * slots_dev + jnp.arange(slots_dev, dtype=jnp.int32)
    matched = (entries[:, None] == slot_ids[None, :]).astype(jnp.int32)
    owner_index = jnp.sum(matched * jnp.arange(entries.shape[0], dtype=jnp.int32)[:, None], axis=0)
    slot_prompt = owner_index // pages_max
    slot_page = owner_index % pages_max
    prompt_pick = (slot_prompt[:, None] == jnp.arange(prompts, dtype=jnp.int32)[None, :]).astype(
        jnp.int32
    )
    slot_limit = jnp.sum(prompt_pick * prompt_len[None, :], axis=1)
    key_pos = slot_page[:, None] * page_len + jnp.arange(page_len, dtype=jnp.int32)[None, :]
    key_live = (key_pos < slot_limit[:, None]).reshape(-1)
    key_prompt = jnp.repeat(slot_prompt, page_len)
    prompt_visible = ((sample_prompt[:, None] == key_prompt[None, :]) & key_live[None, :])[
        :, None, None, :
    ]

    cache_rows = prompt_kv.reshape(slots_dev * page_len, heads_dev, 2 * head_dim)
    prompt_scores = (
        jnp.einsum(
            "snhd,khd->snhk",
            queries,
            cache_rows[:, :, :head_dim],
            preferred_element_type=jnp.float32,
        )
        * inv_sqrt
    )
    high_p, sum_p, weights_p = softmax_part(prompt_scores, prompt_visible)
    mixed_p = jnp.einsum(
        "snhk,khd->snhd", weights_p, cache_rows[:, :, head_dim:], preferred_element_type=jnp.float32
    )

    first_row = page_pos * own_count
    own_queries = lax.dynamic_slice_in_dim(queries, first_row, own_count, 0)
    own_lengths = lax.dynamic_slice_in_dim(tail_len, first_row, own_count, 0)
    tail_scores = (
        jnp.einsum(
            "snhd,sthd->snht",
            own_queries,
            tail_kv[..., :head_dim],
            preferred_element_type=jnp.float32,
        )
        * inv_sqrt
    )
    reach_pos = own_lengths[:, None] + jnp.arange(new_count, dtype=jnp.int32)[None, :]
    tail_visible = (
        jnp.arange(tail_max, dtype=jnp.int32)[None, None, None, :] <= reach_pos[:, :, None, None]
    )
    high_t, sum_t, weights_t = softmax_part(tail_scores, tail_visible)
    mixed_t = jnp.einsum(
        "snht,sthd->snhd", weights_t, tail_kv[..., head_dim:], preferred_element_type=jnp.float32
    )

    def pack(mixed, high, total):
        lanes = mixed.shape[-1]
        parts = [mixed, jnp.broadcast_to(high[..., None], mixed.shape), jnp.broadcast_to(total[..., None], mixed.shape)]
        whole = jnp.concatenate(parts, axis=-1)
        whole = whole.reshape(-1, own_count, new_count, heads_dev, 3 * lanes).transpose(0, 3, 1, 2, 4)
        return whole.reshape(-1, heads_dev * rows_own, 3 * lanes)

    slice_width = stream_in.shape[2]
    column = blk_pos * slice_width
    n_blk = width // slice_width
    own_stream = (
        lax.dynamic_slice_in_dim(stream_in, first_row, own_count, 0)
        .reshape(rows_own, slice_width)
        .astype(jnp.float32)
    )
    stream_full = lax.dynamic_update_slice_in_dim(
        jnp.zeros((rows_own, width), jnp.float32), own_stream, column, 1
    )
    residual_f, scaled = attention_out(
        pack(mixed_p, high_p, sum_p),
        pack(mixed_t, high_t, sum_t)[0],
        w_out,
        stream_full,
        b_out.astype(jnp.float32).reshape(1, width),
    )

    feature_count = ln_gain.shape[0]
    piece_width = b_down.shape[0]
    scaled3 = scaled.reshape(rows_own, n_page, feature_count)
    res3 = lax.dynamic_slice_in_dim(
        residual_f.reshape(rows_own, n_page, feature_count), blk_pos * piece_width, piece_width, 2
    )
    outgoing = jnp.concatenate([scaled3, res3], axis=-1).transpose(1, 0, 2)
    incoming, hidden = up_project(
        outgoing,
        ln_gain.astype(jnp.float32).reshape(1, feature_count),
        ln_bias.astype(jnp.float32).reshape(1, feature_count),
        w_up,
        b_up.astype(jnp.float32).reshape(1, -1),
    )
    residual_piece = incoming.reshape(samples * new_count, feature_count + piece_width)[:, feature_count:]

    projected_t = jnp.einsum("rf,fk->kr", hidden, w_down, preferred_element_type=jnp.float32)
    proj_pieces = projected_t.reshape(n_blk, piece_width, samples * new_count)
    output_t, row_score = output_and_score(
        proj_pieces,
        residual_piece.T,
        b_down.astype(jnp.float32).reshape(piece_width, 1),
        w_score.astype(jnp.float32).reshape(piece_width, 1),
    )
    output = output_t.T
    return (output.reshape(samples, new_count, piece_width), row_score.reshape(samples, new_count))


def solution(mesh):
    placed = (
        P(None, None, "blk", None),
        P("page", None, "blk", None),
        P("page", None, "blk", None),
        P(),
        P(),
        P(),
        P(),
        P(None, None, "blk"),
        P("blk", None),
        P(),
        P("page"),
        P("page"),
        P("page", "blk"),
        P("blk"),
        P("blk", "page"),
        P(("page", "blk")),
        P(("page", "blk")),
    )
    return jax.shard_map(
        body,
        mesh=mesh,
        in_specs=placed,
        out_specs=(P(None, None, ("page", "blk")), P()),
        check_vma=False,
    )
```

```python
import math

import jax
import jax.numpy as jnp
from jax import lax
from jax.experimental import pallas as pl
from jax.experimental.pallas import tpu as pltpu
from jax.sharding import PartitionSpec as P

NEGATIVE = -1e30
AXES = ("page", "blk")
MESH_ID = pl.DeviceIdType.MESH


def device_on(axis, j):
    return tuple(j if name == axis else lax.axis_index(name) for name in AXES)


def enter(sizes):
    barrier = pltpu.get_barrier_semaphore()
    total = 0
    for axis, n in sizes:
        me = lax.axis_index(axis)
        for k in range(1, n):
            peer = lax.rem(me + k, n)
            pl.semaphore_signal(barrier, inc=1, device_id=device_on(axis, peer), device_id_type=MESH_ID)
        total += n - 1
    pl.semaphore_wait(barrier, total)


def send_round(axis, n, source, buf, send_sem, recv_sem):
    me = lax.axis_index(axis)
    copies = []
    for k in range(1, n):
        peer = lax.rem(me + k, n)
        copy = pltpu.make_async_remote_copy(
            src_ref=source(peer),
            dst_ref=buf.at[me],
            send_sem=send_sem.at[k],
            recv_sem=recv_sem.at[k],
            device_id=device_on(axis, peer),
            device_id_type=MESH_ID,
        )
        copy.start()
        copies.append(copy)
    for copy in copies:
        copy.wait()


def slot_sum(buf, n):
    total = buf[0].astype(jnp.float32)
    for j in range(1, n):
        total = total + buf[j].astype(jnp.float32)
    return total


def exchange_kernel(axis, n, x_ref, o_ref, buf, send_sem, recv_sem):
    me = lax.axis_index(axis)
    buf[me] = x_ref[me]
    enter([(axis, n)])
    send_round(axis, n, lambda peer: x_ref.at[peer], buf, send_sem, recv_sem)
    o_ref[...] = buf[...]


def sum_gather_kernel(axis, n, finish, x_ref, extra_ref, o_ref, buf, gat, sems):
    me = lax.axis_index(axis)
    buf[me] = x_ref[me]
    enter([(axis, n)])
    send_round(axis, n, lambda peer: x_ref.at[peer], buf, sems.at[0], sems.at[1])
    gat[me] = finish(slot_sum(buf, n), extra_ref[...]).astype(gat.dtype)
    send_round(axis, n, lambda peer: gat.at[me], gat, sems.at[2], sems.at[3])
    o_ref[...] = gat[...]


def output_phase(n_blk, n_page, x_ref, res_t, bias, score_w, out_ref, score_ref,
                 buf, blk_buf, page_buf, sems):
    me_blk = lax.axis_index("blk")
    me_page = lax.axis_index("page")
    buf[me_blk] = x_ref[me_blk]
    send_round("blk", n_blk, lambda peer: x_ref.at[peer], buf, sems.at[0], sems.at[1])
    output = (slot_sum(buf, n_blk) + res_t + bias).astype(jnp.bfloat16)
    out_ref[...] = output
    blk_buf[me_blk] = jnp.sum(output.astype(jnp.float32) * score_w, axis=0, keepdims=True)
    send_round("blk", n_blk, lambda peer: blk_buf.at[me_blk], blk_buf, sems.at[2], sems.at[3])
    page_buf[me_page] = slot_sum(blk_buf, n_blk)
    send_round("page", n_page, lambda peer: page_buf.at[me_page], page_buf, sems.at[4], sems.at[5])
    score_ref[...] = slot_sum(page_buf, n_page)


def attention_out_kernel(n_page, n_blk, heads, part_ref, tail_ref, w_ref, stream_ref, bias_ref,
                         res_ref, scaled_ref, recv, full, red, gat, sems):
    me_page = lax.axis_index("page")
    me_blk = lax.axis_index("blk")
    recv[me_page] = part_ref[me_page]
    enter([("page", n_page), ("blk", n_blk)])
    send_round("page", n_page, lambda peer: part_ref.at[peer], recv, sems.at[0], sems.at[1])
    hd = w_ref.shape[0] // heads
    tail = tail_ref[...]
    highest = tail[:, hd:2 * hd]
    for j in range(n_page):
        highest = jnp.maximum(highest, recv[j][:, hd:2 * hd])
    scale = jnp.exp(tail[:, hd:2 * hd] - highest)
    weight_sum = tail[:, 2 * hd:] * scale
    weighted = tail[:, :hd] * scale
    for j in range(n_page):
        part = recv[j]
        scale = jnp.exp(part[:, hd:2 * hd] - highest)
        weight_sum = weight_sum + part[:, 2 * hd:] * scale
        weighted = weighted + part[:, :hd] * scale
    attention = (weighted / weight_sum).astype(jnp.bfloat16)
    rows = attention.shape[0] // heads
    if heads > 1:
        attention = jnp.concatenate([attention[h * rows:(h + 1) * rows] for h in range(heads)], axis=1)
    full[...] = jnp.dot(attention, w_ref[...], preferred_element_type=jnp.float32) + stream_ref[...]
    lanes = red.shape[2]
    n_chunk = gat.shape[0]

    def own(ref):
        return ref[:, pl.ds(pl.multiple_of(me_blk * lanes, lanes), lanes)]

    def scatter_copy(t):
        return pltpu.make_async_remote_copy(
            src_ref=full.at[:, pl.ds(t * lanes, lanes)],
            dst_ref=red.at[me_blk],
            send_sem=sems.at[2, t],
            recv_sem=sems.at[3, me_blk],
            device_id=device_on("blk", t),
            device_id_type=MESH_ID,
        )

    def scatter_arrival(s):
        return pltpu.make_async_remote_copy(
            src_ref=full.at[:, pl.ds(0, lanes)],
            dst_ref=red.at[s],
            send_sem=sems.at[2, 0],
            recv_sem=sems.at[3, s],
            device_id=device_on("blk", s),
            device_id_type=MESH_ID,
        )

    def gather_copy(k):
        return pltpu.make_async_remote_copy(
            src_ref=gat.at[me_blk],
            dst_ref=gat.at[me_blk],
            send_sem=sems.at[4, k],
            recv_sem=sems.at[5, me_blk],
            device_id=device_on("blk", lax.rem(me_blk + k, n_blk)),
            device_id_type=MESH_ID,
        )

    def gather_arrival(s):
        return pltpu.make_async_remote_copy(
            src_ref=gat.at[s],
            dst_ref=gat.at[s],
            send_sem=sems.at[4, 0],
            recv_sem=sems.at[5, s],
            device_id=device_on("blk", s),
            device_id_type=MESH_ID,
        )

    for t in range(n_chunk):
        @pl.when(me_blk != t)
        def _():
            scatter_copy(t).start()

    @pl.when(me_blk < n_chunk)
    def _():
        red[me_blk] = own(full)
        for s in range(n_blk):
            @pl.when(me_blk != s)
            def _():
                scatter_arrival(s).wait_recv()
        total = slot_sum(red, n_blk) + own(bias_ref)
        gat[me_blk] = total.astype(jnp.bfloat16).astype(jnp.float32)
        for k in range(1, n_blk):
            gather_copy(k).start()

    for t in range(n_chunk):
        @pl.when(me_blk != t)
        def _():
            scatter_copy(t).wait_send()

    @pl.when(me_blk < n_chunk)
    def _():
        for k in range(1, n_blk):
            gather_copy(k).wait_send()

    for s in range(n_chunk):
        @pl.when(me_blk != s)
        def _():
            gather_arrival(s).wait_recv()

    for t in range(n_chunk):
        res_ref[:, t * lanes:(t + 1) * lanes] = gat[t]
    residual = res_ref[...]
    row_mean = jnp.mean(residual, axis=-1, keepdims=True)
    centred = residual - row_mean
    inverse_std = lax.rsqrt(jnp.mean(centred * centred, axis=-1, keepdims=True) + 1e-05)
    scaled_ref[...] = centred * inverse_std

def mlp_kernel(n_page, n_blk, x_ref, gain_ref, bias_ref, w_ref, b_up_ref, pick_ref, w_down_ref,
               b_down_ref, score_w_ref, out_ref, score_ref,
               recv, up_s, red, hid_ref, pieces, out_buf, blk_buf, page_buf, sems):
    me = lax.axis_index("page")
    recv[me] = x_ref[me]
    enter([("page", n_page), ("blk", n_blk)])
    send_round("page", n_page, lambda peer: x_ref.at[peer], recv, sems.at[0], sems.at[1])
    features = gain_ref.shape[1]
    arrived = jnp.concatenate([recv[j] for j in range(n_page)], axis=0)
    scaled = arrived[:, :features]
    normed = (scaled * gain_ref[...] + bias_ref[...]).astype(jnp.bfloat16)
    up_s[...] = jnp.dot(normed, w_ref[...], preferred_element_type=jnp.float32).astype(jnp.bfloat16)
    block = red.shape[1]
    n_recv = up_s.shape[0] // block

    def rows_of(k):
        return pl.ds(k * block, block)

    def scatter_copy(k):
        return pltpu.make_async_remote_copy(
            src_ref=up_s.at[rows_of(k)],
            dst_ref=red.at[me],
            send_sem=sems.at[2, k],
            recv_sem=sems.at[3, me],
            device_id=device_on("page", 2 * k),
            device_id_type=MESH_ID,
        )

    def scatter_arrival(s):
        return pltpu.make_async_remote_copy(
            src_ref=up_s.at[rows_of(0)],
            dst_ref=red.at[s],
            send_sem=sems.at[2, 0],
            recv_sem=sems.at[3, s],
            device_id=device_on("page", s),
            device_id_type=MESH_ID,
        )

    def gather_copy(k, mine):
        return pltpu.make_async_remote_copy(
            src_ref=hid_ref.at[rows_of(mine)],
            dst_ref=hid_ref.at[rows_of(mine)],
            send_sem=sems.at[4, k],
            recv_sem=sems.at[5, mine],
            device_id=device_on("page", lax.rem(me + k, n_page)),
            device_id_type=MESH_ID,
        )

    def gather_arrival(k):
        return pltpu.make_async_remote_copy(
            src_ref=hid_ref.at[rows_of(k)],
            dst_ref=hid_ref.at[rows_of(k)],
            send_sem=sems.at[4, 0],
            recv_sem=sems.at[5, k],
            device_id=device_on("page", 2 * k),
            device_id_type=MESH_ID,
        )

    for k in range(n_recv):
        @pl.when(me != 2 * k)
        def _():
            scatter_copy(k).start()

    mine = me // 2

    @pl.when(me % 2 == 0)
    def _():
        red[me] = up_s[pl.ds(pl.multiple_of(mine * block, block), block)]
        for s in range(n_page):
            @pl.when(me != s)
            def _():
                scatter_arrival(s).wait_recv()
        total = slot_sum(red, n_page) + b_up_ref[...]
        hid_ref[pl.ds(pl.multiple_of(mine * block, block), block)] = jnp.maximum(total, 0.0).astype(
            jnp.bfloat16
        )
        for k in range(1, n_page):
            gather_copy(k, mine).start()

    for k in range(n_recv):
        @pl.when(me != 2 * k)
        def _():
            scatter_copy(k).wait_send()

    @pl.when(me % 2 == 0)
    def _():
        for k in range(1, n_page):
            gather_copy(k, mine).wait_send()

    for k in range(n_recv):
        @pl.when(me != 2 * k)
        def _():
            gather_arrival(k).wait_recv()

    projected_t = lax.dot_general(
        w_down_ref[...], hid_ref[...], (((0,), (1,)), ((), ())), preferred_element_type=jnp.float32
    )
    width = pieces.shape[1]
    for j in range(n_blk):
        pieces[j] = projected_t[j * width:(j + 1) * width]
    res_t = lax.dot_general(
        pick_ref[...], arrived, (((1,), (1,)), ((), ())),
        precision=lax.Precision.HIGHEST, preferred_element_type=jnp.float32,
    )
    output_phase(n_blk, n_page, pieces, res_t, b_down_ref[...], score_w_ref[...], out_ref, score_ref,
                 out_buf, blk_buf, page_buf, sems.at[6:12])


CALL_IDS = {}


def next_id(axis):
    cid = len(CALL_IDS)
    CALL_IDS[cid] = axis
    return cid


def vmem_specs(count):
    return [pl.BlockSpec(memory_space=pltpu.VMEM)] * count


def exchange(x, axis):
    n = lax.axis_size(axis)
    return pl.pallas_call(
        lambda *refs: exchange_kernel(axis, n, *refs),
        out_shape=jax.ShapeDtypeStruct(x.shape, x.dtype),
        in_specs=vmem_specs(1),
        out_specs=vmem_specs(1)[0],
        scratch_shapes=[
            pltpu.VMEM(x.shape, x.dtype),
            pltpu.SemaphoreType.DMA((n,)),
            pltpu.SemaphoreType.DMA((n,)),
        ],
        compiler_params=pltpu.CompilerParams(collective_id=next_id(axis), has_side_effects=True),
    )(x)


def sum_gather(x, extra, axis, finish, out_dtype):
    n = lax.axis_size(axis)
    return pl.pallas_call(
        lambda *refs: sum_gather_kernel(axis, n, finish, *refs),
        out_shape=jax.ShapeDtypeStruct(x.shape, out_dtype),
        in_specs=vmem_specs(2),
        out_specs=vmem_specs(1)[0],
        scratch_shapes=[
            pltpu.VMEM(x.shape, x.dtype),
            pltpu.VMEM(x.shape, out_dtype),
            pltpu.SemaphoreType.DMA((4, n)),
        ],
        compiler_params=pltpu.CompilerParams(collective_id=next_id(axis), has_side_effects=True),
    )(x, extra)


def attention_out(part, tail, w_out, stream, bias):
    n_page = lax.axis_size("page")
    n_blk = lax.axis_size("blk")
    rows, width = stream.shape
    heads = w_out.shape[0] // (part.shape[2] // 3)
    lanes = 128 * (-(-width // (128 * n_blk)))
    n_chunk = width // lanes
    assert n_chunk * lanes == width
    return pl.pallas_call(
        lambda *refs: attention_out_kernel(n_page, n_blk, heads, *refs),
        out_shape=(
            jax.ShapeDtypeStruct((rows, width), jnp.float32),
            jax.ShapeDtypeStruct((rows, width), jnp.float32),
        ),
        in_specs=vmem_specs(5),
        out_specs=tuple(vmem_specs(2)),
        scratch_shapes=[
            pltpu.VMEM(part.shape, jnp.float32),
            pltpu.VMEM((rows, width), jnp.float32),
            pltpu.VMEM((n_blk, rows, lanes), jnp.float32),
            pltpu.VMEM((n_chunk, rows, lanes), jnp.float32),
            pltpu.SemaphoreType.DMA((6, max(n_blk, n_page))),
        ],
        compiler_params=pltpu.CompilerParams(collective_id=next_id("both"), has_side_effects=True),
    )(part, tail, w_out, stream, bias)


def mlp(outgoing, gain, bias, w_up, b_up, pick, w_down, b_down, score_w):
    n_page = lax.axis_size("page")
    n_blk = lax.axis_size("blk")
    rows = outgoing.shape[0] * outgoing.shape[1]
    ff = w_up.shape[1]
    block = 2 * rows // n_page
    width = b_down.shape[0]
    return pl.pallas_call(
        lambda *refs: mlp_kernel(n_page, n_blk, *refs),
        out_shape=(
            jax.ShapeDtypeStruct((width, rows), jnp.bfloat16),
            jax.ShapeDtypeStruct((1, rows), jnp.float32),
        ),
        in_specs=vmem_specs(9),
        out_specs=tuple(vmem_specs(2)),
        scratch_shapes=[
            pltpu.VMEM(outgoing.shape, jnp.float32),
            pltpu.VMEM((rows, ff), jnp.bfloat16),
            pltpu.VMEM((n_page, block, ff), jnp.bfloat16),
            pltpu.VMEM((rows, ff), jnp.bfloat16),
            pltpu.VMEM((n_blk, width, rows), jnp.float32),
            pltpu.VMEM((n_blk, width, rows), jnp.float32),
            pltpu.VMEM((n_blk, 1, rows), jnp.float32),
            pltpu.VMEM((n_page, 1, rows), jnp.float32),
            pltpu.SemaphoreType.DMA((12, max(n_page, n_blk))),
        ],
        compiler_params=pltpu.CompilerParams(collective_id=next_id("both"), has_side_effects=True),
    )(outgoing, gain, bias, w_up, b_up, pick, w_down, b_down, score_w)


def output_and_score(x, res, bias, score_w):
    n_blk = lax.axis_size("blk")
    n_page = lax.axis_size("page")
    lanes = x.shape[2]
    return pl.pallas_call(
        lambda *refs: output_kernel(n_blk, n_page, *refs),
        out_shape=(
            jax.ShapeDtypeStruct(x.shape[1:], jnp.bfloat16),
            jax.ShapeDtypeStruct((1, lanes), jnp.float32),
        ),
        in_specs=vmem_specs(4),
        out_specs=tuple(vmem_specs(2)),
        scratch_shapes=[
            pltpu.VMEM(x.shape, jnp.float32),
            pltpu.VMEM((n_blk, 1, lanes), jnp.float32),
            pltpu.VMEM((n_page, 1, lanes), jnp.float32),
            pltpu.SemaphoreType.DMA((6, max(n_blk, n_page))),
        ],
        compiler_params=pltpu.CompilerParams(collective_id=next_id("both"), has_side_effects=True),
    )(x, res, bias, score_w)


def softmax_part(scores, visible):
    masked = jnp.where(visible, scores, NEGATIVE)
    highest = jnp.max(masked, axis=-1)
    weights = jnp.where(visible, jnp.exp(scores - highest[..., None]), 0.0)
    return (highest, jnp.sum(weights, axis=-1), weights.astype(jnp.bfloat16))


def ordered_sum(stack):
    total = stack[0]
    for j in range(1, stack.shape[0]):
        total = total + stack[j]
    return total


def body(
    queries,
    prompt_kv,
    tail_kv,
    page_table,
    prompt_len,
    tail_len,
    sample_prompt,
    stream_in,
    w_out,
    b_out,
    ln_gain,
    ln_bias,
    w_up,
    b_up,
    w_down,
    b_down,
    w_score,
):
    CALL_IDS.clear()
    samples, new_count, heads_dev, head_dim = queries.shape
    slots_dev, page_len = (prompt_kv.shape[0], prompt_kv.shape[1])
    own_count, tail_max = (tail_kv.shape[0], tail_kv.shape[1])
    prompts, pages_max = page_table.shape
    n_page = samples // own_count
    page_pos = lax.axis_index("page")
    blk_pos = lax.axis_index("blk")
    inv_sqrt = 1.0 / math.sqrt(head_dim)
    width = w_out.shape[1]
    rows_own = own_count * new_count

    entries = page_table.reshape(-1)
    slot_ids = page_pos * slots_dev + jnp.arange(slots_dev, dtype=jnp.int32)
    matched = (entries[:, None] == slot_ids[None, :]).astype(jnp.int32)
    owner_index = jnp.sum(matched * jnp.arange(entries.shape[0], dtype=jnp.int32)[:, None], axis=0)
    slot_prompt = owner_index // pages_max
    slot_page = owner_index % pages_max
    prompt_pick = (slot_prompt[:, None] == jnp.arange(prompts, dtype=jnp.int32)[None, :]).astype(
        jnp.int32
    )
    slot_limit = jnp.sum(prompt_pick * prompt_len[None, :], axis=1)
    key_pos = slot_page[:, None] * page_len + jnp.arange(page_len, dtype=jnp.int32)[None, :]
    key_live = (key_pos < slot_limit[:, None]).reshape(-1)
    key_prompt = jnp.repeat(slot_prompt, page_len)
    prompt_visible = ((sample_prompt[:, None] == key_prompt[None, :]) & key_live[None, :])[
        :, None, None, :
    ]

    cache_rows = prompt_kv.reshape(slots_dev * page_len, heads_dev, 2 * head_dim)
    prompt_scores = (
        jnp.einsum(
            "snhd,khd->snhk",
            queries,
            cache_rows[:, :, :head_dim],
            preferred_element_type=jnp.float32,
        )
        * inv_sqrt
    )
    high_p, sum_p, weights_p = softmax_part(prompt_scores, prompt_visible)
    mixed_p = jnp.einsum(
        "snhk,khd->snhd", weights_p, cache_rows[:, :, head_dim:], preferred_element_type=jnp.float32
    )

    first_row = page_pos * own_count
    own_queries = lax.dynamic_slice_in_dim(queries, first_row, own_count, 0)
    own_lengths = lax.dynamic_slice_in_dim(tail_len, first_row, own_count, 0)
    tail_scores = (
        jnp.einsum(
            "snhd,sthd->snht",
            own_queries,
            tail_kv[..., :head_dim],
            preferred_element_type=jnp.float32,
        )
        * inv_sqrt
    )
    reach_pos = own_lengths[:, None] + jnp.arange(new_count, dtype=jnp.int32)[None, :]
    tail_visible = (
        jnp.arange(tail_max, dtype=jnp.int32)[None, None, None, :] <= reach_pos[:, :, None, None]
    )
    high_t, sum_t, weights_t = softmax_part(tail_scores, tail_visible)
    mixed_t = jnp.einsum(
        "snht,sthd->snhd", weights_t, tail_kv[..., head_dim:], preferred_element_type=jnp.float32
    )

    def pack(mixed, high, total):
        lanes = mixed.shape[-1]
        parts = [mixed, jnp.broadcast_to(high[..., None], mixed.shape), jnp.broadcast_to(total[..., None], mixed.shape)]
        whole = jnp.concatenate(parts, axis=-1)
        whole = whole.reshape(-1, own_count, new_count, heads_dev, 3 * lanes).transpose(0, 3, 1, 2, 4)
        return whole.reshape(-1, heads_dev * rows_own, 3 * lanes)

    slice_width = stream_in.shape[2]
    column = blk_pos * slice_width
    n_blk = width // slice_width
    own_stream = (
        lax.dynamic_slice_in_dim(stream_in, first_row, own_count, 0)
        .reshape(rows_own, slice_width)
        .astype(jnp.float32)
    )
    stream_full = lax.dynamic_update_slice_in_dim(
        jnp.zeros((rows_own, width), jnp.float32), own_stream, column, 1
    )
    residual_f, scaled = attention_out(
        pack(mixed_p, high_p, sum_p),
        pack(mixed_t, high_t, sum_t)[0],
        w_out,
        stream_full,
        b_out.astype(jnp.float32).reshape(1, width),
    )

    feature_count = ln_gain.shape[0]
    piece_width = b_down.shape[0]
    scaled3 = scaled.reshape(rows_own, n_page, feature_count)
    res3 = lax.dynamic_slice_in_dim(
        residual_f.reshape(rows_own, n_page, feature_count), blk_pos * piece_width, piece_width, 2
    )
    outgoing = jnp.concatenate([scaled3, res3], axis=-1).transpose(1, 0, 2)
    lanes_in = feature_count + piece_width
    pick = (
        jnp.arange(lanes_in, dtype=jnp.int32)[None, :]
        == feature_count + jnp.arange(piece_width, dtype=jnp.int32)[:, None]
    ).astype(jnp.float32)
    output_t, row_score = mlp(
        outgoing,
        ln_gain.astype(jnp.float32).reshape(1, feature_count),
        ln_bias.astype(jnp.float32).reshape(1, feature_count),
        w_up,
        b_up.astype(jnp.float32).reshape(1, -1),
        pick,
        w_down,
        b_down.astype(jnp.float32).reshape(piece_width, 1),
        w_score.astype(jnp.float32).reshape(piece_width, 1),
    )
    output = output_t.T
    return (output.reshape(samples, new_count, piece_width), row_score.reshape(samples, new_count))


def solution(mesh):
    placed = (
        P(None, None, "blk", None),
        P("page", None, "blk", None),
        P("page", None, "blk", None),
        P(),
        P(),
        P(),
        P(),
        P(None, None, "blk"),
        P("blk", None),
        P(),
        P("page"),
        P("page"),
        P("page", "blk"),
        P("blk"),
        P("blk", "page"),
        P(("page", "blk")),
        P(("page", "blk")),
    )
    return jax.shard_map(
        body,
        mesh=mesh,
        in_specs=placed,
        out_specs=(P(None, None, ("page", "blk")), P()),
        check_vma=False,
    )
```

```python
import math

import jax
import jax.numpy as jnp
from jax import lax
from jax.experimental import pallas as pl
from jax.experimental.pallas import tpu as pltpu
from jax.sharding import PartitionSpec as P

NEGATIVE = -1e30
AXES = ("page", "blk")
MESH_ID = pl.DeviceIdType.MESH


def device_on(axis, j):
    return tuple(j if name == axis else lax.axis_index(name) for name in AXES)


def greet(sizes):
    barrier = pltpu.get_barrier_semaphore()
    total = 0
    for axis, n in sizes:
        me = lax.axis_index(axis)
        for k in range(1, n):
            peer = lax.rem(me + k, n)
            pl.semaphore_signal(barrier, inc=1, device_id=device_on(axis, peer), device_id_type=MESH_ID)
        total += n - 1
    return total


def enter(sizes):
    pl.semaphore_wait(pltpu.get_barrier_semaphore(), greet(sizes))


def send_round(axis, n, source, buf, send_sem, recv_sem):
    me = lax.axis_index(axis)
    copies = []
    for k in range(1, n):
        peer = lax.rem(me + k, n)
        copy = pltpu.make_async_remote_copy(
            src_ref=source(peer),
            dst_ref=buf.at[me],
            send_sem=send_sem.at[k],
            recv_sem=recv_sem.at[k],
            device_id=device_on(axis, peer),
            device_id_type=MESH_ID,
        )
        copy.start()
        copies.append(copy)
    for copy in copies:
        copy.wait()


def slot_sum(buf, n):
    total = buf[0].astype(jnp.float32)
    for j in range(1, n):
        total = total + buf[j].astype(jnp.float32)
    return total


def exchange_kernel(axis, n, x_ref, o_ref, buf, send_sem, recv_sem):
    me = lax.axis_index(axis)
    buf[me] = x_ref[me]
    enter([(axis, n)])
    send_round(axis, n, lambda peer: x_ref.at[peer], buf, send_sem, recv_sem)
    o_ref[...] = buf[...]


def sum_gather_kernel(axis, n, finish, x_ref, extra_ref, o_ref, buf, gat, sems):
    me = lax.axis_index(axis)
    buf[me] = x_ref[me]
    enter([(axis, n)])
    send_round(axis, n, lambda peer: x_ref.at[peer], buf, sems.at[0], sems.at[1])
    gat[me] = finish(slot_sum(buf, n), extra_ref[...]).astype(gat.dtype)
    send_round(axis, n, lambda peer: gat.at[me], gat, sems.at[2], sems.at[3])
    o_ref[...] = gat[...]


def output_phase(n_blk, n_page, x_ref, res_t, bias, score_w, out_ref, score_ref,
                 buf, blk_buf, page_buf, sems):
    me_blk = lax.axis_index("blk")
    me_page = lax.axis_index("page")
    buf[me_blk] = x_ref[me_blk]
    send_round("blk", n_blk, lambda peer: x_ref.at[peer], buf, sems.at[0], sems.at[1])
    output = (slot_sum(buf, n_blk) + res_t + bias).astype(jnp.bfloat16)
    out_ref[...] = output
    blk_buf[me_blk] = jnp.sum(output.astype(jnp.float32) * score_w, axis=0, keepdims=True)
    send_round("blk", n_blk, lambda peer: blk_buf.at[me_blk], blk_buf, sems.at[2], sems.at[3])
    page_buf[me_page] = slot_sum(blk_buf, n_blk)
    send_round("page", n_page, lambda peer: page_buf.at[me_page], page_buf, sems.at[4], sems.at[5])
    score_ref[...] = slot_sum(page_buf, n_page)


def softmax_rows(scores, visible):
    highest = jnp.max(jnp.where(visible, scores, NEGATIVE), axis=1, keepdims=True)
    weights = jnp.where(visible, jnp.exp(scores - highest), 0.0)
    return highest, jnp.sum(weights, axis=1, keepdims=True), weights.astype(jnp.bfloat16)


def attention_out_kernel(n_page, n_blk, heads, q_ref, kv_ref, tkv_ref, row_code_ref, key_code_ref,
                         t_lo_ref, t_hi_ref, w_ref, stream_ref, bias_ref,
                         res_ref, scaled_ref, part_ref, recv, full, red, gat, sems):
    me_page = lax.axis_index("page")
    me_blk = lax.axis_index("blk")
    expected = greet([("page", n_page), ("blk", n_blk)])
    hd = kv_ref.shape[1] // (2 * heads)
    own_rows = t_lo_ref.shape[0]
    inv_sqrt = 1.0 / math.sqrt(hd)
    visible = row_code_ref[...] == key_code_ref[...]
    position = lax.broadcasted_iota(jnp.int32, (1, tkv_ref.shape[0]), 1)
    tail_visible = (position >= t_lo_ref[...]) & (position <= t_hi_ref[...])
    own_block = pl.ds(pl.multiple_of(me_page * own_rows, own_rows), own_rows)
    contract = (((1,), (1,)), ((), ()))
    tail_parts = []
    for h in range(heads):
        keys = kv_ref[:, 2 * h * hd:(2 * h + 1) * hd]
        values = kv_ref[:, (2 * h + 1) * hd:(2 * h + 2) * hd]
        query = q_ref[:, h * hd:(h + 1) * hd]
        scores = lax.dot_general(query, keys, contract, preferred_element_type=jnp.float32) * inv_sqrt
        high, total, weights = softmax_rows(scores, visible)
        mixed = jnp.dot(weights, values, preferred_element_type=jnp.float32)
        for j in range(n_page):
            rows = slice(j * own_rows, (j + 1) * own_rows)
            part_ref[j, h * own_rows:(h + 1) * own_rows, :] = jnp.concatenate(
                [
                    mixed[rows],
                    jnp.broadcast_to(high[rows], (own_rows, hd)),
                    jnp.broadcast_to(total[rows], (own_rows, hd)),
                ],
                axis=1,
            )
        keys = tkv_ref[:, 2 * h * hd:(2 * h + 1) * hd]
        values = tkv_ref[:, (2 * h + 1) * hd:(2 * h + 2) * hd]
        query = q_ref[own_block, h * hd:(h + 1) * hd]
        scores = lax.dot_general(query, keys, contract, preferred_element_type=jnp.float32) * inv_sqrt
        high, total, weights = softmax_rows(scores, tail_visible)
        mixed = jnp.dot(weights, values, preferred_element_type=jnp.float32)
        tail_parts.append(
            jnp.concatenate(
                [mixed, jnp.broadcast_to(high, (own_rows, hd)), jnp.broadcast_to(total, (own_rows, hd))],
                axis=1,
            )
        )
    tail = jnp.concatenate(tail_parts, axis=0) if heads > 1 else tail_parts[0]
    pl.semaphore_wait(pltpu.get_barrier_semaphore(), expected)
    recv[me_page] = part_ref[me_page]
    send_round("page", n_page, lambda peer: part_ref.at[peer], recv, sems.at[0], sems.at[1])
    highest = tail[:, hd:2 * hd]
    for j in range(n_page):
        highest = jnp.maximum(highest, recv[j][:, hd:2 * hd])
    scale = jnp.exp(tail[:, hd:2 * hd] - highest)
    weight_sum = tail[:, 2 * hd:] * scale
    weighted = tail[:, :hd] * scale
    for j in range(n_page):
        part = recv[j]
        scale = jnp.exp(part[:, hd:2 * hd] - highest)
        weight_sum = weight_sum + part[:, 2 * hd:] * scale
        weighted = weighted + part[:, :hd] * scale
    attention = (weighted / weight_sum).astype(jnp.bfloat16)
    rows = attention.shape[0] // heads
    if heads > 1:
        attention = jnp.concatenate([attention[h * rows:(h + 1) * rows] for h in range(heads)], axis=1)
    full[...] = jnp.dot(attention, w_ref[...], preferred_element_type=jnp.float32) + stream_ref[...]
    lanes = red.shape[2]
    n_chunk = gat.shape[0]

    def own(ref):
        return ref[:, pl.ds(pl.multiple_of(me_blk * lanes, lanes), lanes)]

    def scatter_copy(t):
        return pltpu.make_async_remote_copy(
            src_ref=full.at[:, pl.ds(t * lanes, lanes)],
            dst_ref=red.at[me_blk],
            send_sem=sems.at[2, t],
            recv_sem=sems.at[3, me_blk],
            device_id=device_on("blk", t),
            device_id_type=MESH_ID,
        )

    def scatter_arrival(s):
        return pltpu.make_async_remote_copy(
            src_ref=full.at[:, pl.ds(0, lanes)],
            dst_ref=red.at[s],
            send_sem=sems.at[2, 0],
            recv_sem=sems.at[3, s],
            device_id=device_on("blk", s),
            device_id_type=MESH_ID,
        )

    def gather_copy(k):
        return pltpu.make_async_remote_copy(
            src_ref=gat.at[me_blk],
            dst_ref=gat.at[me_blk],
            send_sem=sems.at[4, k],
            recv_sem=sems.at[5, me_blk],
            device_id=device_on("blk", lax.rem(me_blk + k, n_blk)),
            device_id_type=MESH_ID,
        )

    def gather_arrival(s):
        return pltpu.make_async_remote_copy(
            src_ref=gat.at[s],
            dst_ref=gat.at[s],
            send_sem=sems.at[4, 0],
            recv_sem=sems.at[5, s],
            device_id=device_on("blk", s),
            device_id_type=MESH_ID,
        )

    for t in range(n_chunk):
        @pl.when(me_blk != t)
        def _():
            scatter_copy(t).start()

    @pl.when(me_blk < n_chunk)
    def _():
        red[me_blk] = own(full)
        for s in range(n_blk):
            @pl.when(me_blk != s)
            def _():
                scatter_arrival(s).wait_recv()
        total = slot_sum(red, n_blk) + own(bias_ref)
        gat[me_blk] = total.astype(jnp.bfloat16).astype(jnp.float32)
        for k in range(1, n_blk):
            gather_copy(k).start()

    for t in range(n_chunk):
        @pl.when(me_blk != t)
        def _():
            scatter_copy(t).wait_send()

    @pl.when(me_blk < n_chunk)
    def _():
        for k in range(1, n_blk):
            gather_copy(k).wait_send()

    for s in range(n_chunk):
        @pl.when(me_blk != s)
        def _():
            gather_arrival(s).wait_recv()

    for t in range(n_chunk):
        res_ref[:, t * lanes:(t + 1) * lanes] = gat[t]
    residual = res_ref[...]
    row_mean = jnp.mean(residual, axis=-1, keepdims=True)
    centred = residual - row_mean
    inverse_std = lax.rsqrt(jnp.mean(centred * centred, axis=-1, keepdims=True) + 1e-05)
    scaled_ref[...] = centred * inverse_std

def mlp_kernel(n_page, n_blk, x_ref, gain_ref, bias_ref, w_ref, b_up_ref, pick_ref, w_down_ref,
               b_down_ref, score_w_ref, out_ref, score_ref,
               recv, up_s, red, hid_ref, pieces, out_buf, blk_buf, page_buf, sems):
    me = lax.axis_index("page")
    recv[me] = x_ref[me]
    enter([("page", n_page), ("blk", n_blk)])
    send_round("page", n_page, lambda peer: x_ref.at[peer], recv, sems.at[0], sems.at[1])
    features = gain_ref.shape[1]
    arrived = jnp.concatenate([recv[j] for j in range(n_page)], axis=0)
    scaled = arrived[:, :features]
    normed = (scaled * gain_ref[...] + bias_ref[...]).astype(jnp.bfloat16)
    up_s[...] = jnp.dot(normed, w_ref[...], preferred_element_type=jnp.float32).astype(jnp.bfloat16)
    block = red.shape[1]
    n_recv = up_s.shape[0] // block

    def rows_of(k):
        return pl.ds(k * block, block)

    def scatter_copy(k):
        return pltpu.make_async_remote_copy(
            src_ref=up_s.at[rows_of(k)],
            dst_ref=red.at[me],
            send_sem=sems.at[2, k],
            recv_sem=sems.at[3, me],
            device_id=device_on("page", 2 * k),
            device_id_type=MESH_ID,
        )

    def scatter_arrival(s):
        return pltpu.make_async_remote_copy(
            src_ref=up_s.at[rows_of(0)],
            dst_ref=red.at[s],
            send_sem=sems.at[2, 0],
            recv_sem=sems.at[3, s],
            device_id=device_on("page", s),
            device_id_type=MESH_ID,
        )

    def gather_copy(k, mine):
        return pltpu.make_async_remote_copy(
            src_ref=hid_ref.at[rows_of(mine)],
            dst_ref=hid_ref.at[rows_of(mine)],
            send_sem=sems.at[4, k],
            recv_sem=sems.at[5, mine],
            device_id=device_on("page", lax.rem(me + k, n_page)),
            device_id_type=MESH_ID,
        )

    def gather_arrival(k):
        return pltpu.make_async_remote_copy(
            src_ref=hid_ref.at[rows_of(k)],
            dst_ref=hid_ref.at[rows_of(k)],
            send_sem=sems.at[4, 0],
            recv_sem=sems.at[5, k],
            device_id=device_on("page", 2 * k),
            device_id_type=MESH_ID,
        )

    for k in range(n_recv):
        @pl.when(me != 2 * k)
        def _():
            scatter_copy(k).start()

    mine = me // 2

    @pl.when(me % 2 == 0)
    def _():
        red[me] = up_s[pl.ds(pl.multiple_of(mine * block, block), block)]
        for s in range(n_page):
            @pl.when(me != s)
            def _():
                scatter_arrival(s).wait_recv()
        total = slot_sum(red, n_page) + b_up_ref[...]
        hid_ref[pl.ds(pl.multiple_of(mine * block, block), block)] = jnp.maximum(total, 0.0).astype(
            jnp.bfloat16
        )
        for k in range(1, n_page):
            gather_copy(k, mine).start()

    for k in range(n_recv):
        @pl.when(me != 2 * k)
        def _():
            scatter_copy(k).wait_send()

    @pl.when(me % 2 == 0)
    def _():
        for k in range(1, n_page):
            gather_copy(k, mine).wait_send()

    for k in range(n_recv):
        @pl.when(me != 2 * k)
        def _():
            gather_arrival(k).wait_recv()

    projected_t = lax.dot_general(
        w_down_ref[...], hid_ref[...], (((0,), (1,)), ((), ())), preferred_element_type=jnp.float32
    )
    width = pieces.shape[1]
    for j in range(n_blk):
        pieces[j] = projected_t[j * width:(j + 1) * width]
    res_t = lax.dot_general(
        pick_ref[...], arrived, (((1,), (1,)), ((), ())),
        precision=lax.Precision.HIGHEST, preferred_element_type=jnp.float32,
    )
    output_phase(n_blk, n_page, pieces, res_t, b_down_ref[...], score_w_ref[...], out_ref, score_ref,
                 out_buf, blk_buf, page_buf, sems.at[6:12])


CALL_IDS = {}


def next_id(axis):
    cid = len(CALL_IDS)
    CALL_IDS[cid] = axis
    return cid


def vmem_specs(count):
    return [pl.BlockSpec(memory_space=pltpu.VMEM)] * count


def exchange(x, axis):
    n = lax.axis_size(axis)
    return pl.pallas_call(
        lambda *refs: exchange_kernel(axis, n, *refs),
        out_shape=jax.ShapeDtypeStruct(x.shape, x.dtype),
        in_specs=vmem_specs(1),
        out_specs=vmem_specs(1)[0],
        scratch_shapes=[
            pltpu.VMEM(x.shape, x.dtype),
            pltpu.SemaphoreType.DMA((n,)),
            pltpu.SemaphoreType.DMA((n,)),
        ],
        compiler_params=pltpu.CompilerParams(collective_id=next_id(axis), has_side_effects=True),
    )(x)


def sum_gather(x, extra, axis, finish, out_dtype):
    n = lax.axis_size(axis)
    return pl.pallas_call(
        lambda *refs: sum_gather_kernel(axis, n, finish, *refs),
        out_shape=jax.ShapeDtypeStruct(x.shape, out_dtype),
        in_specs=vmem_specs(2),
        out_specs=vmem_specs(1)[0],
        scratch_shapes=[
            pltpu.VMEM(x.shape, x.dtype),
            pltpu.VMEM(x.shape, out_dtype),
            pltpu.SemaphoreType.DMA((4, n)),
        ],
        compiler_params=pltpu.CompilerParams(collective_id=next_id(axis), has_side_effects=True),
    )(x, extra)


def attention_out(queries, kv, tkv, row_code, key_code, t_lo, t_hi, w_out, stream, bias, head_dim):
    n_page = lax.axis_size("page")
    n_blk = lax.axis_size("blk")
    rows, width = stream.shape
    heads = kv.shape[1] // (2 * head_dim)
    lanes = 128 * (-(-width // (128 * n_blk)))
    n_chunk = width // lanes
    assert n_chunk * lanes == width
    part_shape = (n_page, heads * rows, 3 * head_dim)
    return pl.pallas_call(
        lambda *refs: attention_out_kernel(n_page, n_blk, heads, *refs),
        out_shape=(
            jax.ShapeDtypeStruct((rows, width), jnp.float32),
            jax.ShapeDtypeStruct((rows, width), jnp.float32),
        ),
        in_specs=vmem_specs(10),
        out_specs=tuple(vmem_specs(2)),
        scratch_shapes=[
            pltpu.VMEM(part_shape, jnp.float32),
            pltpu.VMEM(part_shape, jnp.float32),
            pltpu.VMEM((rows, width), jnp.float32),
            pltpu.VMEM((n_blk, rows, lanes), jnp.float32),
            pltpu.VMEM((n_chunk, rows, lanes), jnp.float32),
            pltpu.SemaphoreType.DMA((6, max(n_blk, n_page))),
        ],
        compiler_params=pltpu.CompilerParams(collective_id=next_id("both"), has_side_effects=True),
    )(queries, kv, tkv, row_code, key_code, t_lo, t_hi, w_out, stream, bias)


def mlp(outgoing, gain, bias, w_up, b_up, pick, w_down, b_down, score_w):
    n_page = lax.axis_size("page")
    n_blk = lax.axis_size("blk")
    rows = outgoing.shape[0] * outgoing.shape[1]
    ff = w_up.shape[1]
    block = 2 * rows // n_page
    width = b_down.shape[0]
    return pl.pallas_call(
        lambda *refs: mlp_kernel(n_page, n_blk, *refs),
        out_shape=(
            jax.ShapeDtypeStruct((width, rows), jnp.bfloat16),
            jax.ShapeDtypeStruct((1, rows), jnp.float32),
        ),
        in_specs=vmem_specs(9),
        out_specs=tuple(vmem_specs(2)),
        scratch_shapes=[
            pltpu.VMEM(outgoing.shape, jnp.float32),
            pltpu.VMEM((rows, ff), jnp.bfloat16),
            pltpu.VMEM((n_page, block, ff), jnp.bfloat16),
            pltpu.VMEM((rows, ff), jnp.bfloat16),
            pltpu.VMEM((n_blk, width, rows), jnp.float32),
            pltpu.VMEM((n_blk, width, rows), jnp.float32),
            pltpu.VMEM((n_blk, 1, rows), jnp.float32),
            pltpu.VMEM((n_page, 1, rows), jnp.float32),
            pltpu.SemaphoreType.DMA((12, max(n_page, n_blk))),
        ],
        compiler_params=pltpu.CompilerParams(collective_id=next_id("both"), has_side_effects=True),
    )(outgoing, gain, bias, w_up, b_up, pick, w_down, b_down, score_w)


def output_and_score(x, res, bias, score_w):
    n_blk = lax.axis_size("blk")
    n_page = lax.axis_size("page")
    lanes = x.shape[2]
    return pl.pallas_call(
        lambda *refs: output_kernel(n_blk, n_page, *refs),
        out_shape=(
            jax.ShapeDtypeStruct(x.shape[1:], jnp.bfloat16),
            jax.ShapeDtypeStruct((1, lanes), jnp.float32),
        ),
        in_specs=vmem_specs(4),
        out_specs=tuple(vmem_specs(2)),
        scratch_shapes=[
            pltpu.VMEM(x.shape, jnp.float32),
            pltpu.VMEM((n_blk, 1, lanes), jnp.float32),
            pltpu.VMEM((n_page, 1, lanes), jnp.float32),
            pltpu.SemaphoreType.DMA((6, max(n_blk, n_page))),
        ],
        compiler_params=pltpu.CompilerParams(collective_id=next_id("both"), has_side_effects=True),
    )(x, res, bias, score_w)


def ordered_sum(stack):
    total = stack[0]
    for j in range(1, stack.shape[0]):
        total = total + stack[j]
    return total


def body(
    queries,
    prompt_kv,
    tail_kv,
    page_table,
    prompt_len,
    tail_len,
    sample_prompt,
    stream_in,
    w_out,
    b_out,
    ln_gain,
    ln_bias,
    w_up,
    b_up,
    w_down,
    b_down,
    w_score,
):
    CALL_IDS.clear()
    samples, new_count, heads_dev, head_dim = queries.shape
    slots_dev, page_len = (prompt_kv.shape[0], prompt_kv.shape[1])
    own_count, tail_max = (tail_kv.shape[0], tail_kv.shape[1])
    prompts, pages_max = page_table.shape
    n_page = samples // own_count
    page_pos = lax.axis_index("page")
    blk_pos = lax.axis_index("blk")
    inv_sqrt = 1.0 / math.sqrt(head_dim)
    width = w_out.shape[1]
    rows_own = own_count * new_count

    entries = page_table.reshape(-1)
    slot_ids = page_pos * slots_dev + jnp.arange(slots_dev, dtype=jnp.int32)
    matched = (entries[:, None] == slot_ids[None, :]).astype(jnp.int32)
    owner_index = jnp.sum(matched * jnp.arange(entries.shape[0], dtype=jnp.int32)[:, None], axis=0)
    slot_prompt = owner_index // pages_max
    slot_page = owner_index % pages_max
    prompt_pick = (slot_prompt[:, None] == jnp.arange(prompts, dtype=jnp.int32)[None, :]).astype(
        jnp.int32
    )
    slot_limit = jnp.sum(prompt_pick * prompt_len[None, :], axis=1)
    key_pos = slot_page[:, None] * page_len + jnp.arange(page_len, dtype=jnp.int32)[None, :]
    key_live = (key_pos < slot_limit[:, None]).reshape(-1)
    key_prompt = jnp.repeat(slot_prompt, page_len)
    key_code = jnp.where(key_live, key_prompt, -1).astype(jnp.int32).reshape(1, -1)
    row_code = jnp.repeat(sample_prompt, new_count).astype(jnp.int32).reshape(-1, 1)

    first_row = page_pos * own_count
    own_lengths = lax.dynamic_slice_in_dim(tail_len, first_row, own_count, 0)
    local_row = jnp.arange(rows_own, dtype=jnp.int32)
    t_lo = (local_row // new_count) * tail_max
    t_hi = t_lo + jnp.repeat(own_lengths, new_count) + local_row % new_count

    slice_width = stream_in.shape[2]
    column = blk_pos * slice_width
    own_stream = (
        lax.dynamic_slice_in_dim(stream_in, first_row, own_count, 0)
        .reshape(rows_own, slice_width)
        .astype(jnp.float32)
    )
    stream_full = lax.dynamic_update_slice_in_dim(
        jnp.zeros((rows_own, width), jnp.float32), own_stream, column, 1
    )
    residual_f, scaled = attention_out(
        queries.reshape(samples * new_count, heads_dev * head_dim),
        prompt_kv.reshape(slots_dev * page_len, heads_dev * 2 * head_dim),
        tail_kv.reshape(own_count * tail_max, heads_dev * 2 * head_dim),
        row_code,
        key_code,
        t_lo.reshape(-1, 1),
        t_hi.reshape(-1, 1),
        w_out,
        stream_full,
        b_out.astype(jnp.float32).reshape(1, width),
        head_dim,
    )

    feature_count = ln_gain.shape[0]
    piece_width = b_down.shape[0]
    scaled3 = scaled.reshape(rows_own, n_page, feature_count)
    res3 = lax.dynamic_slice_in_dim(
        residual_f.reshape(rows_own, n_page, feature_count), blk_pos * piece_width, piece_width, 2
    )
    outgoing = jnp.concatenate([scaled3, res3], axis=-1).transpose(1, 0, 2)
    lanes_in = feature_count + piece_width
    pick = (
        jnp.arange(lanes_in, dtype=jnp.int32)[None, :]
        == feature_count + jnp.arange(piece_width, dtype=jnp.int32)[:, None]
    ).astype(jnp.float32)
    output_t, row_score = mlp(
        outgoing,
        ln_gain.astype(jnp.float32).reshape(1, feature_count),
        ln_bias.astype(jnp.float32).reshape(1, feature_count),
        w_up,
        b_up.astype(jnp.float32).reshape(1, -1),
        pick,
        w_down,
        b_down.astype(jnp.float32).reshape(piece_width, 1),
        w_score.astype(jnp.float32).reshape(piece_width, 1),
    )
    output = output_t.T
    return (output.reshape(samples, new_count, piece_width), row_score.reshape(samples, new_count))


def solution(mesh):
    placed = (
        P(None, None, "blk", None),
        P("page", None, "blk", None),
        P("page", None, "blk", None),
        P(),
        P(),
        P(),
        P(),
        P(None, None, "blk"),
        P("blk", None),
        P(),
        P("page"),
        P("page"),
        P("page", "blk"),
        P("blk"),
        P("blk", "page"),
        P(("page", "blk")),
        P(("page", "blk")),
    )
    return jax.shard_map(
        body,
        mesh=mesh,
        in_specs=placed,
        out_specs=(P(None, None, ("page", "blk")), P()),
        check_vma=False,
    )
```

```python
import math

import jax
import jax.numpy as jnp
from jax import lax
from jax.experimental import pallas as pl
from jax.experimental.pallas import tpu as pltpu
from jax.sharding import PartitionSpec as P

NEGATIVE = -1e30
AXES = ("page", "blk")
MESH_ID = pl.DeviceIdType.MESH


def device_on(axis, j):
    return tuple(j if name == axis else lax.axis_index(name) for name in AXES)


def greet(sizes):
    barrier = pltpu.get_barrier_semaphore()
    total = 0
    for axis, n in sizes:
        me = lax.axis_index(axis)
        for k in range(1, n):
            peer = lax.rem(me + k, n)
            pl.semaphore_signal(barrier, inc=1, device_id=device_on(axis, peer), device_id_type=MESH_ID)
        total += n - 1
    return total


def enter(sizes):
    pl.semaphore_wait(pltpu.get_barrier_semaphore(), greet(sizes))


def send_round(axis, n, source, buf, send_sem, recv_sem):
    me = lax.axis_index(axis)
    copies = []
    for k in range(1, n):
        peer = lax.rem(me + k, n)
        copy = pltpu.make_async_remote_copy(
            src_ref=source(peer),
            dst_ref=buf.at[me],
            send_sem=send_sem.at[k],
            recv_sem=recv_sem.at[k],
            device_id=device_on(axis, peer),
            device_id_type=MESH_ID,
        )
        copy.start()
        copies.append(copy)
    for copy in copies:
        copy.wait()


def slot_sum(buf, n):
    total = buf[0].astype(jnp.float32)
    for j in range(1, n):
        total = total + buf[j].astype(jnp.float32)
    return total


def exchange_kernel(axis, n, x_ref, o_ref, buf, send_sem, recv_sem):
    me = lax.axis_index(axis)
    buf[me] = x_ref[me]
    enter([(axis, n)])
    send_round(axis, n, lambda peer: x_ref.at[peer], buf, send_sem, recv_sem)
    o_ref[...] = buf[...]


def sum_gather_kernel(axis, n, finish, x_ref, extra_ref, o_ref, buf, gat, sems):
    me = lax.axis_index(axis)
    buf[me] = x_ref[me]
    enter([(axis, n)])
    send_round(axis, n, lambda peer: x_ref.at[peer], buf, sems.at[0], sems.at[1])
    gat[me] = finish(slot_sum(buf, n), extra_ref[...]).astype(gat.dtype)
    send_round(axis, n, lambda peer: gat.at[me], gat, sems.at[2], sems.at[3])
    o_ref[...] = gat[...]


def output_phase(n_blk, n_page, x_ref, res_t, bias, score_w, out_ref, score_ref,
                 buf, blk_buf, page_buf, sems):
    me_blk = lax.axis_index("blk")
    me_page = lax.axis_index("page")
    buf[me_blk] = x_ref[me_blk]
    send_round("blk", n_blk, lambda peer: x_ref.at[peer], buf, sems.at[0], sems.at[1])
    output = (slot_sum(buf, n_blk) + res_t + bias).astype(jnp.bfloat16)
    out_ref[...] = output
    blk_buf[me_blk] = jnp.sum(output.astype(jnp.float32) * score_w, axis=0, keepdims=True)
    send_round("blk", n_blk, lambda peer: blk_buf.at[me_blk], blk_buf, sems.at[2], sems.at[3])
    page_buf[me_page] = slot_sum(blk_buf, n_blk)
    send_round("page", n_page, lambda peer: page_buf.at[me_page], page_buf, sems.at[4], sems.at[5])
    score_ref[...] = slot_sum(page_buf, n_page)


def softmax_rows(scores, visible):
    highest = jnp.max(jnp.where(visible, scores, NEGATIVE), axis=1, keepdims=True)
    weights = jnp.where(visible, jnp.exp(scores - highest), 0.0)
    return highest, jnp.sum(weights, axis=1, keepdims=True), weights.astype(jnp.bfloat16)


def attention_out_kernel(n_page, n_blk, heads, q_ref, kv_ref, tkv_ref, row_code_ref, key_code_ref,
                         t_lo_ref, t_hi_ref, w_ref, stream_ref,
                         res_ref, scaled_ref, part_ref, recv, full, res_s, red, gat, sems):
    me_page = lax.axis_index("page")
    me_blk = lax.axis_index("blk")
    expected = greet([("page", n_page), ("blk", n_blk)])
    hd = kv_ref.shape[1] // (2 * heads)
    own_rows = t_lo_ref.shape[0]
    inv_sqrt = 1.0 / math.sqrt(hd)
    visible = row_code_ref[...] == key_code_ref[...]
    position = lax.broadcasted_iota(jnp.int32, (1, tkv_ref.shape[0]), 1)
    tail_visible = (position >= t_lo_ref[...]) & (position <= t_hi_ref[...])
    own_block = pl.ds(pl.multiple_of(me_page * own_rows, own_rows), own_rows)
    contract = (((1,), (1,)), ((), ()))
    tail_parts = []
    for h in range(heads):
        keys = kv_ref[:, 2 * h * hd:(2 * h + 1) * hd]
        values = kv_ref[:, (2 * h + 1) * hd:(2 * h + 2) * hd]
        query = q_ref[:, h * hd:(h + 1) * hd]
        scores = lax.dot_general(query, keys, contract, preferred_element_type=jnp.float32) * inv_sqrt
        high, total, weights = softmax_rows(scores, visible)
        mixed = jnp.dot(weights, values, preferred_element_type=jnp.float32)
        for j in range(n_page):
            rows = slice(j * own_rows, (j + 1) * own_rows)
            part_ref[j, h * own_rows:(h + 1) * own_rows, :] = jnp.concatenate(
                [
                    mixed[rows],
                    jnp.broadcast_to(high[rows], (own_rows, hd)),
                    jnp.broadcast_to(total[rows], (own_rows, hd)),
                ],
                axis=1,
            )
        keys = tkv_ref[:, 2 * h * hd:(2 * h + 1) * hd]
        values = tkv_ref[:, (2 * h + 1) * hd:(2 * h + 2) * hd]
        query = q_ref[own_block, h * hd:(h + 1) * hd]
        scores = lax.dot_general(query, keys, contract, preferred_element_type=jnp.float32) * inv_sqrt
        high, total, weights = softmax_rows(scores, tail_visible)
        mixed = jnp.dot(weights, values, preferred_element_type=jnp.float32)
        tail_parts.append(
            jnp.concatenate(
                [mixed, jnp.broadcast_to(high, (own_rows, hd)), jnp.broadcast_to(total, (own_rows, hd))],
                axis=1,
            )
        )
    tail = jnp.concatenate(tail_parts, axis=0) if heads > 1 else tail_parts[0]
    pl.semaphore_wait(pltpu.get_barrier_semaphore(), expected)
    recv[me_page] = part_ref[me_page]
    send_round("page", n_page, lambda peer: part_ref.at[peer], recv, sems.at[0], sems.at[1])
    highest = tail[:, hd:2 * hd]
    for j in range(n_page):
        highest = jnp.maximum(highest, recv[j][:, hd:2 * hd])
    scale = jnp.exp(tail[:, hd:2 * hd] - highest)
    weight_sum = tail[:, 2 * hd:] * scale
    weighted = tail[:, :hd] * scale
    for j in range(n_page):
        part = recv[j]
        scale = jnp.exp(part[:, hd:2 * hd] - highest)
        weight_sum = weight_sum + part[:, 2 * hd:] * scale
        weighted = weighted + part[:, :hd] * scale
    attention = (weighted / weight_sum).astype(jnp.bfloat16)
    rows = attention.shape[0] // heads
    if heads > 1:
        attention = jnp.concatenate([attention[h * rows:(h + 1) * rows] for h in range(heads)], axis=1)
    full[...] = jnp.dot(attention, w_ref[...], preferred_element_type=jnp.float32) + stream_ref[...]
    lanes = red.shape[2]
    n_chunk = gat.shape[0]

    def own(ref):
        return ref[:, pl.ds(pl.multiple_of(me_blk * lanes, lanes), lanes)]

    def scatter_copy(t):
        return pltpu.make_async_remote_copy(
            src_ref=full.at[:, pl.ds(t * lanes, lanes)],
            dst_ref=red.at[me_blk],
            send_sem=sems.at[2, t],
            recv_sem=sems.at[3, me_blk],
            device_id=device_on("blk", t),
            device_id_type=MESH_ID,
        )

    def scatter_arrival(s):
        return pltpu.make_async_remote_copy(
            src_ref=full.at[:, pl.ds(0, lanes)],
            dst_ref=red.at[s],
            send_sem=sems.at[2, 0],
            recv_sem=sems.at[3, s],
            device_id=device_on("blk", s),
            device_id_type=MESH_ID,
        )

    def gather_copy(k):
        return pltpu.make_async_remote_copy(
            src_ref=gat.at[me_blk],
            dst_ref=gat.at[me_blk],
            send_sem=sems.at[4, k],
            recv_sem=sems.at[5, me_blk],
            device_id=device_on("blk", lax.rem(me_blk + k, n_blk)),
            device_id_type=MESH_ID,
        )

    def gather_arrival(s):
        return pltpu.make_async_remote_copy(
            src_ref=gat.at[s],
            dst_ref=gat.at[s],
            send_sem=sems.at[4, 0],
            recv_sem=sems.at[5, s],
            device_id=device_on("blk", s),
            device_id_type=MESH_ID,
        )

    for t in range(n_chunk):
        @pl.when(me_blk != t)
        def _():
            scatter_copy(t).start()

    @pl.when(me_blk < n_chunk)
    def _():
        red[me_blk] = own(full)
        for s in range(n_blk):
            @pl.when(me_blk != s)
            def _():
                scatter_arrival(s).wait_recv()
        total = slot_sum(red, n_blk)
        gat[me_blk] = total.astype(jnp.bfloat16).astype(jnp.float32)
        for k in range(1, n_blk):
            gather_copy(k).start()

    for t in range(n_chunk):
        @pl.when(me_blk != t)
        def _():
            scatter_copy(t).wait_send()

    @pl.when(me_blk < n_chunk)
    def _():
        for k in range(1, n_blk):
            gather_copy(k).wait_send()

    for s in range(n_chunk):
        @pl.when(me_blk != s)
        def _():
            gather_arrival(s).wait_recv()

    for t in range(n_chunk):
        res_s[:, t * lanes:(t + 1) * lanes] = gat[t]
    residual = res_s[...]
    row_mean = jnp.mean(residual, axis=-1, keepdims=True)
    centred = residual - row_mean
    inverse_std = lax.rsqrt(jnp.mean(centred * centred, axis=-1, keepdims=True) + 1e-05)
    scaled = centred * inverse_std
    group = scaled_ref.shape[2]
    for q in range(n_page):
        scaled_ref[q] = scaled[:, q * group:(q + 1) * group]
        res_ref[q] = residual[:, q * group:(q + 1) * group]

def mlp_kernel(n_page, n_blk, x_ref, r_ref, vec_ref, w_ref, w_down_ref, col_ref, out_ref, score_ref,
               recv, recv_r, up_s, red, hid_ref, pieces, out_buf, blk_buf, page_buf, sems):
    me = lax.axis_index("page")
    recv[me] = x_ref[me]
    recv_r[me] = r_ref[me]
    enter([("page", n_page), ("blk", n_blk)])
    copies = []
    for k in range(1, n_page):
        peer = lax.rem(me + k, n_page)
        for src, dst, idx in ((x_ref, recv, 0), (r_ref, recv_r, 12)):
            copy = pltpu.make_async_remote_copy(
                src_ref=src.at[peer],
                dst_ref=dst.at[me],
                send_sem=sems.at[idx, k],
                recv_sem=sems.at[idx + 1, k],
                device_id=device_on("page", peer),
                device_id_type=MESH_ID,
            )
            copy.start()
            copies.append(copy)
    for copy in copies:
        copy.wait()
    features = x_ref.shape[2]
    pad = -(-features // 128) * 128
    gain = vec_ref[:, 0:features]
    bias = vec_ref[:, pad:pad + features]
    b_up = vec_ref[:, 2 * pad:]
    scaled = jnp.concatenate([recv[j] for j in range(n_page)], axis=0)
    res_rows = jnp.concatenate([recv_r[j] for j in range(n_page)], axis=0)
    normed = (scaled * gain + bias).astype(jnp.bfloat16)
    up_s[...] = jnp.dot(normed, w_ref[...], preferred_element_type=jnp.float32).astype(jnp.bfloat16)
    block = red.shape[1]
    n_recv = up_s.shape[0] // block

    def rows_of(k):
        return pl.ds(k * block, block)

    def scatter_copy(k):
        return pltpu.make_async_remote_copy(
            src_ref=up_s.at[rows_of(k)],
            dst_ref=red.at[me],
            send_sem=sems.at[2, k],
            recv_sem=sems.at[3, me],
            device_id=device_on("page", 2 * k),
            device_id_type=MESH_ID,
        )

    def scatter_arrival(s):
        return pltpu.make_async_remote_copy(
            src_ref=up_s.at[rows_of(0)],
            dst_ref=red.at[s],
            send_sem=sems.at[2, 0],
            recv_sem=sems.at[3, s],
            device_id=device_on("page", s),
            device_id_type=MESH_ID,
        )

    def gather_copy(k, mine):
        return pltpu.make_async_remote_copy(
            src_ref=hid_ref.at[rows_of(mine)],
            dst_ref=hid_ref.at[rows_of(mine)],
            send_sem=sems.at[4, k],
            recv_sem=sems.at[5, mine],
            device_id=device_on("page", lax.rem(me + k, n_page)),
            device_id_type=MESH_ID,
        )

    def gather_arrival(k):
        return pltpu.make_async_remote_copy(
            src_ref=hid_ref.at[rows_of(k)],
            dst_ref=hid_ref.at[rows_of(k)],
            send_sem=sems.at[4, 0],
            recv_sem=sems.at[5, k],
            device_id=device_on("page", 2 * k),
            device_id_type=MESH_ID,
        )

    for k in range(n_recv):
        @pl.when(me != 2 * k)
        def _():
            scatter_copy(k).start()

    mine = me // 2

    @pl.when(me % 2 == 0)
    def _():
        red[me] = up_s[pl.ds(pl.multiple_of(mine * block, block), block)]
        for s in range(n_page):
            @pl.when(me != s)
            def _():
                scatter_arrival(s).wait_recv()
        total = slot_sum(red, n_page) + b_up
        hid_ref[pl.ds(pl.multiple_of(mine * block, block), block)] = jnp.maximum(total, 0.0).astype(
            jnp.bfloat16
        )
        for k in range(1, n_page):
            gather_copy(k, mine).start()

    for k in range(n_recv):
        @pl.when(me != 2 * k)
        def _():
            scatter_copy(k).wait_send()

    @pl.when(me % 2 == 0)
    def _():
        for k in range(1, n_page):
            gather_copy(k, mine).wait_send()

    for k in range(n_recv):
        @pl.when(me != 2 * k)
        def _():
            gather_arrival(k).wait_recv()

    projected_t = lax.dot_general(
        w_down_ref[...], hid_ref[...], (((0,), (1,)), ((), ())), preferred_element_type=jnp.float32
    )
    width = pieces.shape[1]
    for j in range(n_blk):
        pieces[j] = projected_t[j * width:(j + 1) * width]
    eye = (
        lax.broadcasted_iota(jnp.int32, (width, width), 0) == lax.broadcasted_iota(jnp.int32, (width, width), 1)
    ).astype(jnp.float32)
    res_t = lax.dot_general(
        eye, res_rows, (((1,), (1,)), ((), ())),
        precision=lax.Precision.HIGHEST, preferred_element_type=jnp.float32,
    )
    columns = col_ref[...]
    output_phase(n_blk, n_page, pieces, res_t, columns[:, 0:1], columns[:, 1:2], out_ref, score_ref,
                 out_buf, blk_buf, page_buf, sems.at[6:12])


CALL_IDS = {}


def next_id(axis):
    cid = len(CALL_IDS)
    CALL_IDS[cid] = axis
    return cid


def vmem_specs(count):
    return [pl.BlockSpec(memory_space=pltpu.VMEM)] * count


def exchange(x, axis):
    n = lax.axis_size(axis)
    return pl.pallas_call(
        lambda *refs: exchange_kernel(axis, n, *refs),
        out_shape=jax.ShapeDtypeStruct(x.shape, x.dtype),
        in_specs=vmem_specs(1),
        out_specs=vmem_specs(1)[0],
        scratch_shapes=[
            pltpu.VMEM(x.shape, x.dtype),
            pltpu.SemaphoreType.DMA((n,)),
            pltpu.SemaphoreType.DMA((n,)),
        ],
        compiler_params=pltpu.CompilerParams(collective_id=next_id(axis), has_side_effects=True),
    )(x)


def sum_gather(x, extra, axis, finish, out_dtype):
    n = lax.axis_size(axis)
    return pl.pallas_call(
        lambda *refs: sum_gather_kernel(axis, n, finish, *refs),
        out_shape=jax.ShapeDtypeStruct(x.shape, out_dtype),
        in_specs=vmem_specs(2),
        out_specs=vmem_specs(1)[0],
        scratch_shapes=[
            pltpu.VMEM(x.shape, x.dtype),
            pltpu.VMEM(x.shape, out_dtype),
            pltpu.SemaphoreType.DMA((4, n)),
        ],
        compiler_params=pltpu.CompilerParams(collective_id=next_id(axis), has_side_effects=True),
    )(x, extra)


def attention_out(queries, kv, tkv, row_code, key_code, t_lo, t_hi, w_out, stream, head_dim):
    n_page = lax.axis_size("page")
    n_blk = lax.axis_size("blk")
    rows, width = stream.shape
    heads = kv.shape[1] // (2 * head_dim)
    lanes = 128 * (-(-width // (128 * n_blk)))
    n_chunk = width // lanes
    assert n_chunk * lanes == width
    part_shape = (n_page, heads * rows, 3 * head_dim)
    return pl.pallas_call(
        lambda *refs: attention_out_kernel(n_page, n_blk, heads, *refs),
        out_shape=(
            jax.ShapeDtypeStruct((n_page, rows, width // n_page), jnp.float32),
            jax.ShapeDtypeStruct((n_page, rows, width // n_page), jnp.float32),
        ),
        in_specs=vmem_specs(9),
        out_specs=tuple(vmem_specs(2)),
        scratch_shapes=[
            pltpu.VMEM(part_shape, jnp.float32),
            pltpu.VMEM(part_shape, jnp.float32),
            pltpu.VMEM((rows, width), jnp.float32),
            pltpu.VMEM((rows, width), jnp.float32),
            pltpu.VMEM((n_blk, rows, lanes), jnp.float32),
            pltpu.VMEM((n_chunk, rows, lanes), jnp.float32),
            pltpu.SemaphoreType.DMA((6, max(n_blk, n_page))),
        ],
        compiler_params=pltpu.CompilerParams(collective_id=next_id("both"), has_side_effects=True),
    )(queries, kv, tkv, row_code, key_code, t_lo, t_hi, w_out, stream)


def mlp(scaled, res_pieces, vectors, w_up, w_down, columns):
    n_page = lax.axis_size("page")
    n_blk = lax.axis_size("blk")
    rows = scaled.shape[0] * scaled.shape[1]
    ff = w_up.shape[1]
    block = 2 * rows // n_page
    width = columns.shape[0]
    return pl.pallas_call(
        lambda *refs: mlp_kernel(n_page, n_blk, *refs),
        out_shape=(
            jax.ShapeDtypeStruct((width, rows), jnp.bfloat16),
            jax.ShapeDtypeStruct((1, rows), jnp.float32),
        ),
        in_specs=vmem_specs(6),
        out_specs=tuple(vmem_specs(2)),
        scratch_shapes=[
            pltpu.VMEM(scaled.shape, jnp.float32),
            pltpu.VMEM(res_pieces.shape, jnp.float32),
            pltpu.VMEM((rows, ff), jnp.bfloat16),
            pltpu.VMEM((n_page, block, ff), jnp.bfloat16),
            pltpu.VMEM((rows, ff), jnp.bfloat16),
            pltpu.VMEM((n_blk, width, rows), jnp.float32),
            pltpu.VMEM((n_blk, width, rows), jnp.float32),
            pltpu.VMEM((n_blk, 1, rows), jnp.float32),
            pltpu.VMEM((n_page, 1, rows), jnp.float32),
            pltpu.SemaphoreType.DMA((14, max(n_page, n_blk))),
        ],
        compiler_params=pltpu.CompilerParams(collective_id=next_id("both"), has_side_effects=True),
    )(scaled, res_pieces, vectors, w_up, w_down, columns)


def output_and_score(x, res, bias, score_w):
    n_blk = lax.axis_size("blk")
    n_page = lax.axis_size("page")
    lanes = x.shape[2]
    return pl.pallas_call(
        lambda *refs: output_kernel(n_blk, n_page, *refs),
        out_shape=(
            jax.ShapeDtypeStruct(x.shape[1:], jnp.bfloat16),
            jax.ShapeDtypeStruct((1, lanes), jnp.float32),
        ),
        in_specs=vmem_specs(4),
        out_specs=tuple(vmem_specs(2)),
        scratch_shapes=[
            pltpu.VMEM(x.shape, jnp.float32),
            pltpu.VMEM((n_blk, 1, lanes), jnp.float32),
            pltpu.VMEM((n_page, 1, lanes), jnp.float32),
            pltpu.SemaphoreType.DMA((6, max(n_blk, n_page))),
        ],
        compiler_params=pltpu.CompilerParams(collective_id=next_id("both"), has_side_effects=True),
    )(x, res, bias, score_w)


def ordered_sum(stack):
    total = stack[0]
    for j in range(1, stack.shape[0]):
        total = total + stack[j]
    return total


def body(
    queries,
    prompt_kv,
    tail_kv,
    page_table,
    prompt_len,
    tail_len,
    sample_prompt,
    stream_in,
    w_out,
    b_out,
    ln_gain,
    ln_bias,
    w_up,
    b_up,
    w_down,
    b_down,
    w_score,
):
    CALL_IDS.clear()
    samples, new_count, heads_dev, head_dim = queries.shape
    slots_dev, page_len = (prompt_kv.shape[0], prompt_kv.shape[1])
    own_count, tail_max = (tail_kv.shape[0], tail_kv.shape[1])
    prompts, pages_max = page_table.shape
    n_page = samples // own_count
    page_pos = lax.axis_index("page")
    blk_pos = lax.axis_index("blk")
    inv_sqrt = 1.0 / math.sqrt(head_dim)
    width = w_out.shape[1]
    rows_own = own_count * new_count

    entries = page_table.reshape(-1)
    slot_ids = page_pos * slots_dev + jnp.arange(slots_dev, dtype=jnp.int32)
    matched = (entries[:, None] == slot_ids[None, :]).astype(jnp.int32)
    owner_index = jnp.sum(matched * jnp.arange(entries.shape[0], dtype=jnp.int32)[:, None], axis=0)
    slot_prompt = owner_index // pages_max
    slot_page = owner_index % pages_max
    prompt_pick = (slot_prompt[:, None] == jnp.arange(prompts, dtype=jnp.int32)[None, :]).astype(
        jnp.int32
    )
    slot_limit = jnp.sum(prompt_pick * prompt_len[None, :], axis=1)
    key_pos = slot_page[:, None] * page_len + jnp.arange(page_len, dtype=jnp.int32)[None, :]
    key_live = (key_pos < slot_limit[:, None]).reshape(-1)
    key_prompt = jnp.repeat(slot_prompt, page_len)
    key_code = jnp.where(key_live, key_prompt, -1).astype(jnp.int32).reshape(1, -1)
    row_code = jnp.repeat(sample_prompt, new_count).astype(jnp.int32).reshape(-1, 1)

    first_row = page_pos * own_count
    own_lengths = lax.dynamic_slice_in_dim(tail_len, first_row, own_count, 0)
    local_row = jnp.arange(rows_own, dtype=jnp.int32)
    t_lo = (local_row // new_count) * tail_max
    t_hi = t_lo + jnp.repeat(own_lengths, new_count) + local_row % new_count

    slice_width = stream_in.shape[2]
    column = blk_pos * slice_width
    own_stream = (
        lax.dynamic_slice_in_dim(stream_in, first_row, own_count, 0)
        .reshape(rows_own, slice_width)
        .astype(jnp.float32)
    )
    own_bias = lax.dynamic_slice_in_dim(b_out, column, slice_width, 0).astype(jnp.float32)
    stream_full = lax.dynamic_update_slice_in_dim(
        jnp.zeros((rows_own, width), jnp.float32), own_stream + own_bias, column, 1
    )
    residual16, scaled16 = attention_out(
        queries.reshape(samples * new_count, heads_dev * head_dim),
        prompt_kv.reshape(slots_dev * page_len, heads_dev * 2 * head_dim),
        tail_kv.reshape(own_count * tail_max, heads_dev * 2 * head_dim),
        row_code,
        key_code,
        t_lo.reshape(-1, 1),
        t_hi.reshape(-1, 1),
        w_out,
        stream_full,
        head_dim,
    )

    feature_count = ln_gain.shape[0]
    piece_width = b_down.shape[0]
    res_pieces = lax.dynamic_slice_in_dim(residual16, blk_pos * piece_width, piece_width, 2)
    pad = -(-feature_count // 128) * 128
    vectors = jnp.concatenate(
        [
            jnp.pad(ln_gain.astype(jnp.float32), (0, pad - feature_count)),
            jnp.pad(ln_bias.astype(jnp.float32), (0, pad - feature_count)),
            b_up.astype(jnp.float32),
        ]
    ).reshape(1, -1)
    columns = jnp.stack([b_down.astype(jnp.float32), w_score.astype(jnp.float32)], axis=1)
    output_t, row_score = mlp(scaled16, res_pieces, vectors, w_up, w_down, columns)
    output = output_t.T
    return (output.reshape(samples, new_count, piece_width), row_score.reshape(samples, new_count))


def solution(mesh):
    placed = (
        P(None, None, "blk", None),
        P("page", None, "blk", None),
        P("page", None, "blk", None),
        P(),
        P(),
        P(),
        P(),
        P(None, None, "blk"),
        P("blk", None),
        P(),
        P("page"),
        P("page"),
        P("page", "blk"),
        P("blk"),
        P("blk", "page"),
        P(("page", "blk")),
        P(("page", "blk")),
    )
    return jax.shard_map(
        body,
        mesh=mesh,
        in_specs=placed,
        out_specs=(P(None, None, ("page", "blk")), P()),
        check_vma=False,
    )
```

```python
import math

import jax
import jax.numpy as jnp
from jax import lax
from jax.experimental import pallas as pl
from jax.experimental.pallas import tpu as pltpu
from jax.sharding import PartitionSpec as P

NEGATIVE = -1e30
AXES = ("page", "blk")
MESH_ID = pl.DeviceIdType.MESH


def device_on(axis, j):
    return tuple(j if name == axis else lax.axis_index(name) for name in AXES)


def greet(sizes):
    barrier = pltpu.get_barrier_semaphore()
    total = 0
    for axis, n in sizes:
        me = lax.axis_index(axis)
        for k in range(1, n):
            peer = lax.rem(me + k, n)
            pl.semaphore_signal(barrier, inc=1, device_id=device_on(axis, peer), device_id_type=MESH_ID)
        total += n - 1
    return total


def enter(sizes):
    pl.semaphore_wait(pltpu.get_barrier_semaphore(), greet(sizes))


def send_round(axis, n, source, buf, send_sem, recv_sem):
    me = lax.axis_index(axis)
    copies = []
    for k in range(1, n):
        peer = lax.rem(me + k, n)
        copy = pltpu.make_async_remote_copy(
            src_ref=source(peer),
            dst_ref=buf.at[me],
            send_sem=send_sem.at[k],
            recv_sem=recv_sem.at[k],
            device_id=device_on(axis, peer),
            device_id_type=MESH_ID,
        )
        copy.start()
        copies.append(copy)
    for copy in copies:
        copy.wait()


def slot_sum(buf, n):
    total = buf[0].astype(jnp.float32)
    for j in range(1, n):
        total = total + buf[j].astype(jnp.float32)
    return total


def exchange_kernel(axis, n, x_ref, o_ref, buf, send_sem, recv_sem):
    me = lax.axis_index(axis)
    buf[me] = x_ref[me]
    enter([(axis, n)])
    send_round(axis, n, lambda peer: x_ref.at[peer], buf, send_sem, recv_sem)
    o_ref[...] = buf[...]


def sum_gather_kernel(axis, n, finish, x_ref, extra_ref, o_ref, buf, gat, sems):
    me = lax.axis_index(axis)
    buf[me] = x_ref[me]
    enter([(axis, n)])
    send_round(axis, n, lambda peer: x_ref.at[peer], buf, sems.at[0], sems.at[1])
    gat[me] = finish(slot_sum(buf, n), extra_ref[...]).astype(gat.dtype)
    send_round(axis, n, lambda peer: gat.at[me], gat, sems.at[2], sems.at[3])
    o_ref[...] = gat[...]


def output_phase(n_blk, n_page, x_ref, res_t, bias, score_w, out_ref, score_ref,
                 buf, blk_buf, page_buf, sems):
    me_blk = lax.axis_index("blk")
    me_page = lax.axis_index("page")
    buf[me_blk] = x_ref[me_blk]
    send_round("blk", n_blk, lambda peer: x_ref.at[peer], buf, sems.at[0], sems.at[1])
    output = (slot_sum(buf, n_blk) + res_t + bias).astype(jnp.bfloat16)
    out_ref[...] = output
    blk_buf[me_blk] = jnp.sum(output.astype(jnp.float32) * score_w, axis=0, keepdims=True)
    send_round("blk", n_blk, lambda peer: blk_buf.at[me_blk], blk_buf, sems.at[2], sems.at[3])
    page_buf[me_page] = slot_sum(blk_buf, n_blk)
    send_round("page", n_page, lambda peer: page_buf.at[me_page], page_buf, sems.at[4], sems.at[5])
    score_ref[...] = slot_sum(page_buf, n_page)


def softmax_rows(scores, visible):
    highest = jnp.max(jnp.where(visible, scores, NEGATIVE), axis=1, keepdims=True)
    weights = jnp.where(visible, jnp.exp(scores - highest), 0.0)
    return highest, jnp.sum(weights, axis=1, keepdims=True), weights.astype(jnp.bfloat16)


def attention_out_kernel(n_page, n_blk, heads, q_ref, kv_ref, tkv_ref, row_code_ref, key_code_ref,
                         t_lo_ref, t_hi_ref, w_ref, stream_ref,
                         res_ref, scaled_ref, part_ref, recv, full, res_s, red, gat, sems):
    me_page = lax.axis_index("page")
    me_blk = lax.axis_index("blk")
    expected = greet([("page", n_page), ("blk", n_blk)])
    hd = kv_ref.shape[1] // (2 * heads)
    own_rows = t_lo_ref.shape[0]
    inv_sqrt = 1.0 / math.sqrt(hd)
    visible = row_code_ref[...] == key_code_ref[...]
    position = lax.broadcasted_iota(jnp.int32, (1, tkv_ref.shape[0]), 1)
    tail_visible = (position >= t_lo_ref[...]) & (position <= t_hi_ref[...])
    own_block = pl.ds(pl.multiple_of(me_page * own_rows, own_rows), own_rows)
    contract = (((1,), (1,)), ((), ()))
    half = lax.broadcasted_iota(jnp.int32, (1, hd), 1) < hd // 2
    tail_parts = []
    for h in range(heads):
        keys = kv_ref[:, 2 * h * hd:(2 * h + 1) * hd]
        values = kv_ref[:, (2 * h + 1) * hd:(2 * h + 2) * hd]
        query = q_ref[:, h * hd:(h + 1) * hd]
        scores = lax.dot_general(query, keys, contract, preferred_element_type=jnp.float32) * inv_sqrt
        high, total, weights = softmax_rows(scores, visible)
        mixed = jnp.dot(weights, values, preferred_element_type=jnp.float32)
        stats = jnp.where(half, jnp.broadcast_to(high, (high.shape[0], hd)), jnp.broadcast_to(total, (high.shape[0], hd)))
        for j in range(n_page):
            rows = slice(j * own_rows, (j + 1) * own_rows)
            part_ref[j, h * own_rows:(h + 1) * own_rows, :] = jnp.concatenate([mixed[rows], stats[rows]], axis=1)
        keys = tkv_ref[:, 2 * h * hd:(2 * h + 1) * hd]
        values = tkv_ref[:, (2 * h + 1) * hd:(2 * h + 2) * hd]
        query = q_ref[own_block, h * hd:(h + 1) * hd]
        scores = lax.dot_general(query, keys, contract, preferred_element_type=jnp.float32) * inv_sqrt
        high, total, weights = softmax_rows(scores, tail_visible)
        mixed = jnp.dot(weights, values, preferred_element_type=jnp.float32)
        tail_parts.append((mixed, high, total))
    tail_mixed = jnp.concatenate([t[0] for t in tail_parts], axis=0)
    tail_high = jnp.concatenate([t[1] for t in tail_parts], axis=0)
    tail_total = jnp.concatenate([t[2] for t in tail_parts], axis=0)
    pl.semaphore_wait(pltpu.get_barrier_semaphore(), expected)
    recv[me_page] = part_ref[me_page]
    send_round("page", n_page, lambda peer: part_ref.at[peer], recv, sems.at[0], sems.at[1])
    highest = tail_high
    for j in range(n_page):
        highest = jnp.maximum(highest, recv[j][:, hd:hd + 1])
    scale = jnp.exp(tail_high - highest)
    weight_sum = tail_total * scale
    weighted = tail_mixed * scale
    for j in range(n_page):
        part = recv[j]
        scale = jnp.exp(part[:, hd:hd + 1] - highest)
        weight_sum = weight_sum + part[:, hd + hd // 2:hd + hd // 2 + 1] * scale
        weighted = weighted + part[:, :hd] * scale
    attention = (weighted / weight_sum).astype(jnp.bfloat16)
    rows = attention.shape[0] // heads
    if heads > 1:
        attention = jnp.concatenate([attention[h * rows:(h + 1) * rows] for h in range(heads)], axis=1)
    full[...] = jnp.dot(attention, w_ref[...], preferred_element_type=jnp.float32) + stream_ref[...]
    lanes = red.shape[2]
    n_chunk = gat.shape[0]

    def own(ref):
        return ref[:, pl.ds(pl.multiple_of(me_blk * lanes, lanes), lanes)]

    def scatter_copy(t):
        return pltpu.make_async_remote_copy(
            src_ref=full.at[:, pl.ds(t * lanes, lanes)],
            dst_ref=red.at[me_blk],
            send_sem=sems.at[2, t],
            recv_sem=sems.at[3, me_blk],
            device_id=device_on("blk", t),
            device_id_type=MESH_ID,
        )

    def scatter_arrival(s):
        return pltpu.make_async_remote_copy(
            src_ref=full.at[:, pl.ds(0, lanes)],
            dst_ref=red.at[s],
            send_sem=sems.at[2, 0],
            recv_sem=sems.at[3, s],
            device_id=device_on("blk", s),
            device_id_type=MESH_ID,
        )

    def gather_copy(k):
        return pltpu.make_async_remote_copy(
            src_ref=gat.at[me_blk],
            dst_ref=gat.at[me_blk],
            send_sem=sems.at[4, k],
            recv_sem=sems.at[5, me_blk],
            device_id=device_on("blk", lax.rem(me_blk + k, n_blk)),
            device_id_type=MESH_ID,
        )

    def gather_arrival(s):
        return pltpu.make_async_remote_copy(
            src_ref=gat.at[s],
            dst_ref=gat.at[s],
            send_sem=sems.at[4, 0],
            recv_sem=sems.at[5, s],
            device_id=device_on("blk", s),
            device_id_type=MESH_ID,
        )

    for t in range(n_chunk):
        @pl.when(me_blk != t)
        def _():
            scatter_copy(t).start()

    @pl.when(me_blk < n_chunk)
    def _():
        red[me_blk] = own(full)
        for s in range(n_blk):
            @pl.when(me_blk != s)
            def _():
                scatter_arrival(s).wait_recv()
        total = slot_sum(red, n_blk)
        gat[me_blk] = total.astype(jnp.bfloat16).astype(jnp.float32)
        for k in range(1, n_blk):
            gather_copy(k).start()

    for t in range(n_chunk):
        @pl.when(me_blk != t)
        def _():
            scatter_copy(t).wait_send()

    @pl.when(me_blk < n_chunk)
    def _():
        for k in range(1, n_blk):
            gather_copy(k).wait_send()

    for s in range(n_chunk):
        @pl.when(me_blk != s)
        def _():
            gather_arrival(s).wait_recv()

    for t in range(n_chunk):
        res_s[:, t * lanes:(t + 1) * lanes] = gat[t]
    residual = res_s[...]
    row_mean = jnp.mean(residual, axis=-1, keepdims=True)
    centred = residual - row_mean
    inverse_std = lax.rsqrt(jnp.mean(centred * centred, axis=-1, keepdims=True) + 1e-05)
    scaled = centred * inverse_std
    group = scaled_ref.shape[2]
    for q in range(n_page):
        scaled_ref[q] = scaled[:, q * group:(q + 1) * group]
        res_ref[q] = residual[:, q * group:(q + 1) * group]

def mlp_kernel(n_page, n_blk, x_ref, vec_ref, w_ref, w_down_ref, col_ref, out_ref, score_ref,
               recv, up_s, red, hid_ref, pieces, out_buf, blk_buf, page_buf, sems):
    me = lax.axis_index("page")
    recv[me] = x_ref[me]
    enter([("page", n_page), ("blk", n_blk)])
    send_round("page", n_page, lambda peer: x_ref.at[peer], recv, sems.at[0], sems.at[1])
    width = col_ref.shape[0]
    lanes_in = x_ref.shape[2]
    features = lanes_in - width
    pad = -(-features // 128) * 128
    gain = vec_ref[:, 0:features]
    bias = vec_ref[:, pad:pad + features]
    b_up = vec_ref[:, 2 * pad:]
    arrived = jnp.concatenate([recv[j] for j in range(n_page)], axis=0)
    scaled = arrived[:, :features]
    normed = (scaled * gain + bias).astype(jnp.bfloat16)
    up_s[...] = jnp.dot(normed, w_ref[...], preferred_element_type=jnp.float32).astype(jnp.bfloat16)
    block = red.shape[1]
    n_recv = up_s.shape[0] // block

    def rows_of(k):
        return pl.ds(k * block, block)

    def scatter_copy(k):
        return pltpu.make_async_remote_copy(
            src_ref=up_s.at[rows_of(k)],
            dst_ref=red.at[me],
            send_sem=sems.at[2, k],
            recv_sem=sems.at[3, me],
            device_id=device_on("page", 2 * k),
            device_id_type=MESH_ID,
        )

    def scatter_arrival(s):
        return pltpu.make_async_remote_copy(
            src_ref=up_s.at[rows_of(0)],
            dst_ref=red.at[s],
            send_sem=sems.at[2, 0],
            recv_sem=sems.at[3, s],
            device_id=device_on("page", s),
            device_id_type=MESH_ID,
        )

    def gather_copy(k, mine):
        return pltpu.make_async_remote_copy(
            src_ref=hid_ref.at[rows_of(mine)],
            dst_ref=hid_ref.at[rows_of(mine)],
            send_sem=sems.at[4, k],
            recv_sem=sems.at[5, mine],
            device_id=device_on("page", lax.rem(me + k, n_page)),
            device_id_type=MESH_ID,
        )

    def gather_arrival(k):
        return pltpu.make_async_remote_copy(
            src_ref=hid_ref.at[rows_of(k)],
            dst_ref=hid_ref.at[rows_of(k)],
            send_sem=sems.at[4, 0],
            recv_sem=sems.at[5, k],
            device_id=device_on("page", 2 * k),
            device_id_type=MESH_ID,
        )

    for k in range(n_recv):
        @pl.when(me != 2 * k)
        def _():
            scatter_copy(k).start()

    mine = me // 2

    @pl.when(me % 2 == 0)
    def _():
        red[me] = up_s[pl.ds(pl.multiple_of(mine * block, block), block)]
        for s in range(n_page):
            @pl.when(me != s)
            def _():
                scatter_arrival(s).wait_recv()
        total = slot_sum(red, n_page) + b_up
        hid_ref[pl.ds(pl.multiple_of(mine * block, block), block)] = jnp.maximum(total, 0.0).astype(
            jnp.bfloat16
        )
        for k in range(1, n_page):
            gather_copy(k, mine).start()

    for k in range(n_recv):
        @pl.when(me != 2 * k)
        def _():
            scatter_copy(k).wait_send()

    @pl.when(me % 2 == 0)
    def _():
        for k in range(1, n_page):
            gather_copy(k, mine).wait_send()

    for k in range(n_recv):
        @pl.when(me != 2 * k)
        def _():
            gather_arrival(k).wait_recv()

    projected_t = lax.dot_general(
        w_down_ref[...], hid_ref[...], (((0,), (1,)), ((), ())), preferred_element_type=jnp.float32
    )
    for j in range(n_blk):
        pieces[j] = projected_t[j * width:(j + 1) * width]
    pick = (
        lax.broadcasted_iota(jnp.int32, (width, lanes_in), 1)
        == lax.broadcasted_iota(jnp.int32, (width, lanes_in), 0) + features
    ).astype(jnp.float32)
    res_t = lax.dot_general(
        pick, arrived, (((1,), (1,)), ((), ())),
        precision=lax.Precision.HIGHEST, preferred_element_type=jnp.float32,
    )
    columns = col_ref[...]
    output_phase(n_blk, n_page, pieces, res_t, columns[:, 0:1], columns[:, 1:2], out_ref, score_ref,
                 out_buf, blk_buf, page_buf, sems.at[6:12])


CALL_IDS = {}


def next_id(axis):
    cid = len(CALL_IDS)
    CALL_IDS[cid] = axis
    return cid


def vmem_specs(count):
    return [pl.BlockSpec(memory_space=pltpu.VMEM)] * count


def exchange(x, axis):
    n = lax.axis_size(axis)
    return pl.pallas_call(
        lambda *refs: exchange_kernel(axis, n, *refs),
        out_shape=jax.ShapeDtypeStruct(x.shape, x.dtype),
        in_specs=vmem_specs(1),
        out_specs=vmem_specs(1)[0],
        scratch_shapes=[
            pltpu.VMEM(x.shape, x.dtype),
            pltpu.SemaphoreType.DMA((n,)),
            pltpu.SemaphoreType.DMA((n,)),
        ],
        compiler_params=pltpu.CompilerParams(collective_id=next_id(axis), has_side_effects=True),
    )(x)


def sum_gather(x, extra, axis, finish, out_dtype):
    n = lax.axis_size(axis)
    return pl.pallas_call(
        lambda *refs: sum_gather_kernel(axis, n, finish, *refs),
        out_shape=jax.ShapeDtypeStruct(x.shape, out_dtype),
        in_specs=vmem_specs(2),
        out_specs=vmem_specs(1)[0],
        scratch_shapes=[
            pltpu.VMEM(x.shape, x.dtype),
            pltpu.VMEM(x.shape, out_dtype),
            pltpu.SemaphoreType.DMA((4, n)),
        ],
        compiler_params=pltpu.CompilerParams(collective_id=next_id(axis), has_side_effects=True),
    )(x, extra)


def attention_out(queries, kv, tkv, row_code, key_code, t_lo, t_hi, w_out, stream, head_dim):
    n_page = lax.axis_size("page")
    n_blk = lax.axis_size("blk")
    rows, width = stream.shape
    heads = kv.shape[1] // (2 * head_dim)
    lanes = 128 * (-(-width // (128 * n_blk)))
    n_chunk = width // lanes
    assert n_chunk * lanes == width
    part_shape = (n_page, heads * rows, 2 * head_dim)
    return pl.pallas_call(
        lambda *refs: attention_out_kernel(n_page, n_blk, heads, *refs),
        out_shape=(
            jax.ShapeDtypeStruct((n_page, rows, width // n_page), jnp.float32),
            jax.ShapeDtypeStruct((n_page, rows, width // n_page), jnp.float32),
        ),
        in_specs=vmem_specs(9),
        out_specs=tuple(vmem_specs(2)),
        scratch_shapes=[
            pltpu.VMEM(part_shape, jnp.float32),
            pltpu.VMEM(part_shape, jnp.float32),
            pltpu.VMEM((rows, width), jnp.float32),
            pltpu.VMEM((rows, width), jnp.float32),
            pltpu.VMEM((n_blk, rows, lanes), jnp.float32),
            pltpu.VMEM((n_chunk, rows, lanes), jnp.float32),
            pltpu.SemaphoreType.DMA((6, max(n_blk, n_page))),
        ],
        compiler_params=pltpu.CompilerParams(collective_id=next_id("both"), has_side_effects=True),
    )(queries, kv, tkv, row_code, key_code, t_lo, t_hi, w_out, stream)


def mlp(outgoing, vectors, w_up, w_down, columns):
    n_page = lax.axis_size("page")
    n_blk = lax.axis_size("blk")
    rows = outgoing.shape[0] * outgoing.shape[1]
    ff = w_up.shape[1]
    block = 2 * rows // n_page
    width = columns.shape[0]
    return pl.pallas_call(
        lambda *refs: mlp_kernel(n_page, n_blk, *refs),
        out_shape=(
            jax.ShapeDtypeStruct((width, rows), jnp.bfloat16),
            jax.ShapeDtypeStruct((1, rows), jnp.float32),
        ),
        in_specs=vmem_specs(5),
        out_specs=tuple(vmem_specs(2)),
        scratch_shapes=[
            pltpu.VMEM(outgoing.shape, jnp.float32),
            pltpu.VMEM((rows, ff), jnp.bfloat16),
            pltpu.VMEM((n_page, block, ff), jnp.bfloat16),
            pltpu.VMEM((rows, ff), jnp.bfloat16),
            pltpu.VMEM((n_blk, width, rows), jnp.float32),
            pltpu.VMEM((n_blk, width, rows), jnp.float32),
            pltpu.VMEM((n_blk, 1, rows), jnp.float32),
            pltpu.VMEM((n_page, 1, rows), jnp.float32),
            pltpu.SemaphoreType.DMA((12, max(n_page, n_blk))),
        ],
        compiler_params=pltpu.CompilerParams(collective_id=next_id("both"), has_side_effects=True),
    )(outgoing, vectors, w_up, w_down, columns)


def output_and_score(x, res, bias, score_w):
    n_blk = lax.axis_size("blk")
    n_page = lax.axis_size("page")
    lanes = x.shape[2]
    return pl.pallas_call(
        lambda *refs: output_kernel(n_blk, n_page, *refs),
        out_shape=(
            jax.ShapeDtypeStruct(x.shape[1:], jnp.bfloat16),
            jax.ShapeDtypeStruct((1, lanes), jnp.float32),
        ),
        in_specs=vmem_specs(4),
        out_specs=tuple(vmem_specs(2)),
        scratch_shapes=[
            pltpu.VMEM(x.shape, jnp.float32),
            pltpu.VMEM((n_blk, 1, lanes), jnp.float32),
            pltpu.VMEM((n_page, 1, lanes), jnp.float32),
            pltpu.SemaphoreType.DMA((6, max(n_blk, n_page))),
        ],
        compiler_params=pltpu.CompilerParams(collective_id=next_id("both"), has_side_effects=True),
    )(x, res, bias, score_w)


def ordered_sum(stack):
    total = stack[0]
    for j in range(1, stack.shape[0]):
        total = total + stack[j]
    return total


def body(
    queries,
    prompt_kv,
    tail_kv,
    page_table,
    prompt_len,
    tail_len,
    sample_prompt,
    stream_in,
    w_out,
    b_out,
    ln_gain,
    ln_bias,
    w_up,
    b_up,
    w_down,
    b_down,
    w_score,
):
    CALL_IDS.clear()
    samples, new_count, heads_dev, head_dim = queries.shape
    slots_dev, page_len = (prompt_kv.shape[0], prompt_kv.shape[1])
    own_count, tail_max = (tail_kv.shape[0], tail_kv.shape[1])
    prompts, pages_max = page_table.shape
    n_page = samples // own_count
    page_pos = lax.axis_index("page")
    blk_pos = lax.axis_index("blk")
    inv_sqrt = 1.0 / math.sqrt(head_dim)
    width = w_out.shape[1]
    rows_own = own_count * new_count

    entries = page_table.reshape(-1)
    slot_ids = page_pos * slots_dev + jnp.arange(slots_dev, dtype=jnp.int32)
    matched = (entries[:, None] == slot_ids[None, :]).astype(jnp.int32)
    owner_index = jnp.sum(matched * jnp.arange(entries.shape[0], dtype=jnp.int32)[:, None], axis=0)
    slot_prompt = owner_index // pages_max
    slot_page = owner_index % pages_max
    prompt_pick = (slot_prompt[:, None] == jnp.arange(prompts, dtype=jnp.int32)[None, :]).astype(
        jnp.int32
    )
    slot_limit = jnp.sum(prompt_pick * prompt_len[None, :], axis=1)
    key_pos = slot_page[:, None] * page_len + jnp.arange(page_len, dtype=jnp.int32)[None, :]
    key_live = (key_pos < slot_limit[:, None]).reshape(-1)
    key_prompt = jnp.repeat(slot_prompt, page_len)
    key_code = jnp.where(key_live, key_prompt, -1).astype(jnp.int32).reshape(1, -1)
    row_code = jnp.repeat(sample_prompt, new_count).astype(jnp.int32).reshape(-1, 1)

    first_row = page_pos * own_count
    own_lengths = lax.dynamic_slice_in_dim(tail_len, first_row, own_count, 0)
    local_row = jnp.arange(rows_own, dtype=jnp.int32)
    t_lo = (local_row // new_count) * tail_max
    t_hi = t_lo + jnp.repeat(own_lengths, new_count) + local_row % new_count

    slice_width = stream_in.shape[2]
    column = blk_pos * slice_width
    own_stream = (
        lax.dynamic_slice_in_dim(stream_in, first_row, own_count, 0)
        .reshape(rows_own, slice_width)
        .astype(jnp.float32)
    )
    own_bias = lax.dynamic_slice_in_dim(b_out, column, slice_width, 0).astype(jnp.float32)
    stream_full = lax.dynamic_update_slice_in_dim(
        jnp.zeros((rows_own, width), jnp.float32), own_stream + own_bias, column, 1
    )
    residual16, scaled16 = attention_out(
        queries.reshape(samples * new_count, heads_dev * head_dim),
        prompt_kv.reshape(slots_dev * page_len, heads_dev * 2 * head_dim),
        tail_kv.reshape(own_count * tail_max, heads_dev * 2 * head_dim),
        row_code,
        key_code,
        t_lo.reshape(-1, 1),
        t_hi.reshape(-1, 1),
        w_out,
        stream_full,
        head_dim,
    )

    feature_count = ln_gain.shape[0]
    piece_width = b_down.shape[0]
    res_pieces = lax.dynamic_slice_in_dim(residual16, blk_pos * piece_width, piece_width, 2)
    pad = -(-feature_count // 128) * 128
    vectors = jnp.concatenate(
        [
            jnp.pad(ln_gain.astype(jnp.float32), (0, pad - feature_count)),
            jnp.pad(ln_bias.astype(jnp.float32), (0, pad - feature_count)),
            b_up.astype(jnp.float32),
        ]
    ).reshape(1, -1)
    columns = jnp.stack([b_down.astype(jnp.float32), w_score.astype(jnp.float32)], axis=1)
    outgoing = jnp.concatenate([scaled16, res_pieces], axis=-1)
    output_t, row_score = mlp(outgoing, vectors, w_up, w_down, columns)
    output = output_t.T
    return (output.reshape(samples, new_count, piece_width), row_score.reshape(samples, new_count))


def solution(mesh):
    placed = (
        P(None, None, "blk", None),
        P("page", None, "blk", None),
        P("page", None, "blk", None),
        P(),
        P(),
        P(),
        P(),
        P(None, None, "blk"),
        P("blk", None),
        P(),
        P("page"),
        P("page"),
        P("page", "blk"),
        P("blk"),
        P("blk", "page"),
        P(("page", "blk")),
        P(("page", "blk")),
    )
    return jax.shard_map(
        body,
        mesh=mesh,
        in_specs=placed,
        out_specs=(P(None, None, ("page", "blk")), P()),
        check_vma=False,
    )
```

```python
import math

import jax
import jax.numpy as jnp
from jax import lax
from jax.experimental import pallas as pl
from jax.experimental.pallas import tpu as pltpu
from jax.sharding import PartitionSpec as P

NEGATIVE = -1e30
AXES = ("page", "blk")
MESH_ID = pl.DeviceIdType.MESH


def device_on(axis, j):
    return tuple(j if name == axis else lax.axis_index(name) for name in AXES)


def greet(sizes):
    barrier = pltpu.get_barrier_semaphore()
    total = 0
    for axis, n in sizes:
        me = lax.axis_index(axis)
        for k in range(1, n):
            peer = lax.rem(me + k, n)
            pl.semaphore_signal(barrier, inc=1, device_id=device_on(axis, peer), device_id_type=MESH_ID)
        total += n - 1
    return total


def enter(sizes):
    pl.semaphore_wait(pltpu.get_barrier_semaphore(), greet(sizes))


def send_round(axis, n, source, buf, send_sem, recv_sem):
    me = lax.axis_index(axis)
    copies = []
    for k in range(1, n):
        peer = lax.rem(me + k, n)
        copy = pltpu.make_async_remote_copy(
            src_ref=source(peer),
            dst_ref=buf.at[me],
            send_sem=send_sem.at[k],
            recv_sem=recv_sem.at[k],
            device_id=device_on(axis, peer),
            device_id_type=MESH_ID,
        )
        copy.start()
        copies.append(copy)
    for copy in copies:
        copy.wait()


def slot_sum(buf, n):
    total = buf[0].astype(jnp.float32)
    for j in range(1, n):
        total = total + buf[j].astype(jnp.float32)
    return total


def exchange_kernel(axis, n, x_ref, o_ref, buf, send_sem, recv_sem):
    me = lax.axis_index(axis)
    buf[me] = x_ref[me]
    enter([(axis, n)])
    send_round(axis, n, lambda peer: x_ref.at[peer], buf, send_sem, recv_sem)
    o_ref[...] = buf[...]


def sum_gather_kernel(axis, n, finish, x_ref, extra_ref, o_ref, buf, gat, sems):
    me = lax.axis_index(axis)
    buf[me] = x_ref[me]
    enter([(axis, n)])
    send_round(axis, n, lambda peer: x_ref.at[peer], buf, sems.at[0], sems.at[1])
    gat[me] = finish(slot_sum(buf, n), extra_ref[...]).astype(gat.dtype)
    send_round(axis, n, lambda peer: gat.at[me], gat, sems.at[2], sems.at[3])
    o_ref[...] = gat[...]


def output_phase(n_blk, n_page, x_ref, res_t, bias, score_w, out_ref, score_ref,
                 buf, blk_buf, page_buf, sems):
    me_blk = lax.axis_index("blk")
    me_page = lax.axis_index("page")
    buf[me_blk] = x_ref[me_blk]
    send_round("blk", n_blk, lambda peer: x_ref.at[peer], buf, sems.at[0], sems.at[1])
    output = (slot_sum(buf, n_blk) + res_t + bias).astype(jnp.bfloat16)
    lanes = output.shape[1]
    spread = lanes // 2
    source = lax.broadcasted_iota(jnp.int32, (lanes, lanes), 0)
    target = lax.broadcasted_iota(jnp.int32, (lanes, lanes), 1)
    order = (source == (target % spread) * 2 + target // spread).astype(jnp.float32)

    def reorder(value):
        return jnp.dot(value, order, precision=lax.Precision.HIGHEST, preferred_element_type=jnp.float32)

    out_ref[...] = reorder(output.astype(jnp.float32)).astype(jnp.bfloat16)
    blk_buf[me_blk] = jnp.sum(output.astype(jnp.float32) * score_w, axis=0, keepdims=True)
    send_round("blk", n_blk, lambda peer: blk_buf.at[me_blk], blk_buf, sems.at[2], sems.at[3])
    page_buf[me_page] = slot_sum(blk_buf, n_blk)
    send_round("page", n_page, lambda peer: page_buf.at[me_page], page_buf, sems.at[4], sems.at[5])
    score = reorder(slot_sum(page_buf, n_page))
    score_ref[0:1, :] = score[:, :spread]
    score_ref[1:2, :] = score[:, spread:]


def softmax_rows(scores, visible):
    highest = jnp.max(jnp.where(visible, scores, NEGATIVE), axis=1, keepdims=True)
    weights = jnp.where(visible, jnp.exp(scores - highest), 0.0)
    return highest, jnp.sum(weights, axis=1, keepdims=True), weights.astype(jnp.bfloat16)


def attention_out_kernel(n_page, n_blk, heads, q_ref, kv_ref, tkv_ref, row_code_ref, key_code_ref,
                         t_lo_ref, t_hi_ref, w_ref, stream_ref,
                         res_ref, scaled_ref, part_ref, recv, full, res_s, red, gat, sems):
    me_page = lax.axis_index("page")
    me_blk = lax.axis_index("blk")
    expected = greet([("page", n_page), ("blk", n_blk)])
    hd = kv_ref.shape[1] // (2 * heads)
    own_rows = t_lo_ref.shape[0]
    inv_sqrt = 1.0 / math.sqrt(hd)
    visible = row_code_ref[...] == key_code_ref[...]
    position = lax.broadcasted_iota(jnp.int32, (1, tkv_ref.shape[0]), 1)
    tail_visible = (position >= t_lo_ref[...]) & (position <= t_hi_ref[...])
    own_block = pl.ds(pl.multiple_of(me_page * own_rows, own_rows), own_rows)
    contract = (((1,), (1,)), ((), ()))
    half = lax.broadcasted_iota(jnp.int32, (1, hd), 1) < hd // 2
    tail_parts = []
    for h in range(heads):
        keys = kv_ref[:, 2 * h * hd:(2 * h + 1) * hd]
        values = kv_ref[:, (2 * h + 1) * hd:(2 * h + 2) * hd]
        query = q_ref[:, h * hd:(h + 1) * hd]
        scores = lax.dot_general(query, keys, contract, preferred_element_type=jnp.float32) * inv_sqrt
        high, total, weights = softmax_rows(scores, visible)
        mixed = jnp.dot(weights, values, preferred_element_type=jnp.float32)
        stats = jnp.where(half, jnp.broadcast_to(high, (high.shape[0], hd)), jnp.broadcast_to(total, (high.shape[0], hd)))
        for j in range(n_page):
            rows = slice(j * own_rows, (j + 1) * own_rows)
            part_ref[j, h * own_rows:(h + 1) * own_rows, :] = jnp.concatenate([mixed[rows], stats[rows]], axis=1)
        keys = tkv_ref[:, 2 * h * hd:(2 * h + 1) * hd]
        values = tkv_ref[:, (2 * h + 1) * hd:(2 * h + 2) * hd]
        query = q_ref[own_block, h * hd:(h + 1) * hd]
        scores = lax.dot_general(query, keys, contract, preferred_element_type=jnp.float32) * inv_sqrt
        high, total, weights = softmax_rows(scores, tail_visible)
        mixed = jnp.dot(weights, values, preferred_element_type=jnp.float32)
        tail_parts.append((mixed, high, total))
    tail_mixed = jnp.concatenate([t[0] for t in tail_parts], axis=0)
    tail_high = jnp.concatenate([t[1] for t in tail_parts], axis=0)
    tail_total = jnp.concatenate([t[2] for t in tail_parts], axis=0)
    pl.semaphore_wait(pltpu.get_barrier_semaphore(), expected)
    recv[me_page] = part_ref[me_page]
    send_round("page", n_page, lambda peer: part_ref.at[peer], recv, sems.at[0], sems.at[1])
    highest = tail_high
    for j in range(n_page):
        highest = jnp.maximum(highest, recv[j][:, hd:hd + 1])
    scale = jnp.exp(tail_high - highest)
    weight_sum = tail_total * scale
    weighted = tail_mixed * scale
    for j in range(n_page):
        part = recv[j]
        scale = jnp.exp(part[:, hd:hd + 1] - highest)
        weight_sum = weight_sum + part[:, hd + hd // 2:hd + hd // 2 + 1] * scale
        weighted = weighted + part[:, :hd] * scale
    attention = (weighted / weight_sum).astype(jnp.bfloat16)
    rows = attention.shape[0] // heads
    if heads > 1:
        attention = jnp.concatenate([attention[h * rows:(h + 1) * rows] for h in range(heads)], axis=1)
    full[...] = jnp.dot(attention, w_ref[...], preferred_element_type=jnp.float32) + stream_ref[...]
    lanes = red.shape[2]
    n_chunk = gat.shape[0]

    def own(ref):
        return ref[:, pl.ds(pl.multiple_of(me_blk * lanes, lanes), lanes)]

    def scatter_copy(t):
        return pltpu.make_async_remote_copy(
            src_ref=full.at[:, pl.ds(t * lanes, lanes)],
            dst_ref=red.at[me_blk],
            send_sem=sems.at[2, t],
            recv_sem=sems.at[3, me_blk],
            device_id=device_on("blk", t),
            device_id_type=MESH_ID,
        )

    def scatter_arrival(s):
        return pltpu.make_async_remote_copy(
            src_ref=full.at[:, pl.ds(0, lanes)],
            dst_ref=red.at[s],
            send_sem=sems.at[2, 0],
            recv_sem=sems.at[3, s],
            device_id=device_on("blk", s),
            device_id_type=MESH_ID,
        )

    def gather_copy(k):
        return pltpu.make_async_remote_copy(
            src_ref=gat.at[me_blk],
            dst_ref=gat.at[me_blk],
            send_sem=sems.at[4, k],
            recv_sem=sems.at[5, me_blk],
            device_id=device_on("blk", lax.rem(me_blk + k, n_blk)),
            device_id_type=MESH_ID,
        )

    def gather_arrival(s):
        return pltpu.make_async_remote_copy(
            src_ref=gat.at[s],
            dst_ref=gat.at[s],
            send_sem=sems.at[4, 0],
            recv_sem=sems.at[5, s],
            device_id=device_on("blk", s),
            device_id_type=MESH_ID,
        )

    for t in range(n_chunk):
        @pl.when(me_blk != t)
        def _():
            scatter_copy(t).start()

    @pl.when(me_blk < n_chunk)
    def _():
        red[me_blk] = own(full)
        for s in range(n_blk):
            @pl.when(me_blk != s)
            def _():
                scatter_arrival(s).wait_recv()
        total = slot_sum(red, n_blk)
        gat[me_blk] = total.astype(jnp.bfloat16).astype(jnp.float32)
        for k in range(1, n_blk):
            gather_copy(k).start()

    for t in range(n_chunk):
        @pl.when(me_blk != t)
        def _():
            scatter_copy(t).wait_send()

    @pl.when(me_blk < n_chunk)
    def _():
        for k in range(1, n_blk):
            gather_copy(k).wait_send()

    for s in range(n_chunk):
        @pl.when(me_blk != s)
        def _():
            gather_arrival(s).wait_recv()

    for t in range(n_chunk):
        res_s[:, t * lanes:(t + 1) * lanes] = gat[t]
    residual = res_s[...]
    row_mean = jnp.mean(residual, axis=-1, keepdims=True)
    centred = residual - row_mean
    inverse_std = lax.rsqrt(jnp.mean(centred * centred, axis=-1, keepdims=True) + 1e-05)
    scaled = centred * inverse_std
    group = scaled_ref.shape[2]
    for q in range(n_page):
        scaled_ref[q] = scaled[:, q * group:(q + 1) * group]
        res_ref[q] = residual[:, q * group:(q + 1) * group]

def mlp_kernel(n_page, n_blk, x_ref, vec_ref, w_ref, w_down_ref, col_ref, out_ref, score_ref,
               recv, up_s, red, hid_ref, pieces, out_buf, blk_buf, page_buf, sems):
    me = lax.axis_index("page")
    recv[me] = x_ref[me]
    enter([("page", n_page), ("blk", n_blk)])
    send_round("page", n_page, lambda peer: x_ref.at[peer], recv, sems.at[0], sems.at[1])
    width = col_ref.shape[0]
    lanes_in = x_ref.shape[2]
    features = lanes_in - width
    pad = -(-features // 128) * 128
    gain = vec_ref[:, 0:features]
    bias = vec_ref[:, pad:pad + features]
    b_up = vec_ref[:, 2 * pad:]
    arrived = jnp.concatenate([recv[j] for j in range(n_page)], axis=0)
    scaled = arrived[:, :features]
    normed = (scaled * gain + bias).astype(jnp.bfloat16)
    up_s[...] = jnp.dot(normed, w_ref[...], preferred_element_type=jnp.float32).astype(jnp.bfloat16)
    block = red.shape[1]
    n_recv = up_s.shape[0] // block

    def rows_of(k):
        return pl.ds(k * block, block)

    def scatter_copy(k):
        return pltpu.make_async_remote_copy(
            src_ref=up_s.at[rows_of(k)],
            dst_ref=red.at[me],
            send_sem=sems.at[2, k],
            recv_sem=sems.at[3, me],
            device_id=device_on("page", 2 * k),
            device_id_type=MESH_ID,
        )

    def scatter_arrival(s):
        return pltpu.make_async_remote_copy(
            src_ref=up_s.at[rows_of(0)],
            dst_ref=red.at[s],
            send_sem=sems.at[2, 0],
            recv_sem=sems.at[3, s],
            device_id=device_on("page", s),
            device_id_type=MESH_ID,
        )

    def gather_copy(k, mine):
        return pltpu.make_async_remote_copy(
            src_ref=hid_ref.at[rows_of(mine)],
            dst_ref=hid_ref.at[rows_of(mine)],
            send_sem=sems.at[4, k],
            recv_sem=sems.at[5, mine],
            device_id=device_on("page", lax.rem(me + k, n_page)),
            device_id_type=MESH_ID,
        )

    def gather_arrival(k):
        return pltpu.make_async_remote_copy(
            src_ref=hid_ref.at[rows_of(k)],
            dst_ref=hid_ref.at[rows_of(k)],
            send_sem=sems.at[4, 0],
            recv_sem=sems.at[5, k],
            device_id=device_on("page", 2 * k),
            device_id_type=MESH_ID,
        )

    for k in range(n_recv):
        @pl.when(me != 2 * k)
        def _():
            scatter_copy(k).start()

    mine = me // 2

    @pl.when(me % 2 == 0)
    def _():
        red[me] = up_s[pl.ds(pl.multiple_of(mine * block, block), block)]
        for s in range(n_page):
            @pl.when(me != s)
            def _():
                scatter_arrival(s).wait_recv()
        total = slot_sum(red, n_page) + b_up
        hid_ref[pl.ds(pl.multiple_of(mine * block, block), block)] = jnp.maximum(total, 0.0).astype(
            jnp.bfloat16
        )
        for k in range(1, n_page):
            gather_copy(k, mine).start()

    for k in range(n_recv):
        @pl.when(me != 2 * k)
        def _():
            scatter_copy(k).wait_send()

    @pl.when(me % 2 == 0)
    def _():
        for k in range(1, n_page):
            gather_copy(k, mine).wait_send()

    for k in range(n_recv):
        @pl.when(me != 2 * k)
        def _():
            gather_arrival(k).wait_recv()

    projected_t = lax.dot_general(
        w_down_ref[...], hid_ref[...], (((0,), (1,)), ((), ())), preferred_element_type=jnp.float32
    )
    for j in range(n_blk):
        pieces[j] = projected_t[j * width:(j + 1) * width]
    pick = (
        lax.broadcasted_iota(jnp.int32, (width, lanes_in), 1)
        == lax.broadcasted_iota(jnp.int32, (width, lanes_in), 0) + features
    ).astype(jnp.float32)
    res_t = lax.dot_general(
        pick, arrived, (((1,), (1,)), ((), ())),
        precision=lax.Precision.HIGHEST, preferred_element_type=jnp.float32,
    )
    columns = col_ref[...]
    output_phase(n_blk, n_page, pieces, res_t, columns[:, 0:1], columns[:, 1:2], out_ref, score_ref,
                 out_buf, blk_buf, page_buf, sems.at[6:12])


CALL_IDS = {}


def next_id(axis):
    cid = len(CALL_IDS)
    CALL_IDS[cid] = axis
    return cid


def vmem_specs(count):
    return [pl.BlockSpec(memory_space=pltpu.VMEM)] * count


def exchange(x, axis):
    n = lax.axis_size(axis)
    return pl.pallas_call(
        lambda *refs: exchange_kernel(axis, n, *refs),
        out_shape=jax.ShapeDtypeStruct(x.shape, x.dtype),
        in_specs=vmem_specs(1),
        out_specs=vmem_specs(1)[0],
        scratch_shapes=[
            pltpu.VMEM(x.shape, x.dtype),
            pltpu.SemaphoreType.DMA((n,)),
            pltpu.SemaphoreType.DMA((n,)),
        ],
        compiler_params=pltpu.CompilerParams(collective_id=next_id(axis), has_side_effects=True),
    )(x)


def sum_gather(x, extra, axis, finish, out_dtype):
    n = lax.axis_size(axis)
    return pl.pallas_call(
        lambda *refs: sum_gather_kernel(axis, n, finish, *refs),
        out_shape=jax.ShapeDtypeStruct(x.shape, out_dtype),
        in_specs=vmem_specs(2),
        out_specs=vmem_specs(1)[0],
        scratch_shapes=[
            pltpu.VMEM(x.shape, x.dtype),
            pltpu.VMEM(x.shape, out_dtype),
            pltpu.SemaphoreType.DMA((4, n)),
        ],
        compiler_params=pltpu.CompilerParams(collective_id=next_id(axis), has_side_effects=True),
    )(x, extra)


def attention_out(queries, kv, tkv, row_code, key_code, t_lo, t_hi, w_out, stream, head_dim):
    n_page = lax.axis_size("page")
    n_blk = lax.axis_size("blk")
    rows, width = stream.shape
    heads = kv.shape[1] // (2 * head_dim)
    lanes = 128 * (-(-width // (128 * n_blk)))
    n_chunk = width // lanes
    assert n_chunk * lanes == width
    part_shape = (n_page, heads * rows, 2 * head_dim)
    return pl.pallas_call(
        lambda *refs: attention_out_kernel(n_page, n_blk, heads, *refs),
        out_shape=(
            jax.ShapeDtypeStruct((n_page, rows, width // n_page), jnp.float32),
            jax.ShapeDtypeStruct((n_page, rows, width // n_page), jnp.float32),
        ),
        in_specs=vmem_specs(9),
        out_specs=tuple(vmem_specs(2)),
        scratch_shapes=[
            pltpu.VMEM(part_shape, jnp.float32),
            pltpu.VMEM(part_shape, jnp.float32),
            pltpu.VMEM((rows, width), jnp.float32),
            pltpu.VMEM((rows, width), jnp.float32),
            pltpu.VMEM((n_blk, rows, lanes), jnp.float32),
            pltpu.VMEM((n_chunk, rows, lanes), jnp.float32),
            pltpu.SemaphoreType.DMA((6, max(n_blk, n_page))),
        ],
        compiler_params=pltpu.CompilerParams(collective_id=next_id("both"), has_side_effects=True),
    )(queries, kv, tkv, row_code, key_code, t_lo, t_hi, w_out, stream)


def mlp(outgoing, vectors, w_up, w_down, columns):
    n_page = lax.axis_size("page")
    n_blk = lax.axis_size("blk")
    rows = outgoing.shape[0] * outgoing.shape[1]
    ff = w_up.shape[1]
    block = 2 * rows // n_page
    width = columns.shape[0]
    return pl.pallas_call(
        lambda *refs: mlp_kernel(n_page, n_blk, *refs),
        out_shape=(
            jax.ShapeDtypeStruct((width, rows), jnp.bfloat16),
            jax.ShapeDtypeStruct((2, rows // 2), jnp.float32),
        ),
        in_specs=vmem_specs(5),
        out_specs=tuple(vmem_specs(2)),
        scratch_shapes=[
            pltpu.VMEM(outgoing.shape, jnp.float32),
            pltpu.VMEM((rows, ff), jnp.bfloat16),
            pltpu.VMEM((n_page, block, ff), jnp.bfloat16),
            pltpu.VMEM((rows, ff), jnp.bfloat16),
            pltpu.VMEM((n_blk, width, rows), jnp.float32),
            pltpu.VMEM((n_blk, width, rows), jnp.float32),
            pltpu.VMEM((n_blk, 1, rows), jnp.float32),
            pltpu.VMEM((n_page, 1, rows), jnp.float32),
            pltpu.SemaphoreType.DMA((12, max(n_page, n_blk))),
        ],
        compiler_params=pltpu.CompilerParams(collective_id=next_id("both"), has_side_effects=True),
    )(outgoing, vectors, w_up, w_down, columns)


def output_and_score(x, res, bias, score_w):
    n_blk = lax.axis_size("blk")
    n_page = lax.axis_size("page")
    lanes = x.shape[2]
    return pl.pallas_call(
        lambda *refs: output_kernel(n_blk, n_page, *refs),
        out_shape=(
            jax.ShapeDtypeStruct(x.shape[1:], jnp.bfloat16),
            jax.ShapeDtypeStruct((1, lanes), jnp.float32),
        ),
        in_specs=vmem_specs(4),
        out_specs=tuple(vmem_specs(2)),
        scratch_shapes=[
            pltpu.VMEM(x.shape, jnp.float32),
            pltpu.VMEM((n_blk, 1, lanes), jnp.float32),
            pltpu.VMEM((n_page, 1, lanes), jnp.float32),
            pltpu.SemaphoreType.DMA((6, max(n_blk, n_page))),
        ],
        compiler_params=pltpu.CompilerParams(collective_id=next_id("both"), has_side_effects=True),
    )(x, res, bias, score_w)


def ordered_sum(stack):
    total = stack[0]
    for j in range(1, stack.shape[0]):
        total = total + stack[j]
    return total


def body(
    queries,
    prompt_kv,
    tail_kv,
    page_table,
    prompt_len,
    tail_len,
    sample_prompt,
    stream_in,
    w_out,
    b_out,
    ln_gain,
    ln_bias,
    w_up,
    b_up,
    w_down,
    b_down,
    w_score,
):
    CALL_IDS.clear()
    samples, new_count, heads_dev, head_dim = queries.shape
    slots_dev, page_len = (prompt_kv.shape[0], prompt_kv.shape[1])
    own_count, tail_max = (tail_kv.shape[0], tail_kv.shape[1])
    prompts, pages_max = page_table.shape
    n_page = samples // own_count
    page_pos = lax.axis_index("page")
    blk_pos = lax.axis_index("blk")
    inv_sqrt = 1.0 / math.sqrt(head_dim)
    width = w_out.shape[1]
    rows_own = own_count * new_count

    entries = page_table.reshape(-1)
    slot_ids = page_pos * slots_dev + jnp.arange(slots_dev, dtype=jnp.int32)
    matched = (entries[:, None] == slot_ids[None, :]).astype(jnp.int32)
    owner_index = jnp.sum(matched * jnp.arange(entries.shape[0], dtype=jnp.int32)[:, None], axis=0)
    slot_prompt = owner_index // pages_max
    slot_page = owner_index % pages_max
    prompt_pick = (slot_prompt[:, None] == jnp.arange(prompts, dtype=jnp.int32)[None, :]).astype(
        jnp.int32
    )
    slot_limit = jnp.sum(prompt_pick * prompt_len[None, :], axis=1)
    key_pos = slot_page[:, None] * page_len + jnp.arange(page_len, dtype=jnp.int32)[None, :]
    key_live = (key_pos < slot_limit[:, None]).reshape(-1)
    key_prompt = jnp.repeat(slot_prompt, page_len)
    key_code = jnp.where(key_live, key_prompt, -1).astype(jnp.int32).reshape(1, -1)
    row_code = jnp.repeat(sample_prompt, new_count).astype(jnp.int32).reshape(-1, 1)

    first_row = page_pos * own_count
    own_lengths = lax.dynamic_slice_in_dim(tail_len, first_row, own_count, 0)
    local_row = jnp.arange(rows_own, dtype=jnp.int32)
    t_lo = (local_row // new_count) * tail_max
    t_hi = t_lo + jnp.repeat(own_lengths, new_count) + local_row % new_count

    slice_width = stream_in.shape[2]
    column = blk_pos * slice_width
    own_stream = (
        lax.dynamic_slice_in_dim(stream_in, first_row, own_count, 0)
        .reshape(rows_own, slice_width)
        .astype(jnp.float32)
    )
    own_bias = lax.dynamic_slice_in_dim(b_out, column, slice_width, 0).astype(jnp.float32)
    stream_full = lax.dynamic_update_slice_in_dim(
        jnp.zeros((rows_own, width), jnp.float32), own_stream + own_bias, column, 1
    )
    residual16, scaled16 = attention_out(
        queries.reshape(samples * new_count, heads_dev * head_dim),
        prompt_kv.reshape(slots_dev * page_len, heads_dev * 2 * head_dim),
        tail_kv.reshape(own_count * tail_max, heads_dev * 2 * head_dim),
        row_code,
        key_code,
        t_lo.reshape(-1, 1),
        t_hi.reshape(-1, 1),
        w_out,
        stream_full,
        head_dim,
    )

    feature_count = ln_gain.shape[0]
    piece_width = b_down.shape[0]
    res_pieces = lax.dynamic_slice_in_dim(residual16, blk_pos * piece_width, piece_width, 2)
    pad = -(-feature_count // 128) * 128
    vectors = jnp.concatenate(
        [
            jnp.pad(ln_gain.astype(jnp.float32), (0, pad - feature_count)),
            jnp.pad(ln_bias.astype(jnp.float32), (0, pad - feature_count)),
            b_up.astype(jnp.float32),
        ]
    ).reshape(1, -1)
    columns = jnp.stack([b_down.astype(jnp.float32), w_score.astype(jnp.float32)], axis=1)
    outgoing = jnp.concatenate([scaled16, res_pieces], axis=-1)
    output_t, row_score = mlp(outgoing, vectors, w_up, w_down, columns)
    output = output_t.reshape(piece_width, new_count, samples).transpose(2, 1, 0)
    return (output, row_score.T)


def solution(mesh):
    placed = (
        P(None, None, "blk", None),
        P("page", None, "blk", None),
        P("page", None, "blk", None),
        P(),
        P(),
        P(),
        P(),
        P(None, None, "blk"),
        P("blk", None),
        P(),
        P("page"),
        P("page"),
        P("page", "blk"),
        P("blk"),
        P("blk", "page"),
        P(("page", "blk")),
        P(("page", "blk")),
    )
    return jax.shard_map(
        body,
        mesh=mesh,
        in_specs=placed,
        out_specs=(P(None, None, ("page", "blk")), P()),
        check_vma=False,
    )
```

```python
import math

import jax
import jax.numpy as jnp
from jax import lax
from jax.experimental import pallas as pl
from jax.experimental.pallas import tpu as pltpu
from jax.sharding import PartitionSpec as P

NEGATIVE = -1e30
AXES = ("page", "blk")
MESH_ID = pl.DeviceIdType.MESH


def device_on(axis, j):
    return tuple(j if name == axis else lax.axis_index(name) for name in AXES)


def greet(sizes):
    barrier = pltpu.get_barrier_semaphore()
    total = 0
    for axis, n in sizes:
        me = lax.axis_index(axis)
        for k in range(1, n):
            peer = lax.rem(me + k, n)
            pl.semaphore_signal(barrier, inc=1, device_id=device_on(axis, peer), device_id_type=MESH_ID)
        total += n - 1
    return total


def enter(sizes):
    pl.semaphore_wait(pltpu.get_barrier_semaphore(), greet(sizes))


def send_round(axis, n, source, buf, send_sem, recv_sem):
    me = lax.axis_index(axis)
    copies = []
    for k in range(1, n):
        peer = lax.rem(me + k, n)
        copy = pltpu.make_async_remote_copy(
            src_ref=source(peer),
            dst_ref=buf.at[me],
            send_sem=send_sem.at[k],
            recv_sem=recv_sem.at[k],
            device_id=device_on(axis, peer),
            device_id_type=MESH_ID,
        )
        copy.start()
        copies.append(copy)
    for copy in copies:
        copy.wait()


def slot_sum(buf, n):
    total = buf[0].astype(jnp.float32)
    for j in range(1, n):
        total = total + buf[j].astype(jnp.float32)
    return total


def exchange_kernel(axis, n, x_ref, o_ref, buf, send_sem, recv_sem):
    me = lax.axis_index(axis)
    buf[me] = x_ref[me]
    enter([(axis, n)])
    send_round(axis, n, lambda peer: x_ref.at[peer], buf, send_sem, recv_sem)
    o_ref[...] = buf[...]


def sum_gather_kernel(axis, n, finish, x_ref, extra_ref, o_ref, buf, gat, sems):
    me = lax.axis_index(axis)
    buf[me] = x_ref[me]
    enter([(axis, n)])
    send_round(axis, n, lambda peer: x_ref.at[peer], buf, sems.at[0], sems.at[1])
    gat[me] = finish(slot_sum(buf, n), extra_ref[...]).astype(gat.dtype)
    send_round(axis, n, lambda peer: gat.at[me], gat, sems.at[2], sems.at[3])
    o_ref[...] = gat[...]


def output_phase(n_blk, n_page, x_ref, res_t, bias, score_w, out_ref, score_ref,
                 buf, blk_buf, page_buf, sems):
    me_blk = lax.axis_index("blk")
    me_page = lax.axis_index("page")
    buf[me_blk] = x_ref[me_blk]
    send_round("blk", n_blk, lambda peer: x_ref.at[peer], buf, sems.at[0], sems.at[1])
    output = (slot_sum(buf, n_blk) + res_t + bias).astype(jnp.bfloat16)
    out_ref[...] = output
    blk_buf[me_blk] = jnp.sum(output.astype(jnp.float32) * score_w, axis=0, keepdims=True)
    send_round("blk", n_blk, lambda peer: blk_buf.at[me_blk], blk_buf, sems.at[2], sems.at[3])
    page_buf[me_page] = slot_sum(blk_buf, n_blk)
    send_round("page", n_page, lambda peer: page_buf.at[me_page], page_buf, sems.at[4], sems.at[5])
    score_ref[...] = slot_sum(page_buf, n_page)


def softmax_rows(scores, visible):
    highest = jnp.max(jnp.where(visible, scores, NEGATIVE), axis=1, keepdims=True)
    weights = jnp.where(visible, jnp.exp(scores - highest), 0.0)
    return highest, jnp.sum(weights, axis=1, keepdims=True), weights.astype(jnp.bfloat16)


def attention_out_kernel(n_page, n_blk, heads, q_ref, kv_ref, tkv_ref, row_code_ref, key_code_ref,
                         t_lo_ref, t_hi_ref, w_ref, stream_ref,
                         res_ref, scaled_ref, part_ref, recv, full, res_s, red, gat, sems):
    me_page = lax.axis_index("page")
    me_blk = lax.axis_index("blk")
    expected = greet([("page", n_page), ("blk", n_blk)])
    hd = kv_ref.shape[1] // (2 * heads)
    own_rows = t_lo_ref.shape[0]
    inv_sqrt = 1.0 / math.sqrt(hd)
    visible = row_code_ref[...] == key_code_ref[...]
    position = lax.broadcasted_iota(jnp.int32, (1, tkv_ref.shape[0]), 1)
    tail_visible = (position >= t_lo_ref[...]) & (position <= t_hi_ref[...])
    own_block = pl.ds(pl.multiple_of(me_page * own_rows, own_rows), own_rows)
    contract = (((1,), (1,)), ((), ()))
    half = lax.broadcasted_iota(jnp.int32, (1, hd), 1) < hd // 2
    tail_parts = []
    for h in range(heads):
        keys = kv_ref[:, 2 * h * hd:(2 * h + 1) * hd]
        values = kv_ref[:, (2 * h + 1) * hd:(2 * h + 2) * hd]
        query = q_ref[:, h * hd:(h + 1) * hd]
        scores = lax.dot_general(query, keys, contract, preferred_element_type=jnp.float32) * inv_sqrt
        high, total, weights = softmax_rows(scores, visible)
        mixed = jnp.dot(weights, values, preferred_element_type=jnp.float32)
        stats = jnp.where(half, jnp.broadcast_to(high, (high.shape[0], hd)), jnp.broadcast_to(total, (high.shape[0], hd)))
        for j in range(n_page):
            rows = slice(j * own_rows, (j + 1) * own_rows)
            part_ref[j, h * own_rows:(h + 1) * own_rows, :] = jnp.concatenate([mixed[rows], stats[rows]], axis=1)
        keys = tkv_ref[:, 2 * h * hd:(2 * h + 1) * hd]
        values = tkv_ref[:, (2 * h + 1) * hd:(2 * h + 2) * hd]
        query = q_ref[own_block, h * hd:(h + 1) * hd]
        scores = lax.dot_general(query, keys, contract, preferred_element_type=jnp.float32) * inv_sqrt
        high, total, weights = softmax_rows(scores, tail_visible)
        mixed = jnp.dot(weights, values, preferred_element_type=jnp.float32)
        tail_parts.append((mixed, high, total))
    tail_mixed = jnp.concatenate([t[0] for t in tail_parts], axis=0)
    tail_high = jnp.concatenate([t[1] for t in tail_parts], axis=0)
    tail_total = jnp.concatenate([t[2] for t in tail_parts], axis=0)
    pl.semaphore_wait(pltpu.get_barrier_semaphore(), expected)
    recv[me_page] = part_ref[me_page]
    send_round("page", n_page, lambda peer: part_ref.at[peer], recv, sems.at[0], sems.at[1])
    highest = tail_high
    for j in range(n_page):
        highest = jnp.maximum(highest, recv[j][:, hd:hd + 1])
    scale = jnp.exp(tail_high - highest)
    weight_sum = tail_total * scale
    weighted = tail_mixed * scale
    for j in range(n_page):
        part = recv[j]
        scale = jnp.exp(part[:, hd:hd + 1] - highest)
        weight_sum = weight_sum + part[:, hd + hd // 2:hd + hd // 2 + 1] * scale
        weighted = weighted + part[:, :hd] * scale
    attention = (weighted / weight_sum).astype(jnp.bfloat16)
    rows = attention.shape[0] // heads
    if heads > 1:
        attention = jnp.concatenate([attention[h * rows:(h + 1) * rows] for h in range(heads)], axis=1)
    full[...] = jnp.dot(attention, w_ref[...], preferred_element_type=jnp.float32) + stream_ref[...]
    lanes = red.shape[2]
    n_chunk = gat.shape[0]

    def own(ref):
        return ref[:, pl.ds(pl.multiple_of(me_blk * lanes, lanes), lanes)]

    def scatter_copy(t):
        return pltpu.make_async_remote_copy(
            src_ref=full.at[:, pl.ds(t * lanes, lanes)],
            dst_ref=red.at[me_blk],
            send_sem=sems.at[2, t],
            recv_sem=sems.at[3, me_blk],
            device_id=device_on("blk", t),
            device_id_type=MESH_ID,
        )

    def scatter_arrival(s):
        return pltpu.make_async_remote_copy(
            src_ref=full.at[:, pl.ds(0, lanes)],
            dst_ref=red.at[s],
            send_sem=sems.at[2, 0],
            recv_sem=sems.at[3, s],
            device_id=device_on("blk", s),
            device_id_type=MESH_ID,
        )

    def gather_copy(k):
        return pltpu.make_async_remote_copy(
            src_ref=gat.at[me_blk],
            dst_ref=gat.at[me_blk],
            send_sem=sems.at[4, k],
            recv_sem=sems.at[5, me_blk],
            device_id=device_on("blk", lax.rem(me_blk + k, n_blk)),
            device_id_type=MESH_ID,
        )

    def gather_arrival(s):
        return pltpu.make_async_remote_copy(
            src_ref=gat.at[s],
            dst_ref=gat.at[s],
            send_sem=sems.at[4, 0],
            recv_sem=sems.at[5, s],
            device_id=device_on("blk", s),
            device_id_type=MESH_ID,
        )

    for t in range(n_chunk):
        @pl.when(me_blk != t)
        def _():
            scatter_copy(t).start()

    @pl.when(me_blk < n_chunk)
    def _():
        red[me_blk] = own(full)
        for s in range(n_blk):
            @pl.when(me_blk != s)
            def _():
                scatter_arrival(s).wait_recv()
        total = slot_sum(red, n_blk)
        gat[me_blk] = total.astype(jnp.bfloat16).astype(jnp.float32)
        for k in range(1, n_blk):
            gather_copy(k).start()

    for t in range(n_chunk):
        @pl.when(me_blk != t)
        def _():
            scatter_copy(t).wait_send()

    @pl.when(me_blk < n_chunk)
    def _():
        for k in range(1, n_blk):
            gather_copy(k).wait_send()

    for s in range(n_chunk):
        @pl.when(me_blk != s)
        def _():
            gather_arrival(s).wait_recv()

    for t in range(n_chunk):
        res_s[:, t * lanes:(t + 1) * lanes] = gat[t]
    residual = res_s[...]
    row_mean = jnp.mean(residual, axis=-1, keepdims=True)
    centred = residual - row_mean
    inverse_std = lax.rsqrt(jnp.mean(centred * centred, axis=-1, keepdims=True) + 1e-05)
    scaled = centred * inverse_std
    group = scaled_ref.shape[2]
    for q in range(n_page):
        scaled_ref[q] = scaled[:, q * group:(q + 1) * group]
        res_ref[q] = residual[:, q * group:(q + 1) * group]

def mlp_kernel(n_page, n_blk, x_ref, vec_ref, w_ref, w_down_ref, col_ref, out_ref, score_ref,
               recv, up_s, red, hid_ref, pieces, out_buf, blk_buf, page_buf, sems):
    me = lax.axis_index("page")
    recv[me] = x_ref[me]
    enter([("page", n_page), ("blk", n_blk)])
    send_round("page", n_page, lambda peer: x_ref.at[peer], recv, sems.at[0], sems.at[1])
    width = col_ref.shape[0]
    lanes_in = x_ref.shape[2]
    features = lanes_in - width
    pad = -(-features // 128) * 128
    gain = vec_ref[:, 0:features]
    bias = vec_ref[:, pad:pad + features]
    b_up = vec_ref[:, 2 * pad:]
    arrived = jnp.concatenate([recv[j] for j in range(n_page)], axis=0)
    scaled = arrived[:, :features]
    normed = (scaled * gain + bias).astype(jnp.bfloat16)
    up_s[...] = jnp.dot(normed, w_ref[...], preferred_element_type=jnp.float32).astype(jnp.bfloat16)
    block = red.shape[1]
    n_recv = up_s.shape[0] // block

    def rows_of(k):
        return pl.ds(k * block, block)

    def scatter_copy(k):
        return pltpu.make_async_remote_copy(
            src_ref=up_s.at[rows_of(k)],
            dst_ref=red.at[me],
            send_sem=sems.at[2, k],
            recv_sem=sems.at[3, me],
            device_id=device_on("page", 2 * k),
            device_id_type=MESH_ID,
        )

    def scatter_arrival(s):
        return pltpu.make_async_remote_copy(
            src_ref=up_s.at[rows_of(0)],
            dst_ref=red.at[s],
            send_sem=sems.at[2, 0],
            recv_sem=sems.at[3, s],
            device_id=device_on("page", s),
            device_id_type=MESH_ID,
        )

    def gather_copy(k, mine):
        return pltpu.make_async_remote_copy(
            src_ref=hid_ref.at[rows_of(mine)],
            dst_ref=hid_ref.at[rows_of(mine)],
            send_sem=sems.at[4, k],
            recv_sem=sems.at[5, mine],
            device_id=device_on("page", lax.rem(me + k, n_page)),
            device_id_type=MESH_ID,
        )

    def gather_arrival(k):
        return pltpu.make_async_remote_copy(
            src_ref=hid_ref.at[rows_of(k)],
            dst_ref=hid_ref.at[rows_of(k)],
            send_sem=sems.at[4, 0],
            recv_sem=sems.at[5, k],
            device_id=device_on("page", 2 * k),
            device_id_type=MESH_ID,
        )

    for k in range(n_recv):
        @pl.when(me != 2 * k)
        def _():
            scatter_copy(k).start()

    mine = me // 2

    @pl.when(me % 2 == 0)
    def _():
        red[me] = up_s[pl.ds(pl.multiple_of(mine * block, block), block)]
        for s in range(n_page):
            @pl.when(me != s)
            def _():
                scatter_arrival(s).wait_recv()
        total = slot_sum(red, n_page) + b_up
        hid_ref[pl.ds(pl.multiple_of(mine * block, block), block)] = jnp.maximum(total, 0.0).astype(
            jnp.bfloat16
        )
        for k in range(1, n_page):
            gather_copy(k, mine).start()

    for k in range(n_recv):
        @pl.when(me != 2 * k)
        def _():
            scatter_copy(k).wait_send()

    @pl.when(me % 2 == 0)
    def _():
        for k in range(1, n_page):
            gather_copy(k, mine).wait_send()

    for k in range(n_recv):
        @pl.when(me != 2 * k)
        def _():
            gather_arrival(k).wait_recv()

    projected_t = lax.dot_general(
        w_down_ref[...], hid_ref[...], (((1,), (1,)), ((), ())), preferred_element_type=jnp.float32
    )
    for j in range(n_blk):
        pieces[j] = projected_t[j * width:(j + 1) * width]
    pick = (
        lax.broadcasted_iota(jnp.int32, (width, lanes_in), 1)
        == lax.broadcasted_iota(jnp.int32, (width, lanes_in), 0) + features
    ).astype(jnp.float32)
    res_t = lax.dot_general(
        pick, arrived, (((1,), (1,)), ((), ())),
        precision=lax.Precision.HIGHEST, preferred_element_type=jnp.float32,
    )
    columns = col_ref[...]
    output_phase(n_blk, n_page, pieces, res_t, columns[:, 0:1], columns[:, 1:2], out_ref, score_ref,
                 out_buf, blk_buf, page_buf, sems.at[6:12])


CALL_IDS = {}


def next_id(axis):
    cid = len(CALL_IDS)
    CALL_IDS[cid] = axis
    return cid


def vmem_specs(count):
    return [pl.BlockSpec(memory_space=pltpu.VMEM)] * count


def exchange(x, axis):
    n = lax.axis_size(axis)
    return pl.pallas_call(
        lambda *refs: exchange_kernel(axis, n, *refs),
        out_shape=jax.ShapeDtypeStruct(x.shape, x.dtype),
        in_specs=vmem_specs(1),
        out_specs=vmem_specs(1)[0],
        scratch_shapes=[
            pltpu.VMEM(x.shape, x.dtype),
            pltpu.SemaphoreType.DMA((n,)),
            pltpu.SemaphoreType.DMA((n,)),
        ],
        compiler_params=pltpu.CompilerParams(collective_id=next_id(axis), has_side_effects=True),
    )(x)


def sum_gather(x, extra, axis, finish, out_dtype):
    n = lax.axis_size(axis)
    return pl.pallas_call(
        lambda *refs: sum_gather_kernel(axis, n, finish, *refs),
        out_shape=jax.ShapeDtypeStruct(x.shape, out_dtype),
        in_specs=vmem_specs(2),
        out_specs=vmem_specs(1)[0],
        scratch_shapes=[
            pltpu.VMEM(x.shape, x.dtype),
            pltpu.VMEM(x.shape, out_dtype),
            pltpu.SemaphoreType.DMA((4, n)),
        ],
        compiler_params=pltpu.CompilerParams(collective_id=next_id(axis), has_side_effects=True),
    )(x, extra)


def attention_out(queries, kv, tkv, row_code, key_code, t_lo, t_hi, w_out, stream, head_dim):
    n_page = lax.axis_size("page")
    n_blk = lax.axis_size("blk")
    rows, width = stream.shape
    heads = kv.shape[1] // (2 * head_dim)
    lanes = 128 * (-(-width // (128 * n_blk)))
    n_chunk = width // lanes
    assert n_chunk * lanes == width
    part_shape = (n_page, heads * rows, 2 * head_dim)
    return pl.pallas_call(
        lambda *refs: attention_out_kernel(n_page, n_blk, heads, *refs),
        out_shape=(
            jax.ShapeDtypeStruct((n_page, rows, width // n_page), jnp.float32),
            jax.ShapeDtypeStruct((n_page, rows, width // n_page), jnp.float32),
        ),
        in_specs=vmem_specs(9),
        out_specs=tuple(vmem_specs(2)),
        scratch_shapes=[
            pltpu.VMEM(part_shape, jnp.float32),
            pltpu.VMEM(part_shape, jnp.float32),
            pltpu.VMEM((rows, width), jnp.float32),
            pltpu.VMEM((rows, width), jnp.float32),
            pltpu.VMEM((n_blk, rows, lanes), jnp.float32),
            pltpu.VMEM((n_chunk, rows, lanes), jnp.float32),
            pltpu.SemaphoreType.DMA((6, max(n_blk, n_page))),
        ],
        compiler_params=pltpu.CompilerParams(collective_id=next_id("both"), has_side_effects=True),
    )(queries, kv, tkv, row_code, key_code, t_lo, t_hi, w_out, stream)


def mlp(outgoing, vectors, w_up, w_down, columns):
    n_page = lax.axis_size("page")
    n_blk = lax.axis_size("blk")
    rows = outgoing.shape[0] * outgoing.shape[1]
    ff = w_up.shape[1]
    block = 2 * rows // n_page
    width = columns.shape[0]
    return pl.pallas_call(
        lambda *refs: mlp_kernel(n_page, n_blk, *refs),
        out_shape=(
            jax.ShapeDtypeStruct((width, rows), jnp.bfloat16),
            jax.ShapeDtypeStruct((1, rows), jnp.float32),
        ),
        in_specs=vmem_specs(5),
        out_specs=tuple(vmem_specs(2)),
        scratch_shapes=[
            pltpu.VMEM(outgoing.shape, jnp.float32),
            pltpu.VMEM((rows, ff), jnp.bfloat16),
            pltpu.VMEM((n_page, block, ff), jnp.bfloat16),
            pltpu.VMEM((rows, ff), jnp.bfloat16),
            pltpu.VMEM((n_blk, width, rows), jnp.float32),
            pltpu.VMEM((n_blk, width, rows), jnp.float32),
            pltpu.VMEM((n_blk, 1, rows), jnp.float32),
            pltpu.VMEM((n_page, 1, rows), jnp.float32),
            pltpu.SemaphoreType.DMA((12, max(n_page, n_blk))),
        ],
        compiler_params=pltpu.CompilerParams(collective_id=next_id("both"), has_side_effects=True),
    )(outgoing, vectors, w_up, w_down, columns)


def output_and_score(x, res, bias, score_w):
    n_blk = lax.axis_size("blk")
    n_page = lax.axis_size("page")
    lanes = x.shape[2]
    return pl.pallas_call(
        lambda *refs: output_kernel(n_blk, n_page, *refs),
        out_shape=(
            jax.ShapeDtypeStruct(x.shape[1:], jnp.bfloat16),
            jax.ShapeDtypeStruct((1, lanes), jnp.float32),
        ),
        in_specs=vmem_specs(4),
        out_specs=tuple(vmem_specs(2)),
        scratch_shapes=[
            pltpu.VMEM(x.shape, jnp.float32),
            pltpu.VMEM((n_blk, 1, lanes), jnp.float32),
            pltpu.VMEM((n_page, 1, lanes), jnp.float32),
            pltpu.SemaphoreType.DMA((6, max(n_blk, n_page))),
        ],
        compiler_params=pltpu.CompilerParams(collective_id=next_id("both"), has_side_effects=True),
    )(x, res, bias, score_w)


def ordered_sum(stack):
    total = stack[0]
    for j in range(1, stack.shape[0]):
        total = total + stack[j]
    return total


def body(
    queries,
    prompt_kv,
    tail_kv,
    page_table,
    prompt_len,
    tail_len,
    sample_prompt,
    stream_in,
    w_out,
    b_out,
    ln_gain,
    ln_bias,
    w_up,
    b_up,
    w_down,
    b_down,
    w_score,
):
    CALL_IDS.clear()
    samples, new_count, heads_dev, head_dim = queries.shape
    slots_dev, page_len = (prompt_kv.shape[0], prompt_kv.shape[1])
    own_count, tail_max = (tail_kv.shape[0], tail_kv.shape[1])
    prompts, pages_max = page_table.shape
    n_page = samples // own_count
    page_pos = lax.axis_index("page")
    blk_pos = lax.axis_index("blk")
    inv_sqrt = 1.0 / math.sqrt(head_dim)
    width = w_out.shape[1]
    rows_own = own_count * new_count

    entries = page_table.reshape(-1)
    slot_ids = page_pos * slots_dev + jnp.arange(slots_dev, dtype=jnp.int32)
    matched = (entries[:, None] == slot_ids[None, :]).astype(jnp.int32)
    owner_index = jnp.sum(matched * jnp.arange(entries.shape[0], dtype=jnp.int32)[:, None], axis=0)
    slot_prompt = owner_index // pages_max
    slot_page = owner_index % pages_max
    prompt_pick = (slot_prompt[:, None] == jnp.arange(prompts, dtype=jnp.int32)[None, :]).astype(
        jnp.int32
    )
    slot_limit = jnp.sum(prompt_pick * prompt_len[None, :], axis=1)
    key_pos = slot_page[:, None] * page_len + jnp.arange(page_len, dtype=jnp.int32)[None, :]
    key_live = (key_pos < slot_limit[:, None]).reshape(-1)
    key_prompt = jnp.repeat(slot_prompt, page_len)
    key_code = jnp.where(key_live, key_prompt, -1).astype(jnp.int32).reshape(1, -1)
    row_code = jnp.repeat(sample_prompt, new_count).astype(jnp.int32).reshape(-1, 1)

    first_row = page_pos * own_count
    own_lengths = lax.dynamic_slice_in_dim(tail_len, first_row, own_count, 0)
    local_row = jnp.arange(rows_own, dtype=jnp.int32)
    t_lo = (local_row // new_count) * tail_max
    t_hi = t_lo + jnp.repeat(own_lengths, new_count) + local_row % new_count

    slice_width = stream_in.shape[2]
    column = blk_pos * slice_width
    own_stream = (
        lax.dynamic_slice_in_dim(stream_in, first_row, own_count, 0)
        .reshape(rows_own, slice_width)
        .astype(jnp.float32)
    )
    own_bias = lax.dynamic_slice_in_dim(b_out, column, slice_width, 0).astype(jnp.float32)
    stream_full = lax.dynamic_update_slice_in_dim(
        jnp.zeros((rows_own, width), jnp.float32), own_stream + own_bias, column, 1
    )
    residual16, scaled16 = attention_out(
        queries.reshape(samples * new_count, heads_dev * head_dim),
        prompt_kv.reshape(slots_dev * page_len, heads_dev * 2 * head_dim),
        tail_kv.reshape(own_count * tail_max, heads_dev * 2 * head_dim),
        row_code,
        key_code,
        t_lo.reshape(-1, 1),
        t_hi.reshape(-1, 1),
        w_out,
        stream_full,
        head_dim,
    )

    feature_count = ln_gain.shape[0]
    piece_width = b_down.shape[0]
    res_pieces = lax.dynamic_slice_in_dim(residual16, blk_pos * piece_width, piece_width, 2)
    pad = -(-feature_count // 128) * 128
    vectors = jnp.concatenate(
        [
            jnp.pad(ln_gain.astype(jnp.float32), (0, pad - feature_count)),
            jnp.pad(ln_bias.astype(jnp.float32), (0, pad - feature_count)),
            b_up.astype(jnp.float32),
        ]
    ).reshape(1, -1)
    columns = jnp.stack([b_down.astype(jnp.float32), w_score.astype(jnp.float32)], axis=1)
    outgoing = jnp.concatenate([scaled16, res_pieces], axis=-1)
    output_t, row_score = mlp(outgoing, vectors, w_up, w_down.T, columns)
    output = output_t.T
    return (output.reshape(samples, new_count, piece_width), row_score.reshape(samples, new_count))


def solution(mesh):
    placed = (
        P(None, None, "blk", None),
        P("page", None, "blk", None),
        P("page", None, "blk", None),
        P(),
        P(),
        P(),
        P(),
        P(None, None, "blk"),
        P("blk", None),
        P(),
        P("page"),
        P("page"),
        P("page", "blk"),
        P("blk"),
        P("blk", "page"),
        P(("page", "blk")),
        P(("page", "blk")),
    )
    return jax.shard_map(
        body,
        mesh=mesh,
        in_specs=placed,
        out_specs=(P(None, None, ("page", "blk")), P()),
        check_vma=False,
    )
```

```python
import math

import jax
import jax.numpy as jnp
from jax import lax
from jax.experimental import pallas as pl
from jax.experimental.pallas import tpu as pltpu
from jax.sharding import PartitionSpec as P

NEGATIVE = -1e30
AXES = ("page", "blk")
MESH_ID = pl.DeviceIdType.MESH


def device_on(axis, j):
    return tuple(j if name == axis else lax.axis_index(name) for name in AXES)


def greet(sizes):
    barrier = pltpu.get_barrier_semaphore()
    total = 0
    for axis, n in sizes:
        me = lax.axis_index(axis)
        for k in range(1, n):
            peer = lax.rem(me + k, n)
            pl.semaphore_signal(barrier, inc=1, device_id=device_on(axis, peer), device_id_type=MESH_ID)
        total += n - 1
    return total


def enter(sizes):
    pl.semaphore_wait(pltpu.get_barrier_semaphore(), greet(sizes))


def send_round(axis, n, source, buf, send_sem, recv_sem):
    me = lax.axis_index(axis)
    copies = []
    for k in range(1, n):
        peer = lax.rem(me + k, n)
        copy = pltpu.make_async_remote_copy(
            src_ref=source(peer),
            dst_ref=buf.at[me],
            send_sem=send_sem.at[k],
            recv_sem=recv_sem.at[k],
            device_id=device_on(axis, peer),
            device_id_type=MESH_ID,
        )
        copy.start()
        copies.append(copy)
    for copy in copies:
        copy.wait()


def slot_sum(buf, n):
    total = buf[0].astype(jnp.float32)
    for j in range(1, n):
        total = total + buf[j].astype(jnp.float32)
    return total


def exchange_kernel(axis, n, x_ref, o_ref, buf, send_sem, recv_sem):
    me = lax.axis_index(axis)
    buf[me] = x_ref[me]
    enter([(axis, n)])
    send_round(axis, n, lambda peer: x_ref.at[peer], buf, send_sem, recv_sem)
    o_ref[...] = buf[...]


def sum_gather_kernel(axis, n, finish, x_ref, extra_ref, o_ref, buf, gat, sems):
    me = lax.axis_index(axis)
    buf[me] = x_ref[me]
    enter([(axis, n)])
    send_round(axis, n, lambda peer: x_ref.at[peer], buf, sems.at[0], sems.at[1])
    gat[me] = finish(slot_sum(buf, n), extra_ref[...]).astype(gat.dtype)
    send_round(axis, n, lambda peer: gat.at[me], gat, sems.at[2], sems.at[3])
    o_ref[...] = gat[...]


def output_phase(n_blk, n_page, x_ref, res_t, bias, score_w, out_ref, score_ref,
                 buf, blk_buf, page_buf, sems):
    me_blk = lax.axis_index("blk")
    me_page = lax.axis_index("page")
    buf[me_blk] = x_ref[me_blk]
    send_round("blk", n_blk, lambda peer: x_ref.at[peer], buf, sems.at[0], sems.at[1])
    output = (slot_sum(buf, n_blk) + res_t + bias).astype(jnp.bfloat16)
    out_ref[...] = output
    blk_buf[me_blk] = jnp.sum(output.astype(jnp.float32) * score_w, axis=0, keepdims=True)
    send_round("blk", n_blk, lambda peer: blk_buf.at[me_blk], blk_buf, sems.at[2], sems.at[3])
    page_buf[me_page] = slot_sum(blk_buf, n_blk)
    send_round("page", n_page, lambda peer: page_buf.at[me_page], page_buf, sems.at[4], sems.at[5])
    score_ref[...] = slot_sum(page_buf, n_page)


def softmax_rows(scores, visible):
    highest = jnp.max(jnp.where(visible, scores, NEGATIVE), axis=1, keepdims=True)
    weights = jnp.where(visible, jnp.exp(scores - highest), 0.0)
    return highest, jnp.sum(weights, axis=1, keepdims=True), weights.astype(jnp.bfloat16)


def attention_out_kernel(n_page, n_blk, heads, q_ref, kv_ref, tkv_ref, row_code_ref, key_code_ref,
                         t_lo_ref, t_hi_ref, w_ref, stream_ref,
                         res_ref, scaled_ref, part_ref, recv, full, res_s, red, gat, sems):
    me_page = lax.axis_index("page")
    me_blk = lax.axis_index("blk")
    expected = greet([("page", n_page), ("blk", n_blk)])
    hd = kv_ref.shape[1] // (2 * heads)
    own_rows = t_lo_ref.shape[0]
    inv_sqrt = 1.0 / math.sqrt(hd)
    visible = row_code_ref[...] == key_code_ref[...]
    position = lax.broadcasted_iota(jnp.int32, (1, tkv_ref.shape[0]), 1)
    tail_visible = (position >= t_lo_ref[...]) & (position <= t_hi_ref[...])
    own_block = pl.ds(pl.multiple_of(me_page * own_rows, own_rows), own_rows)
    contract = (((1,), (1,)), ((), ()))
    half = lax.broadcasted_iota(jnp.int32, (1, hd), 1) < hd // 2
    tail_parts = []
    for h in range(heads):
        keys = kv_ref[:, 2 * h * hd:(2 * h + 1) * hd]
        values = kv_ref[:, (2 * h + 1) * hd:(2 * h + 2) * hd]
        query = q_ref[:, h * hd:(h + 1) * hd]
        scores = lax.dot_general(query, keys, contract, preferred_element_type=jnp.float32) * inv_sqrt
        high, total, weights = softmax_rows(scores, visible)
        mixed = jnp.dot(weights, values, preferred_element_type=jnp.float32)
        stats = jnp.where(half, jnp.broadcast_to(high, (high.shape[0], hd)), jnp.broadcast_to(total, (high.shape[0], hd)))
        for j in range(n_page):
            rows = slice(j * own_rows, (j + 1) * own_rows)
            part_ref[j, h * own_rows:(h + 1) * own_rows, :] = jnp.concatenate([mixed[rows], stats[rows]], axis=1)
        keys = tkv_ref[:, 2 * h * hd:(2 * h + 1) * hd]
        values = tkv_ref[:, (2 * h + 1) * hd:(2 * h + 2) * hd]
        query = q_ref[own_block, h * hd:(h + 1) * hd]
        scores = lax.dot_general(query, keys, contract, preferred_element_type=jnp.float32) * inv_sqrt
        high, total, weights = softmax_rows(scores, tail_visible)
        mixed = jnp.dot(weights, values, preferred_element_type=jnp.float32)
        tail_parts.append((mixed, high, total))
    tail_mixed = jnp.concatenate([t[0] for t in tail_parts], axis=0)
    tail_high = jnp.concatenate([t[1] for t in tail_parts], axis=0)
    tail_total = jnp.concatenate([t[2] for t in tail_parts], axis=0)
    pl.semaphore_wait(pltpu.get_barrier_semaphore(), expected)
    recv[me_page] = part_ref[me_page]
    send_round("page", n_page, lambda peer: part_ref.at[peer], recv, sems.at[0], sems.at[1])
    highest = tail_high
    for j in range(n_page):
        highest = jnp.maximum(highest, recv[j][:, hd:hd + 1])
    scale = jnp.exp(tail_high - highest)
    weight_sum = tail_total * scale
    weighted = tail_mixed * scale
    for j in range(n_page):
        part = recv[j]
        scale = jnp.exp(part[:, hd:hd + 1] - highest)
        weight_sum = weight_sum + part[:, hd + hd // 2:hd + hd // 2 + 1] * scale
        weighted = weighted + part[:, :hd] * scale
    attention = (weighted / weight_sum).astype(jnp.bfloat16)
    rows = attention.shape[0] // heads
    if heads > 1:
        attention = jnp.concatenate([attention[h * rows:(h + 1) * rows] for h in range(heads)], axis=1)
    full[...] = jnp.dot(attention, w_ref[...], preferred_element_type=jnp.float32) + stream_ref[...]
    lanes = red.shape[2]
    n_chunk = gat.shape[0]

    def own(ref):
        return ref[:, pl.ds(pl.multiple_of(me_blk * lanes, lanes), lanes)]

    def scatter_copy(t):
        return pltpu.make_async_remote_copy(
            src_ref=full.at[:, pl.ds(t * lanes, lanes)],
            dst_ref=red.at[me_blk],
            send_sem=sems.at[2, t],
            recv_sem=sems.at[3, me_blk],
            device_id=device_on("blk", t),
            device_id_type=MESH_ID,
        )

    def scatter_arrival(s):
        return pltpu.make_async_remote_copy(
            src_ref=full.at[:, pl.ds(0, lanes)],
            dst_ref=red.at[s],
            send_sem=sems.at[2, 0],
            recv_sem=sems.at[3, s],
            device_id=device_on("blk", s),
            device_id_type=MESH_ID,
        )

    def gather_copy(k):
        return pltpu.make_async_remote_copy(
            src_ref=gat.at[me_blk],
            dst_ref=gat.at[me_blk],
            send_sem=sems.at[4, k],
            recv_sem=sems.at[5, me_blk],
            device_id=device_on("blk", lax.rem(me_blk + k, n_blk)),
            device_id_type=MESH_ID,
        )

    def gather_arrival(s):
        return pltpu.make_async_remote_copy(
            src_ref=gat.at[s],
            dst_ref=gat.at[s],
            send_sem=sems.at[4, 0],
            recv_sem=sems.at[5, s],
            device_id=device_on("blk", s),
            device_id_type=MESH_ID,
        )

    for t in range(n_chunk):
        @pl.when(me_blk != t)
        def _():
            scatter_copy(t).start()

    @pl.when(me_blk < n_chunk)
    def _():
        red[me_blk] = own(full)
        for s in range(n_blk):
            @pl.when(me_blk != s)
            def _():
                scatter_arrival(s).wait_recv()
        total = slot_sum(red, n_blk)
        gat[me_blk] = total.astype(jnp.bfloat16).astype(jnp.float32)
        for k in range(1, n_blk):
            gather_copy(k).start()

    for t in range(n_chunk):
        @pl.when(me_blk != t)
        def _():
            scatter_copy(t).wait_send()

    @pl.when(me_blk < n_chunk)
    def _():
        for k in range(1, n_blk):
            gather_copy(k).wait_send()

    for s in range(n_chunk):
        @pl.when(me_blk != s)
        def _():
            gather_arrival(s).wait_recv()

    for t in range(n_chunk):
        res_s[:, t * lanes:(t + 1) * lanes] = gat[t]
    residual = res_s[...]
    row_mean = jnp.mean(residual, axis=-1, keepdims=True)
    centred = residual - row_mean
    inverse_std = lax.rsqrt(jnp.mean(centred * centred, axis=-1, keepdims=True) + 1e-05)
    scaled = centred * inverse_std
    group = res_ref.shape[2]
    scaled_ref[...] = jnp.zeros(scaled_ref.shape, jnp.float32)
    for q in range(n_page):
        scaled_ref[q, :, 0:group] = scaled[:, q * group:(q + 1) * group]
        res_ref[q] = residual[:, q * group:(q + 1) * group]

def mlp_kernel(n_page, n_blk, features, x_ref, vec_ref, w_ref, w_down_ref, col_ref, out_ref, score_ref,
               recv, up_s, red, hid_ref, pieces, out_buf, blk_buf, page_buf, sems):
    me = lax.axis_index("page")
    recv[me] = x_ref[me]
    send_round("page", n_page, lambda peer: x_ref.at[peer], recv, sems.at[0], sems.at[1])
    width = col_ref.shape[0]
    lanes_in = x_ref.shape[2]
    pad = -(-features // 128) * 128
    gain = vec_ref[:, 0:features]
    bias = vec_ref[:, pad:pad + features]
    b_up = vec_ref[:, 2 * pad:]
    arrived = jnp.concatenate([recv[j] for j in range(n_page)], axis=0)
    scaled = arrived[:, :features]
    normed = (scaled * gain + bias).astype(jnp.bfloat16)
    up_s[...] = jnp.dot(normed, w_ref[...], preferred_element_type=jnp.float32).astype(jnp.bfloat16)
    block = red.shape[1]
    n_recv = up_s.shape[0] // block

    def rows_of(k):
        return pl.ds(k * block, block)

    def scatter_copy(k):
        return pltpu.make_async_remote_copy(
            src_ref=up_s.at[rows_of(k)],
            dst_ref=red.at[me],
            send_sem=sems.at[2, k],
            recv_sem=sems.at[3, me],
            device_id=device_on("page", 2 * k),
            device_id_type=MESH_ID,
        )

    def scatter_arrival(s):
        return pltpu.make_async_remote_copy(
            src_ref=up_s.at[rows_of(0)],
            dst_ref=red.at[s],
            send_sem=sems.at[2, 0],
            recv_sem=sems.at[3, s],
            device_id=device_on("page", s),
            device_id_type=MESH_ID,
        )

    def gather_copy(k, mine):
        return pltpu.make_async_remote_copy(
            src_ref=hid_ref.at[rows_of(mine)],
            dst_ref=hid_ref.at[rows_of(mine)],
            send_sem=sems.at[4, k],
            recv_sem=sems.at[5, mine],
            device_id=device_on("page", lax.rem(me + k, n_page)),
            device_id_type=MESH_ID,
        )

    def gather_arrival(k):
        return pltpu.make_async_remote_copy(
            src_ref=hid_ref.at[rows_of(k)],
            dst_ref=hid_ref.at[rows_of(k)],
            send_sem=sems.at[4, 0],
            recv_sem=sems.at[5, k],
            device_id=device_on("page", 2 * k),
            device_id_type=MESH_ID,
        )

    for k in range(n_recv):
        @pl.when(me != 2 * k)
        def _():
            scatter_copy(k).start()

    mine = me // 2

    @pl.when(me % 2 == 0)
    def _():
        red[me] = up_s[pl.ds(pl.multiple_of(mine * block, block), block)]
        for s in range(n_page):
            @pl.when(me != s)
            def _():
                scatter_arrival(s).wait_recv()
        total = slot_sum(red, n_page) + b_up
        hid_ref[pl.ds(pl.multiple_of(mine * block, block), block)] = jnp.maximum(total, 0.0).astype(
            jnp.bfloat16
        )
        for k in range(1, n_page):
            gather_copy(k, mine).start()

    for k in range(n_recv):
        @pl.when(me != 2 * k)
        def _():
            scatter_copy(k).wait_send()

    @pl.when(me % 2 == 0)
    def _():
        for k in range(1, n_page):
            gather_copy(k, mine).wait_send()

    for k in range(n_recv):
        @pl.when(me != 2 * k)
        def _():
            gather_arrival(k).wait_recv()

    projected_t = lax.dot_general(
        w_down_ref[...], hid_ref[...], (((1,), (1,)), ((), ())), preferred_element_type=jnp.float32
    )
    for j in range(n_blk):
        pieces[j] = projected_t[j * width:(j + 1) * width]
    pick = (
        lax.broadcasted_iota(jnp.int32, (width, lanes_in), 1)
        == lax.broadcasted_iota(jnp.int32, (width, lanes_in), 0) + features
    ).astype(jnp.float32)
    res_t = lax.dot_general(
        pick, arrived, (((1,), (1,)), ((), ())),
        precision=lax.Precision.HIGHEST, preferred_element_type=jnp.float32,
    )
    columns = col_ref[...]
    output_phase(n_blk, n_page, pieces, res_t, columns[:, 0:1], columns[:, 1:2], out_ref, score_ref,
                 out_buf, blk_buf, page_buf, sems.at[6:12])


def layer_kernel(n_page, n_blk, heads, features, q_ref, kv_ref, tkv_ref, row_code_ref, key_code_ref,
                 t_lo_ref, t_hi_ref, w_ref, stream_ref, vec_ref, w_up_ref, w_down_ref, col_ref,
                 out_ref, score_ref, res16, sc16, part_ref, recv1, full, res_s, red1, gat, sems1,
                 recv2, up_s, red2, hid_ref, pieces, out_buf, blk_buf, page_buf, sems2):
    attention_out_kernel(n_page, n_blk, heads, q_ref, kv_ref, tkv_ref, row_code_ref, key_code_ref,
                         t_lo_ref, t_hi_ref, w_ref, stream_ref, res16, sc16, part_ref, recv1, full,
                         res_s, red1, gat, sems1)
    me_blk = lax.axis_index("blk")
    width = col_ref.shape[0]
    lanes_in = sc16.shape[2]
    source = lax.broadcasted_iota(jnp.int32, (features, lanes_in), 0)
    target = lax.broadcasted_iota(jnp.int32, (features, lanes_in), 1)
    chosen = (target >= features) & (target < features + width) & (source == target - features + me_blk * width)
    place = chosen.astype(jnp.float32)
    for q in range(n_page):
        sc16[q] = sc16[q] + jnp.dot(
            res16[q], place, precision=lax.Precision.HIGHEST, preferred_element_type=jnp.float32
        )
    mlp_kernel(n_page, n_blk, features, sc16, vec_ref, w_up_ref, w_down_ref, col_ref, out_ref, score_ref,
               recv2, up_s, red2, hid_ref, pieces, out_buf, blk_buf, page_buf, sems2)


CALL_IDS = {}


def next_id(axis):
    cid = len(CALL_IDS)
    CALL_IDS[cid] = axis
    return cid


def vmem_specs(count):
    return [pl.BlockSpec(memory_space=pltpu.VMEM)] * count


def exchange(x, axis):
    n = lax.axis_size(axis)
    return pl.pallas_call(
        lambda *refs: exchange_kernel(axis, n, *refs),
        out_shape=jax.ShapeDtypeStruct(x.shape, x.dtype),
        in_specs=vmem_specs(1),
        out_specs=vmem_specs(1)[0],
        scratch_shapes=[
            pltpu.VMEM(x.shape, x.dtype),
            pltpu.SemaphoreType.DMA((n,)),
            pltpu.SemaphoreType.DMA((n,)),
        ],
        compiler_params=pltpu.CompilerParams(collective_id=next_id(axis), has_side_effects=True),
    )(x)


def sum_gather(x, extra, axis, finish, out_dtype):
    n = lax.axis_size(axis)
    return pl.pallas_call(
        lambda *refs: sum_gather_kernel(axis, n, finish, *refs),
        out_shape=jax.ShapeDtypeStruct(x.shape, out_dtype),
        in_specs=vmem_specs(2),
        out_specs=vmem_specs(1)[0],
        scratch_shapes=[
            pltpu.VMEM(x.shape, x.dtype),
            pltpu.VMEM(x.shape, out_dtype),
            pltpu.SemaphoreType.DMA((4, n)),
        ],
        compiler_params=pltpu.CompilerParams(collective_id=next_id(axis), has_side_effects=True),
    )(x, extra)


def attention_out(queries, kv, tkv, row_code, key_code, t_lo, t_hi, w_out, stream, head_dim):
    n_page = lax.axis_size("page")
    n_blk = lax.axis_size("blk")
    rows, width = stream.shape
    heads = kv.shape[1] // (2 * head_dim)
    lanes = 128 * (-(-width // (128 * n_blk)))
    n_chunk = width // lanes
    assert n_chunk * lanes == width
    part_shape = (n_page, heads * rows, 2 * head_dim)
    return pl.pallas_call(
        lambda *refs: attention_out_kernel(n_page, n_blk, heads, *refs),
        out_shape=(
            jax.ShapeDtypeStruct((n_page, rows, width // n_page), jnp.float32),
            jax.ShapeDtypeStruct((n_page, rows, width // n_page), jnp.float32),
        ),
        in_specs=vmem_specs(9),
        out_specs=tuple(vmem_specs(2)),
        scratch_shapes=[
            pltpu.VMEM(part_shape, jnp.float32),
            pltpu.VMEM(part_shape, jnp.float32),
            pltpu.VMEM((rows, width), jnp.float32),
            pltpu.VMEM((rows, width), jnp.float32),
            pltpu.VMEM((n_blk, rows, lanes), jnp.float32),
            pltpu.VMEM((n_chunk, rows, lanes), jnp.float32),
            pltpu.SemaphoreType.DMA((6, max(n_blk, n_page))),
        ],
        compiler_params=pltpu.CompilerParams(collective_id=next_id("both"), has_side_effects=True),
    )(queries, kv, tkv, row_code, key_code, t_lo, t_hi, w_out, stream)


def mlp(outgoing, vectors, w_up, w_down, columns):
    n_page = lax.axis_size("page")
    n_blk = lax.axis_size("blk")
    rows = outgoing.shape[0] * outgoing.shape[1]
    ff = w_up.shape[1]
    block = 2 * rows // n_page
    width = columns.shape[0]
    return pl.pallas_call(
        lambda *refs: mlp_kernel(n_page, n_blk, *refs),
        out_shape=(
            jax.ShapeDtypeStruct((width, rows), jnp.bfloat16),
            jax.ShapeDtypeStruct((1, rows), jnp.float32),
        ),
        in_specs=vmem_specs(5),
        out_specs=tuple(vmem_specs(2)),
        scratch_shapes=[
            pltpu.VMEM(outgoing.shape, jnp.float32),
            pltpu.VMEM((rows, ff), jnp.bfloat16),
            pltpu.VMEM((n_page, block, ff), jnp.bfloat16),
            pltpu.VMEM((rows, ff), jnp.bfloat16),
            pltpu.VMEM((n_blk, width, rows), jnp.float32),
            pltpu.VMEM((n_blk, width, rows), jnp.float32),
            pltpu.VMEM((n_blk, 1, rows), jnp.float32),
            pltpu.VMEM((n_page, 1, rows), jnp.float32),
            pltpu.SemaphoreType.DMA((12, max(n_page, n_blk))),
        ],
        compiler_params=pltpu.CompilerParams(collective_id=next_id("both"), has_side_effects=True),
    )(outgoing, vectors, w_up, w_down, columns)


def layer(queries, kv, tkv, row_code, key_code, t_lo, t_hi, w_out, stream, head_dim,
          vectors, w_up, w_down_t, columns, features):
    n_page = lax.axis_size("page")
    n_blk = lax.axis_size("blk")
    rows, width = stream.shape
    heads = kv.shape[1] // (2 * head_dim)
    lanes = 128 * (-(-width // (128 * n_blk)))
    n_chunk = width // lanes
    assert n_chunk * lanes == width
    part_shape = (n_page, heads * rows, 2 * head_dim)
    lanes_in = -(-(features + columns.shape[0]) // 128) * 128
    all_rows = rows * n_page
    ff = w_up.shape[1]
    block = 2 * all_rows // n_page
    piece = columns.shape[0]
    return pl.pallas_call(
        lambda *refs: layer_kernel(n_page, n_blk, heads, features, *refs),
        out_shape=(
            jax.ShapeDtypeStruct((piece, all_rows), jnp.bfloat16),
            jax.ShapeDtypeStruct((1, all_rows), jnp.float32),
        ),
        in_specs=vmem_specs(13),
        out_specs=tuple(vmem_specs(2)),
        scratch_shapes=[
            pltpu.VMEM((n_page, rows, features), jnp.float32),
            pltpu.VMEM((n_page, rows, lanes_in), jnp.float32),
            pltpu.VMEM(part_shape, jnp.float32),
            pltpu.VMEM(part_shape, jnp.float32),
            pltpu.VMEM((rows, width), jnp.float32),
            pltpu.VMEM((rows, width), jnp.float32),
            pltpu.VMEM((n_blk, rows, lanes), jnp.float32),
            pltpu.VMEM((n_chunk, rows, lanes), jnp.float32),
            pltpu.SemaphoreType.DMA((6, max(n_blk, n_page))),
            pltpu.VMEM((n_page, rows, lanes_in), jnp.float32),
            pltpu.VMEM((all_rows, ff), jnp.bfloat16),
            pltpu.VMEM((n_page, block, ff), jnp.bfloat16),
            pltpu.VMEM((all_rows, ff), jnp.bfloat16),
            pltpu.VMEM((n_blk, piece, all_rows), jnp.float32),
            pltpu.VMEM((n_blk, piece, all_rows), jnp.float32),
            pltpu.VMEM((n_blk, 1, all_rows), jnp.float32),
            pltpu.VMEM((n_page, 1, all_rows), jnp.float32),
            pltpu.SemaphoreType.DMA((12, max(n_page, n_blk))),
        ],
        compiler_params=pltpu.CompilerParams(collective_id=next_id("both"), has_side_effects=True),
    )(queries, kv, tkv, row_code, key_code, t_lo, t_hi, w_out, stream, vectors, w_up, w_down_t, columns)


def output_and_score(x, res, bias, score_w):
    n_blk = lax.axis_size("blk")
    n_page = lax.axis_size("page")
    lanes = x.shape[2]
    return pl.pallas_call(
        lambda *refs: output_kernel(n_blk, n_page, *refs),
        out_shape=(
            jax.ShapeDtypeStruct(x.shape[1:], jnp.bfloat16),
            jax.ShapeDtypeStruct((1, lanes), jnp.float32),
        ),
        in_specs=vmem_specs(4),
        out_specs=tuple(vmem_specs(2)),
        scratch_shapes=[
            pltpu.VMEM(x.shape, jnp.float32),
            pltpu.VMEM((n_blk, 1, lanes), jnp.float32),
            pltpu.VMEM((n_page, 1, lanes), jnp.float32),
            pltpu.SemaphoreType.DMA((6, max(n_blk, n_page))),
        ],
        compiler_params=pltpu.CompilerParams(collective_id=next_id("both"), has_side_effects=True),
    )(x, res, bias, score_w)


def ordered_sum(stack):
    total = stack[0]
    for j in range(1, stack.shape[0]):
        total = total + stack[j]
    return total


def body(
    queries,
    prompt_kv,
    tail_kv,
    page_table,
    prompt_len,
    tail_len,
    sample_prompt,
    stream_in,
    w_out,
    b_out,
    ln_gain,
    ln_bias,
    w_up,
    b_up,
    w_down,
    b_down,
    w_score,
):
    CALL_IDS.clear()
    samples, new_count, heads_dev, head_dim = queries.shape
    slots_dev, page_len = (prompt_kv.shape[0], prompt_kv.shape[1])
    own_count, tail_max = (tail_kv.shape[0], tail_kv.shape[1])
    prompts, pages_max = page_table.shape
    n_page = samples // own_count
    page_pos = lax.axis_index("page")
    blk_pos = lax.axis_index("blk")
    inv_sqrt = 1.0 / math.sqrt(head_dim)
    width = w_out.shape[1]
    rows_own = own_count * new_count

    entries = page_table.reshape(-1)
    slot_ids = page_pos * slots_dev + jnp.arange(slots_dev, dtype=jnp.int32)
    matched = (entries[:, None] == slot_ids[None, :]).astype(jnp.int32)
    owner_index = jnp.sum(matched * jnp.arange(entries.shape[0], dtype=jnp.int32)[:, None], axis=0)
    slot_prompt = owner_index // pages_max
    slot_page = owner_index % pages_max
    prompt_pick = (slot_prompt[:, None] == jnp.arange(prompts, dtype=jnp.int32)[None, :]).astype(
        jnp.int32
    )
    slot_limit = jnp.sum(prompt_pick * prompt_len[None, :], axis=1)
    key_pos = slot_page[:, None] * page_len + jnp.arange(page_len, dtype=jnp.int32)[None, :]
    key_live = (key_pos < slot_limit[:, None]).reshape(-1)
    key_prompt = jnp.repeat(slot_prompt, page_len)
    key_code = jnp.where(key_live, key_prompt, -1).astype(jnp.int32).reshape(1, -1)
    row_code = jnp.repeat(sample_prompt, new_count).astype(jnp.int32).reshape(-1, 1)

    first_row = page_pos * own_count
    own_lengths = lax.dynamic_slice_in_dim(tail_len, first_row, own_count, 0)
    local_row = jnp.arange(rows_own, dtype=jnp.int32)
    t_lo = (local_row // new_count) * tail_max
    t_hi = t_lo + jnp.repeat(own_lengths, new_count) + local_row % new_count

    slice_width = stream_in.shape[2]
    column = blk_pos * slice_width
    own_stream = (
        lax.dynamic_slice_in_dim(stream_in, first_row, own_count, 0)
        .reshape(rows_own, slice_width)
        .astype(jnp.float32)
    )
    own_bias = lax.dynamic_slice_in_dim(b_out, column, slice_width, 0).astype(jnp.float32)
    stream_full = lax.dynamic_update_slice_in_dim(
        jnp.zeros((rows_own, width), jnp.float32), own_stream + own_bias, column, 1
    )
    feature_count = ln_gain.shape[0]
    piece_width = b_down.shape[0]
    pad = -(-feature_count // 128) * 128
    vectors = jnp.concatenate(
        [
            jnp.pad(ln_gain.astype(jnp.float32), (0, pad - feature_count)),
            jnp.pad(ln_bias.astype(jnp.float32), (0, pad - feature_count)),
            b_up.astype(jnp.float32),
        ]
    ).reshape(1, -1)
    columns = jnp.stack([b_down.astype(jnp.float32), w_score.astype(jnp.float32)], axis=1)
    output_t, row_score = layer(
        queries.reshape(samples * new_count, heads_dev * head_dim),
        prompt_kv.reshape(slots_dev * page_len, heads_dev * 2 * head_dim),
        tail_kv.reshape(own_count * tail_max, heads_dev * 2 * head_dim),
        row_code,
        key_code,
        t_lo.reshape(-1, 1),
        t_hi.reshape(-1, 1),
        w_out,
        stream_full,
        head_dim,
        vectors,
        w_up,
        w_down.T,
        columns,
        feature_count,
    )
    output = output_t.T
    return (output.reshape(samples, new_count, piece_width), row_score.reshape(samples, new_count))


def solution(mesh):
    placed = (
        P(None, None, "blk", None),
        P("page", None, "blk", None),
        P("page", None, "blk", None),
        P(),
        P(),
        P(),
        P(),
        P(None, None, "blk"),
        P("blk", None),
        P(),
        P("page"),
        P("page"),
        P("page", "blk"),
        P("blk"),
        P("blk", "page"),
        P(("page", "blk")),
        P(("page", "blk")),
    )
    return jax.shard_map(
        body,
        mesh=mesh,
        in_specs=placed,
        out_specs=(P(None, None, ("page", "blk")), P()),
        check_vma=False,
    )
```

```python
import math

import jax
import jax.numpy as jnp
from jax import lax
from jax.experimental import pallas as pl
from jax.experimental.pallas import tpu as pltpu
from jax.sharding import PartitionSpec as P

NEGATIVE = -1e30
AXES = ("page", "blk")
MESH_ID = pl.DeviceIdType.MESH


def device_on(axis, j):
    return tuple(j if name == axis else lax.axis_index(name) for name in AXES)


def greet(sizes):
    barrier = pltpu.get_barrier_semaphore()
    total = 0
    for axis, n in sizes:
        me = lax.axis_index(axis)
        for k in range(1, n):
            peer = lax.rem(me + k, n)
            pl.semaphore_signal(barrier, inc=1, device_id=device_on(axis, peer), device_id_type=MESH_ID)
        total += n - 1
    return total


def enter(sizes):
    pl.semaphore_wait(pltpu.get_barrier_semaphore(), greet(sizes))


def send_round(axis, n, source, buf, send_sem, recv_sem):
    me = lax.axis_index(axis)
    copies = []
    for k in range(1, n):
        peer = lax.rem(me + k, n)
        copy = pltpu.make_async_remote_copy(
            src_ref=source(peer),
            dst_ref=buf.at[me],
            send_sem=send_sem.at[k],
            recv_sem=recv_sem.at[k],
            device_id=device_on(axis, peer),
            device_id_type=MESH_ID,
        )
        copy.start()
        copies.append(copy)
    for copy in copies:
        copy.wait()


def slot_sum(buf, n):
    total = buf[0].astype(jnp.float32)
    for j in range(1, n):
        total = total + buf[j].astype(jnp.float32)
    return total


def exchange_kernel(axis, n, x_ref, o_ref, buf, send_sem, recv_sem):
    me = lax.axis_index(axis)
    buf[me] = x_ref[me]
    enter([(axis, n)])
    send_round(axis, n, lambda peer: x_ref.at[peer], buf, send_sem, recv_sem)
    o_ref[...] = buf[...]


def sum_gather_kernel(axis, n, finish, x_ref, extra_ref, o_ref, buf, gat, sems):
    me = lax.axis_index(axis)
    buf[me] = x_ref[me]
    enter([(axis, n)])
    send_round(axis, n, lambda peer: x_ref.at[peer], buf, sems.at[0], sems.at[1])
    gat[me] = finish(slot_sum(buf, n), extra_ref[...]).astype(gat.dtype)
    send_round(axis, n, lambda peer: gat.at[me], gat, sems.at[2], sems.at[3])
    o_ref[...] = gat[...]


def output_phase(n_blk, n_page, x_ref, res_t, bias, score_w, out_ref, score_ref,
                 buf, blk_buf, page_buf, sems):
    me_blk = lax.axis_index("blk")
    me_page = lax.axis_index("page")
    buf[me_blk] = x_ref[me_blk]
    send_round("blk", n_blk, lambda peer: x_ref.at[peer], buf, sems.at[0], sems.at[1])
    output = (slot_sum(buf, n_blk) + res_t + bias).astype(jnp.bfloat16)
    out_ref[...] = output
    blk_buf[me_blk] = jnp.sum(output.astype(jnp.float32) * score_w, axis=0, keepdims=True)
    send_round("blk", n_blk, lambda peer: blk_buf.at[me_blk], blk_buf, sems.at[2], sems.at[3])
    page_buf[me_page] = slot_sum(blk_buf, n_blk)
    send_round("page", n_page, lambda peer: page_buf.at[me_page], page_buf, sems.at[4], sems.at[5])
    score_ref[...] = slot_sum(page_buf, n_page)


def softmax_rows(scores, visible):
    highest = jnp.max(jnp.where(visible, scores, NEGATIVE), axis=1, keepdims=True)
    weights = jnp.where(visible, jnp.exp(scores - highest), 0.0)
    return highest, jnp.sum(weights, axis=1, keepdims=True), weights.astype(jnp.bfloat16)


def attention_out_kernel(n_page, n_blk, heads, q_ref, kv_ref, tkv_ref, row_code_ref, key_code_ref,
                         t_lo_ref, t_hi_ref, w_ref, stream_ref,
                         res_ref, scaled_ref, part_ref, recv, full, res_s, red, gat, sems):
    me_page = lax.axis_index("page")
    me_blk = lax.axis_index("blk")
    expected = greet([("page", n_page), ("blk", n_blk)])
    hd = kv_ref.shape[1] // (2 * heads)
    own_rows = t_lo_ref.shape[0]
    inv_sqrt = 1.0 / math.sqrt(hd)
    visible = row_code_ref[...] == key_code_ref[...]
    position = lax.broadcasted_iota(jnp.int32, (1, tkv_ref.shape[0]), 1)
    tail_visible = (position >= t_lo_ref[...]) & (position <= t_hi_ref[...])
    own_block = pl.ds(pl.multiple_of(me_page * own_rows, own_rows), own_rows)
    contract = (((1,), (1,)), ((), ()))
    half = lax.broadcasted_iota(jnp.int32, (1, hd), 1) < hd // 2
    tail_parts = []
    for h in range(heads):
        keys = kv_ref[:, 2 * h * hd:(2 * h + 1) * hd]
        values = kv_ref[:, (2 * h + 1) * hd:(2 * h + 2) * hd]
        query = q_ref[:, h * hd:(h + 1) * hd]
        scores = lax.dot_general(query, keys, contract, preferred_element_type=jnp.float32) * inv_sqrt
        high, total, weights = softmax_rows(scores, visible)
        mixed = jnp.dot(weights, values, preferred_element_type=jnp.float32)
        stats = jnp.where(half, jnp.broadcast_to(high, (high.shape[0], hd)), jnp.broadcast_to(total, (high.shape[0], hd)))
        for j in range(n_page):
            rows = slice(j * own_rows, (j + 1) * own_rows)
            part_ref[j, h * own_rows:(h + 1) * own_rows, :] = jnp.concatenate([mixed[rows], stats[rows]], axis=1)
        keys = tkv_ref[:, 2 * h * hd:(2 * h + 1) * hd]
        values = tkv_ref[:, (2 * h + 1) * hd:(2 * h + 2) * hd]
        query = q_ref[own_block, h * hd:(h + 1) * hd]
        scores = lax.dot_general(query, keys, contract, preferred_element_type=jnp.float32) * inv_sqrt
        high, total, weights = softmax_rows(scores, tail_visible)
        mixed = jnp.dot(weights, values, preferred_element_type=jnp.float32)
        tail_parts.append((mixed, high, total))
    tail_mixed = jnp.concatenate([t[0] for t in tail_parts], axis=0)
    tail_high = jnp.concatenate([t[1] for t in tail_parts], axis=0)
    tail_total = jnp.concatenate([t[2] for t in tail_parts], axis=0)
    pl.semaphore_wait(pltpu.get_barrier_semaphore(), expected)
    recv[me_page] = part_ref[me_page]
    send_round("page", n_page, lambda peer: part_ref.at[peer], recv, sems.at[0], sems.at[1])
    highest = tail_high
    for j in range(n_page):
        highest = jnp.maximum(highest, recv[j][:, hd:hd + 1])
    scale = jnp.exp(tail_high - highest)
    weight_sum = tail_total * scale
    weighted = tail_mixed * scale
    for j in range(n_page):
        part = recv[j]
        scale = jnp.exp(part[:, hd:hd + 1] - highest)
        weight_sum = weight_sum + part[:, hd + hd // 2:hd + hd // 2 + 1] * scale
        weighted = weighted + part[:, :hd] * scale
    attention = (weighted / weight_sum).astype(jnp.bfloat16)
    rows = attention.shape[0] // heads
    if heads > 1:
        attention = jnp.concatenate([attention[h * rows:(h + 1) * rows] for h in range(heads)], axis=1)
    full[...] = jnp.dot(attention, w_ref[...], preferred_element_type=jnp.float32) + stream_ref[...]
    lanes = red.shape[2]
    n_chunk = gat.shape[0]

    def own(ref):
        return ref[:, pl.ds(pl.multiple_of(me_blk * lanes, lanes), lanes)]

    def scatter_copy(t):
        return pltpu.make_async_remote_copy(
            src_ref=full.at[:, pl.ds(t * lanes, lanes)],
            dst_ref=red.at[me_blk],
            send_sem=sems.at[2, t],
            recv_sem=sems.at[3, me_blk],
            device_id=device_on("blk", t),
            device_id_type=MESH_ID,
        )

    def scatter_arrival(s):
        return pltpu.make_async_remote_copy(
            src_ref=full.at[:, pl.ds(0, lanes)],
            dst_ref=red.at[s],
            send_sem=sems.at[2, 0],
            recv_sem=sems.at[3, s],
            device_id=device_on("blk", s),
            device_id_type=MESH_ID,
        )

    def gather_copy(k):
        return pltpu.make_async_remote_copy(
            src_ref=gat.at[me_blk],
            dst_ref=gat.at[me_blk],
            send_sem=sems.at[4, k],
            recv_sem=sems.at[5, me_blk],
            device_id=device_on("blk", lax.rem(me_blk + k, n_blk)),
            device_id_type=MESH_ID,
        )

    def gather_arrival(s):
        return pltpu.make_async_remote_copy(
            src_ref=gat.at[s],
            dst_ref=gat.at[s],
            send_sem=sems.at[4, 0],
            recv_sem=sems.at[5, s],
            device_id=device_on("blk", s),
            device_id_type=MESH_ID,
        )

    for t in range(n_chunk):
        @pl.when(me_blk != t)
        def _():
            scatter_copy(t).start()

    @pl.when(me_blk < n_chunk)
    def _():
        red[me_blk] = own(full)
        for s in range(n_blk):
            @pl.when(me_blk != s)
            def _():
                scatter_arrival(s).wait_recv()
        total = slot_sum(red, n_blk)
        gat[me_blk] = total.astype(jnp.bfloat16).astype(jnp.float32)
        for k in range(1, n_blk):
            gather_copy(k).start()

    for t in range(n_chunk):
        @pl.when(me_blk != t)
        def _():
            scatter_copy(t).wait_send()

    @pl.when(me_blk < n_chunk)
    def _():
        for k in range(1, n_blk):
            gather_copy(k).wait_send()

    for s in range(n_chunk):
        @pl.when(me_blk != s)
        def _():
            gather_arrival(s).wait_recv()

    for t in range(n_chunk):
        res_s[:, t * lanes:(t + 1) * lanes] = gat[t]
    residual = res_s[...]
    row_mean = jnp.mean(residual, axis=-1, keepdims=True)
    centred = residual - row_mean
    inverse_std = lax.rsqrt(jnp.mean(centred * centred, axis=-1, keepdims=True) + 1e-05)
    scaled = centred * inverse_std
    group = res_ref.shape[2]
    scaled_ref[...] = jnp.zeros(scaled_ref.shape, jnp.float32)
    for q in range(n_page):
        scaled_ref[q, :, 0:group] = scaled[:, q * group:(q + 1) * group]
        res_ref[q] = residual[:, q * group:(q + 1) * group]

def mlp_kernel(n_page, n_blk, features, x_ref, vec_ref, w_ref, w_down_ref, col_ref, out_ref, score_ref,
               recv, up_s, red, hid_ref, pieces, out_buf, blk_buf, page_buf, sems):
    me = lax.axis_index("page")
    recv[me] = x_ref[me]
    send_round("page", n_page, lambda peer: x_ref.at[peer], recv, sems.at[0], sems.at[1])
    width = col_ref.shape[0]
    lanes_in = x_ref.shape[2]
    pad = -(-features // 128) * 128
    gain = vec_ref[:, 0:features]
    bias = vec_ref[:, pad:pad + features]
    b_up = vec_ref[:, 2 * pad:]
    arrived = jnp.concatenate([recv[j] for j in range(n_page)], axis=0)
    scaled = arrived[:, :features]
    normed = (scaled * gain + bias).astype(jnp.bfloat16)
    up_s[...] = jnp.dot(normed, w_ref[...], preferred_element_type=jnp.float32).astype(jnp.bfloat16)
    block = red.shape[1]
    n_recv = up_s.shape[0] // block

    def rows_of(k):
        return pl.ds(k * block, block)

    def scatter_copy(k):
        return pltpu.make_async_remote_copy(
            src_ref=up_s.at[rows_of(k)],
            dst_ref=red.at[me],
            send_sem=sems.at[2, k],
            recv_sem=sems.at[3, me],
            device_id=device_on("page", 2 * k),
            device_id_type=MESH_ID,
        )

    def scatter_arrival(s):
        return pltpu.make_async_remote_copy(
            src_ref=up_s.at[rows_of(0)],
            dst_ref=red.at[s],
            send_sem=sems.at[2, 0],
            recv_sem=sems.at[3, s],
            device_id=device_on("page", s),
            device_id_type=MESH_ID,
        )

    def gather_copy(k, mine):
        return pltpu.make_async_remote_copy(
            src_ref=hid_ref.at[rows_of(mine)],
            dst_ref=hid_ref.at[rows_of(mine)],
            send_sem=sems.at[4, k],
            recv_sem=sems.at[5, mine],
            device_id=device_on("page", lax.rem(me + k, n_page)),
            device_id_type=MESH_ID,
        )

    def gather_arrival(k):
        return pltpu.make_async_remote_copy(
            src_ref=hid_ref.at[rows_of(k)],
            dst_ref=hid_ref.at[rows_of(k)],
            send_sem=sems.at[4, 0],
            recv_sem=sems.at[5, k],
            device_id=device_on("page", 2 * k),
            device_id_type=MESH_ID,
        )

    for k in range(n_recv):
        @pl.when(me != 2 * k)
        def _():
            scatter_copy(k).start()

    mine = me // 2

    @pl.when(me % 2 == 0)
    def _():
        red[me] = up_s[pl.ds(pl.multiple_of(mine * block, block), block)]
        for s in range(n_page):
            @pl.when(me != s)
            def _():
                scatter_arrival(s).wait_recv()
        total = slot_sum(red, n_page) + b_up
        hid_ref[pl.ds(pl.multiple_of(mine * block, block), block)] = jnp.maximum(total, 0.0).astype(
            jnp.bfloat16
        )
        for k in range(1, n_page):
            gather_copy(k, mine).start()

    for k in range(n_recv):
        @pl.when(me != 2 * k)
        def _():
            scatter_copy(k).wait_send()

    @pl.when(me % 2 == 0)
    def _():
        for k in range(1, n_page):
            gather_copy(k, mine).wait_send()

    for k in range(n_recv):
        @pl.when(me != 2 * k)
        def _():
            gather_arrival(k).wait_recv()

    projected_t = lax.dot_general(
        w_down_ref[...], hid_ref[...], (((1,), (1,)), ((), ())), preferred_element_type=jnp.float32
    )
    for j in range(n_blk):
        pieces[j] = projected_t[j * width:(j + 1) * width]
    pick = (
        lax.broadcasted_iota(jnp.int32, (width, lanes_in), 1)
        == lax.broadcasted_iota(jnp.int32, (width, lanes_in), 0) + features
    ).astype(jnp.bfloat16)
    res_t = lax.dot_general(
        pick, arrived.astype(jnp.bfloat16), (((1,), (1,)), ((), ())), preferred_element_type=jnp.float32
    )
    columns = col_ref[...]
    output_phase(n_blk, n_page, pieces, res_t, columns[:, 0:1], columns[:, 1:2], out_ref, score_ref,
                 out_buf, blk_buf, page_buf, sems.at[6:12])


def layer_kernel(n_page, n_blk, heads, features, q_ref, kv_ref, tkv_ref, row_code_ref, key_code_ref,
                 t_lo_ref, t_hi_ref, w_ref, stream_ref, vec_ref, w_up_ref, w_down_ref, col_ref,
                 out_ref, score_ref, res16, sc16, part_ref, recv1, full, res_s, red1, gat, sems1,
                 recv2, up_s, red2, hid_ref, pieces, out_buf, blk_buf, page_buf, sems2):
    attention_out_kernel(n_page, n_blk, heads, q_ref, kv_ref, tkv_ref, row_code_ref, key_code_ref,
                         t_lo_ref, t_hi_ref, w_ref, stream_ref, res16, sc16, part_ref, recv1, full,
                         res_s, red1, gat, sems1)
    me_blk = lax.axis_index("blk")
    width = col_ref.shape[0]
    lanes_in = sc16.shape[2]
    source = lax.broadcasted_iota(jnp.int32, (features, lanes_in), 0)
    target = lax.broadcasted_iota(jnp.int32, (features, lanes_in), 1)
    chosen = (target >= features) & (target < features + width) & (source == target - features + me_blk * width)
    place = chosen.astype(jnp.bfloat16)
    for q in range(n_page):
        sc16[q] = sc16[q] + jnp.dot(
            res16[q].astype(jnp.bfloat16), place, preferred_element_type=jnp.float32
        )
    mlp_kernel(n_page, n_blk, features, sc16, vec_ref, w_up_ref, w_down_ref, col_ref, out_ref, score_ref,
               recv2, up_s, red2, hid_ref, pieces, out_buf, blk_buf, page_buf, sems2)


CALL_IDS = {}


def next_id(axis):
    cid = len(CALL_IDS)
    CALL_IDS[cid] = axis
    return cid


def vmem_specs(count):
    return [pl.BlockSpec(memory_space=pltpu.VMEM)] * count


def exchange(x, axis):
    n = lax.axis_size(axis)
    return pl.pallas_call(
        lambda *refs: exchange_kernel(axis, n, *refs),
        out_shape=jax.ShapeDtypeStruct(x.shape, x.dtype),
        in_specs=vmem_specs(1),
        out_specs=vmem_specs(1)[0],
        scratch_shapes=[
            pltpu.VMEM(x.shape, x.dtype),
            pltpu.SemaphoreType.DMA((n,)),
            pltpu.SemaphoreType.DMA((n,)),
        ],
        compiler_params=pltpu.CompilerParams(collective_id=next_id(axis), has_side_effects=True),
    )(x)


def sum_gather(x, extra, axis, finish, out_dtype):
    n = lax.axis_size(axis)
    return pl.pallas_call(
        lambda *refs: sum_gather_kernel(axis, n, finish, *refs),
        out_shape=jax.ShapeDtypeStruct(x.shape, out_dtype),
        in_specs=vmem_specs(2),
        out_specs=vmem_specs(1)[0],
        scratch_shapes=[
            pltpu.VMEM(x.shape, x.dtype),
            pltpu.VMEM(x.shape, out_dtype),
            pltpu.SemaphoreType.DMA((4, n)),
        ],
        compiler_params=pltpu.CompilerParams(collective_id=next_id(axis), has_side_effects=True),
    )(x, extra)


def attention_out(queries, kv, tkv, row_code, key_code, t_lo, t_hi, w_out, stream, head_dim):
    n_page = lax.axis_size("page")
    n_blk = lax.axis_size("blk")
    rows, width = stream.shape
    heads = kv.shape[1] // (2 * head_dim)
    lanes = 128 * (-(-width // (128 * n_blk)))
    n_chunk = width // lanes
    assert n_chunk * lanes == width
    part_shape = (n_page, heads * rows, 2 * head_dim)
    return pl.pallas_call(
        lambda *refs: attention_out_kernel(n_page, n_blk, heads, *refs),
        out_shape=(
            jax.ShapeDtypeStruct((n_page, rows, width // n_page), jnp.float32),
            jax.ShapeDtypeStruct((n_page, rows, width // n_page), jnp.float32),
        ),
        in_specs=vmem_specs(9),
        out_specs=tuple(vmem_specs(2)),
        scratch_shapes=[
            pltpu.VMEM(part_shape, jnp.float32),
            pltpu.VMEM(part_shape, jnp.float32),
            pltpu.VMEM((rows, width), jnp.float32),
            pltpu.VMEM((rows, width), jnp.float32),
            pltpu.VMEM((n_blk, rows, lanes), jnp.float32),
            pltpu.VMEM((n_chunk, rows, lanes), jnp.float32),
            pltpu.SemaphoreType.DMA((6, max(n_blk, n_page))),
        ],
        compiler_params=pltpu.CompilerParams(collective_id=next_id("both"), has_side_effects=True),
    )(queries, kv, tkv, row_code, key_code, t_lo, t_hi, w_out, stream)


def mlp(outgoing, vectors, w_up, w_down, columns):
    n_page = lax.axis_size("page")
    n_blk = lax.axis_size("blk")
    rows = outgoing.shape[0] * outgoing.shape[1]
    ff = w_up.shape[1]
    block = 2 * rows // n_page
    width = columns.shape[0]
    return pl.pallas_call(
        lambda *refs: mlp_kernel(n_page, n_blk, *refs),
        out_shape=(
            jax.ShapeDtypeStruct((width, rows), jnp.bfloat16),
            jax.ShapeDtypeStruct((1, rows), jnp.float32),
        ),
        in_specs=vmem_specs(5),
        out_specs=tuple(vmem_specs(2)),
        scratch_shapes=[
            pltpu.VMEM(outgoing.shape, jnp.float32),
            pltpu.VMEM((rows, ff), jnp.bfloat16),
            pltpu.VMEM((n_page, block, ff), jnp.bfloat16),
            pltpu.VMEM((rows, ff), jnp.bfloat16),
            pltpu.VMEM((n_blk, width, rows), jnp.float32),
            pltpu.VMEM((n_blk, width, rows), jnp.float32),
            pltpu.VMEM((n_blk, 1, rows), jnp.float32),
            pltpu.VMEM((n_page, 1, rows), jnp.float32),
            pltpu.SemaphoreType.DMA((12, max(n_page, n_blk))),
        ],
        compiler_params=pltpu.CompilerParams(collective_id=next_id("both"), has_side_effects=True),
    )(outgoing, vectors, w_up, w_down, columns)


def layer(queries, kv, tkv, row_code, key_code, t_lo, t_hi, w_out, stream, head_dim,
          vectors, w_up, w_down_t, columns, features):
    n_page = lax.axis_size("page")
    n_blk = lax.axis_size("blk")
    rows, width = stream.shape
    heads = kv.shape[1] // (2 * head_dim)
    lanes = 128 * (-(-width // (128 * n_blk)))
    n_chunk = width // lanes
    assert n_chunk * lanes == width
    part_shape = (n_page, heads * rows, 2 * head_dim)
    lanes_in = -(-(features + columns.shape[0]) // 128) * 128
    all_rows = rows * n_page
    ff = w_up.shape[1]
    block = 2 * all_rows // n_page
    piece = columns.shape[0]
    return pl.pallas_call(
        lambda *refs: layer_kernel(n_page, n_blk, heads, features, *refs),
        out_shape=(
            jax.ShapeDtypeStruct((piece, all_rows), jnp.bfloat16),
            jax.ShapeDtypeStruct((1, all_rows), jnp.float32),
        ),
        in_specs=vmem_specs(13),
        out_specs=tuple(vmem_specs(2)),
        scratch_shapes=[
            pltpu.VMEM((n_page, rows, features), jnp.float32),
            pltpu.VMEM((n_page, rows, lanes_in), jnp.float32),
            pltpu.VMEM(part_shape, jnp.float32),
            pltpu.VMEM(part_shape, jnp.float32),
            pltpu.VMEM((rows, width), jnp.float32),
            pltpu.VMEM((rows, width), jnp.float32),
            pltpu.VMEM((n_blk, rows, lanes), jnp.float32),
            pltpu.VMEM((n_chunk, rows, lanes), jnp.float32),
            pltpu.SemaphoreType.DMA((6, max(n_blk, n_page))),
            pltpu.VMEM((n_page, rows, lanes_in), jnp.float32),
            pltpu.VMEM((all_rows, ff), jnp.bfloat16),
            pltpu.VMEM((n_page, block, ff), jnp.bfloat16),
            pltpu.VMEM((all_rows, ff), jnp.bfloat16),
            pltpu.VMEM((n_blk, piece, all_rows), jnp.float32),
            pltpu.VMEM((n_blk, piece, all_rows), jnp.float32),
            pltpu.VMEM((n_blk, 1, all_rows), jnp.float32),
            pltpu.VMEM((n_page, 1, all_rows), jnp.float32),
            pltpu.SemaphoreType.DMA((12, max(n_page, n_blk))),
        ],
        compiler_params=pltpu.CompilerParams(collective_id=next_id("both"), has_side_effects=True),
    )(queries, kv, tkv, row_code, key_code, t_lo, t_hi, w_out, stream, vectors, w_up, w_down_t, columns)


def output_and_score(x, res, bias, score_w):
    n_blk = lax.axis_size("blk")
    n_page = lax.axis_size("page")
    lanes = x.shape[2]
    return pl.pallas_call(
        lambda *refs: output_kernel(n_blk, n_page, *refs),
        out_shape=(
            jax.ShapeDtypeStruct(x.shape[1:], jnp.bfloat16),
            jax.ShapeDtypeStruct((1, lanes), jnp.float32),
        ),
        in_specs=vmem_specs(4),
        out_specs=tuple(vmem_specs(2)),
        scratch_shapes=[
            pltpu.VMEM(x.shape, jnp.float32),
            pltpu.VMEM((n_blk, 1, lanes), jnp.float32),
            pltpu.VMEM((n_page, 1, lanes), jnp.float32),
            pltpu.SemaphoreType.DMA((6, max(n_blk, n_page))),
        ],
        compiler_params=pltpu.CompilerParams(collective_id=next_id("both"), has_side_effects=True),
    )(x, res, bias, score_w)


def ordered_sum(stack):
    total = stack[0]
    for j in range(1, stack.shape[0]):
        total = total + stack[j]
    return total


def body(
    queries,
    prompt_kv,
    tail_kv,
    page_table,
    prompt_len,
    tail_len,
    sample_prompt,
    stream_in,
    w_out,
    b_out,
    ln_gain,
    ln_bias,
    w_up,
    b_up,
    w_down,
    b_down,
    w_score,
):
    CALL_IDS.clear()
    samples, new_count, heads_dev, head_dim = queries.shape
    slots_dev, page_len = (prompt_kv.shape[0], prompt_kv.shape[1])
    own_count, tail_max = (tail_kv.shape[0], tail_kv.shape[1])
    prompts, pages_max = page_table.shape
    n_page = samples // own_count
    page_pos = lax.axis_index("page")
    blk_pos = lax.axis_index("blk")
    inv_sqrt = 1.0 / math.sqrt(head_dim)
    width = w_out.shape[1]
    rows_own = own_count * new_count

    entries = page_table.reshape(-1)
    slot_ids = page_pos * slots_dev + jnp.arange(slots_dev, dtype=jnp.int32)
    matched = (entries[:, None] == slot_ids[None, :]).astype(jnp.int32)
    owner_index = jnp.sum(matched * jnp.arange(entries.shape[0], dtype=jnp.int32)[:, None], axis=0)
    slot_prompt = owner_index // pages_max
    slot_page = owner_index % pages_max
    prompt_pick = (slot_prompt[:, None] == jnp.arange(prompts, dtype=jnp.int32)[None, :]).astype(
        jnp.int32
    )
    slot_limit = jnp.sum(prompt_pick * prompt_len[None, :], axis=1)
    key_pos = slot_page[:, None] * page_len + jnp.arange(page_len, dtype=jnp.int32)[None, :]
    key_live = (key_pos < slot_limit[:, None]).reshape(-1)
    key_prompt = jnp.repeat(slot_prompt, page_len)
    key_code = jnp.where(key_live, key_prompt, -1).astype(jnp.int32).reshape(1, -1)
    row_code = jnp.repeat(sample_prompt, new_count).astype(jnp.int32).reshape(-1, 1)

    first_row = page_pos * own_count
    own_lengths = lax.dynamic_slice_in_dim(tail_len, first_row, own_count, 0)
    local_row = jnp.arange(rows_own, dtype=jnp.int32)
    t_lo = (local_row // new_count) * tail_max
    t_hi = t_lo + jnp.repeat(own_lengths, new_count) + local_row % new_count

    slice_width = stream_in.shape[2]
    column = blk_pos * slice_width
    own_stream = (
        lax.dynamic_slice_in_dim(stream_in, first_row, own_count, 0)
        .reshape(rows_own, slice_width)
        .astype(jnp.float32)
    )
    own_bias = lax.dynamic_slice_in_dim(b_out, column, slice_width, 0).astype(jnp.float32)
    stream_full = lax.dynamic_update_slice_in_dim(
        jnp.zeros((rows_own, width), jnp.float32), own_stream + own_bias, column, 1
    )
    feature_count = ln_gain.shape[0]
    piece_width = b_down.shape[0]
    pad = -(-feature_count // 128) * 128
    vectors = jnp.concatenate(
        [
            jnp.pad(ln_gain.astype(jnp.float32), (0, pad - feature_count)),
            jnp.pad(ln_bias.astype(jnp.float32), (0, pad - feature_count)),
            b_up.astype(jnp.float32),
        ]
    ).reshape(1, -1)
    columns = jnp.stack([b_down.astype(jnp.float32), w_score.astype(jnp.float32)], axis=1)
    output_t, row_score = layer(
        queries.reshape(samples * new_count, heads_dev * head_dim),
        prompt_kv.reshape(slots_dev * page_len, heads_dev * 2 * head_dim),
        tail_kv.reshape(own_count * tail_max, heads_dev * 2 * head_dim),
        row_code,
        key_code,
        t_lo.reshape(-1, 1),
        t_hi.reshape(-1, 1),
        w_out,
        stream_full,
        head_dim,
        vectors,
        w_up,
        w_down.T,
        columns,
        feature_count,
    )
    output = output_t.T
    return (output.reshape(samples, new_count, piece_width), row_score.reshape(samples, new_count))


def solution(mesh):
    placed = (
        P(None, None, "blk", None),
        P("page", None, "blk", None),
        P("page", None, "blk", None),
        P(),
        P(),
        P(),
        P(),
        P(None, None, "blk"),
        P("blk", None),
        P(),
        P("page"),
        P("page"),
        P("page", "blk"),
        P("blk"),
        P("blk", "page"),
        P(("page", "blk")),
        P(("page", "blk")),
    )
    return jax.shard_map(
        body,
        mesh=mesh,
        in_specs=placed,
        out_specs=(P(None, None, ("page", "blk")), P()),
        check_vma=False,
    )
```

```python
import math

import jax
import jax.numpy as jnp
from jax import lax
from jax.experimental import pallas as pl
from jax.experimental.pallas import tpu as pltpu
from jax.sharding import PartitionSpec as P

NEGATIVE = -1e30
AXES = ("page", "blk")
MESH_ID = pl.DeviceIdType.MESH


def device_on(axis, j):
    return tuple(j if name == axis else lax.axis_index(name) for name in AXES)


def greet(sizes):
    barrier = pltpu.get_barrier_semaphore()
    total = 0
    for axis, n in sizes:
        me = lax.axis_index(axis)
        for k in range(1, n):
            peer = lax.rem(me + k, n)
            pl.semaphore_signal(barrier, inc=1, device_id=device_on(axis, peer), device_id_type=MESH_ID)
        total += n - 1
    return total


def enter(sizes):
    pl.semaphore_wait(pltpu.get_barrier_semaphore(), greet(sizes))


def send_round(axis, n, source, buf, send_sem, recv_sem):
    me = lax.axis_index(axis)
    copies = []
    for k in range(1, n):
        peer = lax.rem(me + k, n)
        copy = pltpu.make_async_remote_copy(
            src_ref=source(peer),
            dst_ref=buf.at[me],
            send_sem=send_sem.at[k],
            recv_sem=recv_sem.at[k],
            device_id=device_on(axis, peer),
            device_id_type=MESH_ID,
        )
        copy.start()
        copies.append(copy)
    for copy in copies:
        copy.wait()


def slot_sum(buf, n):
    total = buf[0].astype(jnp.float32)
    for j in range(1, n):
        total = total + buf[j].astype(jnp.float32)
    return total


def exchange_kernel(axis, n, x_ref, o_ref, buf, send_sem, recv_sem):
    me = lax.axis_index(axis)
    buf[me] = x_ref[me]
    enter([(axis, n)])
    send_round(axis, n, lambda peer: x_ref.at[peer], buf, send_sem, recv_sem)
    o_ref[...] = buf[...]


def sum_gather_kernel(axis, n, finish, x_ref, extra_ref, o_ref, buf, gat, sems):
    me = lax.axis_index(axis)
    buf[me] = x_ref[me]
    enter([(axis, n)])
    send_round(axis, n, lambda peer: x_ref.at[peer], buf, sems.at[0], sems.at[1])
    gat[me] = finish(slot_sum(buf, n), extra_ref[...]).astype(gat.dtype)
    send_round(axis, n, lambda peer: gat.at[me], gat, sems.at[2], sems.at[3])
    o_ref[...] = gat[...]


def output_phase(n_blk, n_page, x_ref, res_t, bias, score_w, out_ref, score_ref,
                 buf, blk_buf, page_buf, sems):
    me_blk = lax.axis_index("blk")
    me_page = lax.axis_index("page")
    buf[me_blk] = x_ref[me_blk]
    send_round("blk", n_blk, lambda peer: x_ref.at[peer], buf, sems.at[0], sems.at[1])
    output = (slot_sum(buf, n_blk) + res_t + bias).astype(jnp.bfloat16)
    out_ref[...] = output
    blk_buf[me_blk] = jnp.sum(output.astype(jnp.float32) * score_w, axis=0, keepdims=True)
    send_round("blk", n_blk, lambda peer: blk_buf.at[me_blk], blk_buf, sems.at[2], sems.at[3])
    page_buf[me_page] = slot_sum(blk_buf, n_blk)
    send_round("page", n_page, lambda peer: page_buf.at[me_page], page_buf, sems.at[4], sems.at[5])
    score_ref[...] = slot_sum(page_buf, n_page)


def softmax_rows(scores, visible):
    highest = jnp.max(jnp.where(visible, scores, NEGATIVE), axis=1, keepdims=True)
    weights = jnp.where(visible, jnp.exp(scores - highest), 0.0)
    return highest, jnp.sum(weights, axis=1, keepdims=True), weights.astype(jnp.bfloat16)


def attention_out_kernel(n_page, n_blk, heads, q_ref, kv_ref, tkv_ref, row_code_ref, key_code_ref,
                         t_lo_ref, t_hi_ref, w_ref, stream_ref,
                         res_ref, scaled_ref, part_ref, recv, full, res_s, red, gat, sems):
    me_page = lax.axis_index("page")
    me_blk = lax.axis_index("blk")
    expected = greet([("page", n_page), ("blk", n_blk)])
    hd = kv_ref.shape[1] // (2 * heads)
    own_rows = t_lo_ref.shape[0]
    inv_sqrt = 1.0 / math.sqrt(hd)
    visible = row_code_ref[...] == key_code_ref[...]
    position = lax.broadcasted_iota(jnp.int32, (1, tkv_ref.shape[0]), 1)
    tail_visible = (position >= t_lo_ref[...]) & (position <= t_hi_ref[...])
    own_block = pl.ds(pl.multiple_of(me_page * own_rows, own_rows), own_rows)
    contract = (((1,), (1,)), ((), ()))
    half = lax.broadcasted_iota(jnp.int32, (1, hd), 1) < hd // 2
    tail_parts = []
    for h in range(heads):
        keys = kv_ref[:, 2 * h * hd:(2 * h + 1) * hd]
        values = kv_ref[:, (2 * h + 1) * hd:(2 * h + 2) * hd]
        query = q_ref[:, h * hd:(h + 1) * hd]
        scores = lax.dot_general(query, keys, contract, preferred_element_type=jnp.float32) * inv_sqrt
        high, total, weights = softmax_rows(scores, visible)
        mixed = jnp.dot(weights, values, preferred_element_type=jnp.float32)
        stats = jnp.where(half, jnp.broadcast_to(high, (high.shape[0], hd)), jnp.broadcast_to(total, (high.shape[0], hd)))
        for j in range(n_page):
            rows = slice(j * own_rows, (j + 1) * own_rows)
            part_ref[j, h * own_rows:(h + 1) * own_rows, :] = jnp.concatenate([mixed[rows], stats[rows]], axis=1)
        keys = tkv_ref[:, 2 * h * hd:(2 * h + 1) * hd]
        values = tkv_ref[:, (2 * h + 1) * hd:(2 * h + 2) * hd]
        query = q_ref[own_block, h * hd:(h + 1) * hd]
        scores = lax.dot_general(query, keys, contract, preferred_element_type=jnp.float32) * inv_sqrt
        high, total, weights = softmax_rows(scores, tail_visible)
        mixed = jnp.dot(weights, values, preferred_element_type=jnp.float32)
        tail_parts.append((mixed, high, total))
    tail_mixed = jnp.concatenate([t[0] for t in tail_parts], axis=0)
    tail_high = jnp.concatenate([t[1] for t in tail_parts], axis=0)
    tail_total = jnp.concatenate([t[2] for t in tail_parts], axis=0)
    pl.semaphore_wait(pltpu.get_barrier_semaphore(), expected)
    recv[me_page] = part_ref[me_page]
    send_round("page", n_page, lambda peer: part_ref.at[peer], recv, sems.at[0], sems.at[1])
    highest = tail_high
    for j in range(n_page):
        highest = jnp.maximum(highest, recv[j][:, hd:hd + 1])
    scale = jnp.exp(tail_high - highest)
    weight_sum = tail_total * scale
    weighted = tail_mixed * scale
    for j in range(n_page):
        part = recv[j]
        scale = jnp.exp(part[:, hd:hd + 1] - highest)
        weight_sum = weight_sum + part[:, hd + hd // 2:hd + hd // 2 + 1] * scale
        weighted = weighted + part[:, :hd] * scale
    attention = (weighted / weight_sum).astype(jnp.bfloat16)
    rows = attention.shape[0] // heads
    if heads > 1:
        attention = jnp.concatenate([attention[h * rows:(h + 1) * rows] for h in range(heads)], axis=1)
    full[...] = jnp.dot(attention, w_ref[...], preferred_element_type=jnp.float32) + stream_ref[...]
    lanes = red.shape[2]
    n_chunk = gat.shape[0]

    def own(ref):
        return ref[:, pl.ds(pl.multiple_of(me_blk * lanes, lanes), lanes)]

    def scatter_copy(t):
        return pltpu.make_async_remote_copy(
            src_ref=full.at[:, pl.ds(t * lanes, lanes)],
            dst_ref=red.at[me_blk],
            send_sem=sems.at[2, t],
            recv_sem=sems.at[3, me_blk],
            device_id=device_on("blk", t),
            device_id_type=MESH_ID,
        )

    def scatter_arrival(s):
        return pltpu.make_async_remote_copy(
            src_ref=full.at[:, pl.ds(0, lanes)],
            dst_ref=red.at[s],
            send_sem=sems.at[2, 0],
            recv_sem=sems.at[3, s],
            device_id=device_on("blk", s),
            device_id_type=MESH_ID,
        )

    def gather_copy(k):
        return pltpu.make_async_remote_copy(
            src_ref=gat.at[me_blk],
            dst_ref=gat.at[me_blk],
            send_sem=sems.at[4, k],
            recv_sem=sems.at[5, me_blk],
            device_id=device_on("blk", lax.rem(me_blk + k, n_blk)),
            device_id_type=MESH_ID,
        )

    def gather_arrival(s):
        return pltpu.make_async_remote_copy(
            src_ref=gat.at[s],
            dst_ref=gat.at[s],
            send_sem=sems.at[4, 0],
            recv_sem=sems.at[5, s],
            device_id=device_on("blk", s),
            device_id_type=MESH_ID,
        )

    for t in range(n_chunk):
        @pl.when(me_blk != t)
        def _():
            scatter_copy(t).start()

    @pl.when(me_blk < n_chunk)
    def _():
        red[me_blk] = own(full)
        for s in range(n_blk):
            @pl.when(me_blk != s)
            def _():
                scatter_arrival(s).wait_recv()
        total = slot_sum(red, n_blk)
        gat[me_blk] = total.astype(jnp.bfloat16).astype(jnp.float32)
        for k in range(1, n_blk):
            gather_copy(k).start()

    for t in range(n_chunk):
        @pl.when(me_blk != t)
        def _():
            scatter_copy(t).wait_send()

    @pl.when(me_blk < n_chunk)
    def _():
        for k in range(1, n_blk):
            gather_copy(k).wait_send()

    for s in range(n_chunk):
        @pl.when(me_blk != s)
        def _():
            gather_arrival(s).wait_recv()

    for t in range(n_chunk):
        res_s[:, t * lanes:(t + 1) * lanes] = gat[t]
    residual = res_s[...]
    row_mean = jnp.mean(residual, axis=-1, keepdims=True)
    centred = residual - row_mean
    inverse_std = lax.rsqrt(jnp.mean(centred * centred, axis=-1, keepdims=True) + 1e-05)
    scaled = centred * inverse_std
    group = res_ref.shape[2]
    scaled_ref[...] = jnp.zeros(scaled_ref.shape, jnp.float32)
    for q in range(n_page):
        scaled_ref[q, :, 0:group] = scaled[:, q * group:(q + 1) * group]
        res_ref[q] = residual[:, q * group:(q + 1) * group]

def mlp_kernel(n_page, n_blk, features, x_ref, vec_ref, w_ref, w_down_ref, col_ref, out_ref, score_ref,
               recv, up_s, red, hid_ref, pieces, out_buf, blk_buf, page_buf, sems):
    me = lax.axis_index("page")
    recv[me] = x_ref[me]
    send_round("page", n_page, lambda peer: x_ref.at[peer], recv, sems.at[0], sems.at[1])
    width = col_ref.shape[0]
    lanes_in = x_ref.shape[2]
    pad = -(-features // 128) * 128
    gain = vec_ref[:, 0:features]
    bias = vec_ref[:, pad:pad + features]
    b_up = vec_ref[:, 2 * pad:]
    arrived = jnp.concatenate([recv[j] for j in range(n_page)], axis=0)
    scaled = arrived[:, :features]
    normed = (scaled * gain + bias).astype(jnp.bfloat16)
    up_s[...] = jnp.dot(normed, w_ref[...], preferred_element_type=jnp.float32).astype(jnp.bfloat16)
    block = red.shape[1]
    n_recv = up_s.shape[0] // block

    def rows_of(k):
        return pl.ds(k * block, block)

    def scatter_copy(k):
        return pltpu.make_async_remote_copy(
            src_ref=up_s.at[rows_of(k)],
            dst_ref=red.at[me],
            send_sem=sems.at[2, k],
            recv_sem=sems.at[3, me],
            device_id=device_on("page", 2 * k),
            device_id_type=MESH_ID,
        )

    def scatter_arrival(s):
        return pltpu.make_async_remote_copy(
            src_ref=up_s.at[rows_of(0)],
            dst_ref=red.at[s],
            send_sem=sems.at[2, 0],
            recv_sem=sems.at[3, s],
            device_id=device_on("page", s),
            device_id_type=MESH_ID,
        )

    def gather_copy(k, mine):
        return pltpu.make_async_remote_copy(
            src_ref=hid_ref.at[rows_of(mine)],
            dst_ref=hid_ref.at[rows_of(mine)],
            send_sem=sems.at[4, k],
            recv_sem=sems.at[5, mine],
            device_id=device_on("page", lax.rem(me + k, n_page)),
            device_id_type=MESH_ID,
        )

    def gather_arrival(k):
        return pltpu.make_async_remote_copy(
            src_ref=hid_ref.at[rows_of(k)],
            dst_ref=hid_ref.at[rows_of(k)],
            send_sem=sems.at[4, 0],
            recv_sem=sems.at[5, k],
            device_id=device_on("page", 2 * k),
            device_id_type=MESH_ID,
        )

    for k in range(n_recv):
        @pl.when(me != 2 * k)
        def _():
            scatter_copy(k).start()

    mine = me // 2

    @pl.when(me % 2 == 0)
    def _():
        red[me] = up_s[pl.ds(pl.multiple_of(mine * block, block), block)]
        for s in range(n_page):
            @pl.when(me != s)
            def _():
                scatter_arrival(s).wait_recv()
        total = slot_sum(red, n_page) + b_up
        hid_ref[pl.ds(pl.multiple_of(mine * block, block), block)] = jnp.maximum(total, 0.0).astype(
            jnp.bfloat16
        )
        for k in range(1, n_page):
            gather_copy(k, mine).start()

    for k in range(n_recv):
        @pl.when(me != 2 * k)
        def _():
            scatter_copy(k).wait_send()

    @pl.when(me % 2 == 0)
    def _():
        for k in range(1, n_page):
            gather_copy(k, mine).wait_send()

    for k in range(n_recv):
        @pl.when(me != 2 * k)
        def _():
            gather_arrival(k).wait_recv()

    projected_t = lax.dot_general(
        w_down_ref[...], hid_ref[...], (((1,), (1,)), ((), ())), preferred_element_type=jnp.float32
    )
    for j in range(n_blk):
        pieces[j] = projected_t[j * width:(j + 1) * width]
    pick = (
        lax.broadcasted_iota(jnp.int32, (width, lanes_in), 1)
        == lax.broadcasted_iota(jnp.int32, (width, lanes_in), 0) + features
    ).astype(jnp.bfloat16)
    res_t = lax.dot_general(
        pick, arrived.astype(jnp.bfloat16), (((1,), (1,)), ((), ())), preferred_element_type=jnp.float32
    )
    columns = col_ref[...]
    output_phase(n_blk, n_page, pieces, res_t, columns[:, 0:1], columns[:, 1:2], out_ref, score_ref,
                 out_buf, blk_buf, page_buf, sems.at[6:12])


def layer_kernel(n_page, n_blk, heads, features, q_ref, kv_ref, tkv_ref, row_code_ref, key_code_ref,
                 t_lo_ref, t_hi_ref, w_ref, stream_ref, vec_ref, w_up_ref, w_down_ref, col_ref,
                 out_ref, score_ref, res16, sc16, part_ref, recv1, full, res_s, red1, gat, sems1,
                 recv2, up_s, red2, hid_ref, pieces, out_buf, blk_buf, page_buf, sems2):
    attention_out_kernel(n_page, n_blk, heads, q_ref, kv_ref, tkv_ref, row_code_ref, key_code_ref,
                         t_lo_ref, t_hi_ref, w_ref, stream_ref, res16, sc16, part_ref, recv1, full,
                         res_s, red1, gat, sems1)
    me_blk = lax.axis_index("blk")
    width = col_ref.shape[0]
    lanes_in = sc16.shape[2]
    source = lax.broadcasted_iota(jnp.int32, (features, lanes_in), 0)
    target = lax.broadcasted_iota(jnp.int32, (features, lanes_in), 1)
    chosen = (target >= features) & (target < features + width) & (source == target - features + me_blk * width)
    place = chosen.astype(jnp.bfloat16)
    rows = res16.shape[1]
    stacked = jnp.concatenate([res16[q] for q in range(n_page)], axis=0).astype(jnp.bfloat16)
    placed = jnp.dot(stacked, place, preferred_element_type=jnp.float32)
    for q in range(n_page):
        sc16[q] = sc16[q] + placed[q * rows:(q + 1) * rows]
    mlp_kernel(n_page, n_blk, features, sc16, vec_ref, w_up_ref, w_down_ref, col_ref, out_ref, score_ref,
               recv2, up_s, red2, hid_ref, pieces, out_buf, blk_buf, page_buf, sems2)


CALL_IDS = {}


def next_id(axis):
    cid = len(CALL_IDS)
    CALL_IDS[cid] = axis
    return cid


def vmem_specs(count):
    return [pl.BlockSpec(memory_space=pltpu.VMEM)] * count


def exchange(x, axis):
    n = lax.axis_size(axis)
    return pl.pallas_call(
        lambda *refs: exchange_kernel(axis, n, *refs),
        out_shape=jax.ShapeDtypeStruct(x.shape, x.dtype),
        in_specs=vmem_specs(1),
        out_specs=vmem_specs(1)[0],
        scratch_shapes=[
            pltpu.VMEM(x.shape, x.dtype),
            pltpu.SemaphoreType.DMA((n,)),
            pltpu.SemaphoreType.DMA((n,)),
        ],
        compiler_params=pltpu.CompilerParams(collective_id=next_id(axis), has_side_effects=True),
    )(x)


def sum_gather(x, extra, axis, finish, out_dtype):
    n = lax.axis_size(axis)
    return pl.pallas_call(
        lambda *refs: sum_gather_kernel(axis, n, finish, *refs),
        out_shape=jax.ShapeDtypeStruct(x.shape, out_dtype),
        in_specs=vmem_specs(2),
        out_specs=vmem_specs(1)[0],
        scratch_shapes=[
            pltpu.VMEM(x.shape, x.dtype),
            pltpu.VMEM(x.shape, out_dtype),
            pltpu.SemaphoreType.DMA((4, n)),
        ],
        compiler_params=pltpu.CompilerParams(collective_id=next_id(axis), has_side_effects=True),
    )(x, extra)


def attention_out(queries, kv, tkv, row_code, key_code, t_lo, t_hi, w_out, stream, head_dim):
    n_page = lax.axis_size("page")
    n_blk = lax.axis_size("blk")
    rows, width = stream.shape
    heads = kv.shape[1] // (2 * head_dim)
    lanes = 128 * (-(-width // (128 * n_blk)))
    n_chunk = width // lanes
    assert n_chunk * lanes == width
    part_shape = (n_page, heads * rows, 2 * head_dim)
    return pl.pallas_call(
        lambda *refs: attention_out_kernel(n_page, n_blk, heads, *refs),
        out_shape=(
            jax.ShapeDtypeStruct((n_page, rows, width // n_page), jnp.float32),
            jax.ShapeDtypeStruct((n_page, rows, width // n_page), jnp.float32),
        ),
        in_specs=vmem_specs(9),
        out_specs=tuple(vmem_specs(2)),
        scratch_shapes=[
            pltpu.VMEM(part_shape, jnp.float32),
            pltpu.VMEM(part_shape, jnp.float32),
            pltpu.VMEM((rows, width), jnp.float32),
            pltpu.VMEM((rows, width), jnp.float32),
            pltpu.VMEM((n_blk, rows, lanes), jnp.float32),
            pltpu.VMEM((n_chunk, rows, lanes), jnp.float32),
            pltpu.SemaphoreType.DMA((6, max(n_blk, n_page))),
        ],
        compiler_params=pltpu.CompilerParams(collective_id=next_id("both"), has_side_effects=True),
    )(queries, kv, tkv, row_code, key_code, t_lo, t_hi, w_out, stream)


def mlp(outgoing, vectors, w_up, w_down, columns):
    n_page = lax.axis_size("page")
    n_blk = lax.axis_size("blk")
    rows = outgoing.shape[0] * outgoing.shape[1]
    ff = w_up.shape[1]
    block = 2 * rows // n_page
    width = columns.shape[0]
    return pl.pallas_call(
        lambda *refs: mlp_kernel(n_page, n_blk, *refs),
        out_shape=(
            jax.ShapeDtypeStruct((width, rows), jnp.bfloat16),
            jax.ShapeDtypeStruct((1, rows), jnp.float32),
        ),
        in_specs=vmem_specs(5),
        out_specs=tuple(vmem_specs(2)),
        scratch_shapes=[
            pltpu.VMEM(outgoing.shape, jnp.float32),
            pltpu.VMEM((rows, ff), jnp.bfloat16),
            pltpu.VMEM((n_page, block, ff), jnp.bfloat16),
            pltpu.VMEM((rows, ff), jnp.bfloat16),
            pltpu.VMEM((n_blk, width, rows), jnp.float32),
            pltpu.VMEM((n_blk, width, rows), jnp.float32),
            pltpu.VMEM((n_blk, 1, rows), jnp.float32),
            pltpu.VMEM((n_page, 1, rows), jnp.float32),
            pltpu.SemaphoreType.DMA((12, max(n_page, n_blk))),
        ],
        compiler_params=pltpu.CompilerParams(collective_id=next_id("both"), has_side_effects=True),
    )(outgoing, vectors, w_up, w_down, columns)


def layer(queries, kv, tkv, row_code, key_code, t_lo, t_hi, w_out, stream, head_dim,
          vectors, w_up, w_down_t, columns, features):
    n_page = lax.axis_size("page")
    n_blk = lax.axis_size("blk")
    rows, width = stream.shape
    heads = kv.shape[1] // (2 * head_dim)
    lanes = 128 * (-(-width // (128 * n_blk)))
    n_chunk = width // lanes
    assert n_chunk * lanes == width
    part_shape = (n_page, heads * rows, 2 * head_dim)
    lanes_in = -(-(features + columns.shape[0]) // 128) * 128
    all_rows = rows * n_page
    ff = w_up.shape[1]
    block = 2 * all_rows // n_page
    piece = columns.shape[0]
    return pl.pallas_call(
        lambda *refs: layer_kernel(n_page, n_blk, heads, features, *refs),
        out_shape=(
            jax.ShapeDtypeStruct((piece, all_rows), jnp.bfloat16),
            jax.ShapeDtypeStruct((1, all_rows), jnp.float32),
        ),
        in_specs=vmem_specs(13),
        out_specs=tuple(vmem_specs(2)),
        scratch_shapes=[
            pltpu.VMEM((n_page, rows, features), jnp.float32),
            pltpu.VMEM((n_page, rows, lanes_in), jnp.float32),
            pltpu.VMEM(part_shape, jnp.float32),
            pltpu.VMEM(part_shape, jnp.float32),
            pltpu.VMEM((rows, width), jnp.float32),
            pltpu.VMEM((rows, width), jnp.float32),
            pltpu.VMEM((n_blk, rows, lanes), jnp.float32),
            pltpu.VMEM((n_chunk, rows, lanes), jnp.float32),
            pltpu.SemaphoreType.DMA((6, max(n_blk, n_page))),
            pltpu.VMEM((n_page, rows, lanes_in), jnp.float32),
            pltpu.VMEM((all_rows, ff), jnp.bfloat16),
            pltpu.VMEM((n_page, block, ff), jnp.bfloat16),
            pltpu.VMEM((all_rows, ff), jnp.bfloat16),
            pltpu.VMEM((n_blk, piece, all_rows), jnp.float32),
            pltpu.VMEM((n_blk, piece, all_rows), jnp.float32),
            pltpu.VMEM((n_blk, 1, all_rows), jnp.float32),
            pltpu.VMEM((n_page, 1, all_rows), jnp.float32),
            pltpu.SemaphoreType.DMA((12, max(n_page, n_blk))),
        ],
        compiler_params=pltpu.CompilerParams(collective_id=next_id("both"), has_side_effects=True),
    )(queries, kv, tkv, row_code, key_code, t_lo, t_hi, w_out, stream, vectors, w_up, w_down_t, columns)


def output_and_score(x, res, bias, score_w):
    n_blk = lax.axis_size("blk")
    n_page = lax.axis_size("page")
    lanes = x.shape[2]
    return pl.pallas_call(
        lambda *refs: output_kernel(n_blk, n_page, *refs),
        out_shape=(
            jax.ShapeDtypeStruct(x.shape[1:], jnp.bfloat16),
            jax.ShapeDtypeStruct((1, lanes), jnp.float32),
        ),
        in_specs=vmem_specs(4),
        out_specs=tuple(vmem_specs(2)),
        scratch_shapes=[
            pltpu.VMEM(x.shape, jnp.float32),
            pltpu.VMEM((n_blk, 1, lanes), jnp.float32),
            pltpu.VMEM((n_page, 1, lanes), jnp.float32),
            pltpu.SemaphoreType.DMA((6, max(n_blk, n_page))),
        ],
        compiler_params=pltpu.CompilerParams(collective_id=next_id("both"), has_side_effects=True),
    )(x, res, bias, score_w)


def ordered_sum(stack):
    total = stack[0]
    for j in range(1, stack.shape[0]):
        total = total + stack[j]
    return total


def body(
    queries,
    prompt_kv,
    tail_kv,
    page_table,
    prompt_len,
    tail_len,
    sample_prompt,
    stream_in,
    w_out,
    b_out,
    ln_gain,
    ln_bias,
    w_up,
    b_up,
    w_down,
    b_down,
    w_score,
):
    CALL_IDS.clear()
    samples, new_count, heads_dev, head_dim = queries.shape
    slots_dev, page_len = (prompt_kv.shape[0], prompt_kv.shape[1])
    own_count, tail_max = (tail_kv.shape[0], tail_kv.shape[1])
    prompts, pages_max = page_table.shape
    n_page = samples // own_count
    page_pos = lax.axis_index("page")
    blk_pos = lax.axis_index("blk")
    inv_sqrt = 1.0 / math.sqrt(head_dim)
    width = w_out.shape[1]
    rows_own = own_count * new_count

    entries = page_table.reshape(-1)
    slot_ids = page_pos * slots_dev + jnp.arange(slots_dev, dtype=jnp.int32)
    matched = (entries[:, None] == slot_ids[None, :]).astype(jnp.int32)
    owner_index = jnp.sum(matched * jnp.arange(entries.shape[0], dtype=jnp.int32)[:, None], axis=0)
    slot_prompt = owner_index // pages_max
    slot_page = owner_index % pages_max
    prompt_pick = (slot_prompt[:, None] == jnp.arange(prompts, dtype=jnp.int32)[None, :]).astype(
        jnp.int32
    )
    slot_limit = jnp.sum(prompt_pick * prompt_len[None, :], axis=1)
    key_pos = slot_page[:, None] * page_len + jnp.arange(page_len, dtype=jnp.int32)[None, :]
    key_live = (key_pos < slot_limit[:, None]).reshape(-1)
    key_prompt = jnp.repeat(slot_prompt, page_len)
    key_code = jnp.where(key_live, key_prompt, -1).astype(jnp.int32).reshape(1, -1)
    row_code = jnp.repeat(sample_prompt, new_count).astype(jnp.int32).reshape(-1, 1)

    first_row = page_pos * own_count
    own_lengths = lax.dynamic_slice_in_dim(tail_len, first_row, own_count, 0)
    local_row = jnp.arange(rows_own, dtype=jnp.int32)
    t_lo = (local_row // new_count) * tail_max
    t_hi = t_lo + jnp.repeat(own_lengths, new_count) + local_row % new_count

    slice_width = stream_in.shape[2]
    column = blk_pos * slice_width
    own_stream = (
        lax.dynamic_slice_in_dim(stream_in, first_row, own_count, 0)
        .reshape(rows_own, slice_width)
        .astype(jnp.float32)
    )
    own_bias = lax.dynamic_slice_in_dim(b_out, column, slice_width, 0).astype(jnp.float32)
    stream_full = lax.dynamic_update_slice_in_dim(
        jnp.zeros((rows_own, width), jnp.float32), own_stream + own_bias, column, 1
    )
    feature_count = ln_gain.shape[0]
    piece_width = b_down.shape[0]
    pad = -(-feature_count // 128) * 128
    vectors = jnp.concatenate(
        [
            jnp.pad(ln_gain.astype(jnp.float32), (0, pad - feature_count)),
            jnp.pad(ln_bias.astype(jnp.float32), (0, pad - feature_count)),
            b_up.astype(jnp.float32),
        ]
    ).reshape(1, -1)
    columns = jnp.stack([b_down.astype(jnp.float32), w_score.astype(jnp.float32)], axis=1)
    output_t, row_score = layer(
        queries.reshape(samples * new_count, heads_dev * head_dim),
        prompt_kv.reshape(slots_dev * page_len, heads_dev * 2 * head_dim),
        tail_kv.reshape(own_count * tail_max, heads_dev * 2 * head_dim),
        row_code,
        key_code,
        t_lo.reshape(-1, 1),
        t_hi.reshape(-1, 1),
        w_out,
        stream_full,
        head_dim,
        vectors,
        w_up,
        w_down.T,
        columns,
        feature_count,
    )
    output = output_t.T
    return (output.reshape(samples, new_count, piece_width), row_score.reshape(samples, new_count))


def solution(mesh):
    placed = (
        P(None, None, "blk", None),
        P("page", None, "blk", None),
        P("page", None, "blk", None),
        P(),
        P(),
        P(),
        P(),
        P(None, None, "blk"),
        P("blk", None),
        P(),
        P("page"),
        P("page"),
        P("page", "blk"),
        P("blk"),
        P("blk", "page"),
        P(("page", "blk")),
        P(("page", "blk")),
    )
    return jax.shard_map(
        body,
        mesh=mesh,
        in_specs=placed,
        out_specs=(P(None, None, ("page", "blk")), P()),
        check_vma=False,
    )
```
